128 devices in a mesh: pol: 4 (over y_hi, core), fsdp: 32 (over y_lo, z, x).
Axes of the slice: x: 4, y: 4 (y_hi: 2, y_lo: 2; y = y_hi * 2 + y_lo), z: 4, core: 2. Of those that a mesh axis runs over, the one named last changes fastest.
Arguments:
- gate_pre: bfloat16 [4, 4096, 20480], P('pol', None, 'fsdp'), may hold values from -6 to 6
- up_pre: bfloat16 [4, 4096, 20480], P('pol', None, 'fsdp'), may hold values from -360 to 360
- lag: bfloat16 [4, 20480, 2304], P('pol', 'fsdp'), may hold values from -6 to 6
- task: bfloat16 [4, 20480, 2304], P('pol', 'fsdp'), may hold values from -30 to 30
- cotangent: bfloat16 [4, 4096, 2304], P('pol', 'fsdp'), may hold values from -6 to 6
- buckets: int32 [4, 4096], P('pol', 'fsdp'), may hold values from 0 to 31
- advantages: float32 [4, 32], P('pol'), may hold values from -4 to 4
Outputs:
- new_lag: bfloat16 [4, 20480, 2304], P('pol', 'fsdp')
- merged: bfloat16 [4, 20480, 2304], P('pol', 'fsdp')
The draws below stay inside these ranges and needn't reach their ends.
All inputs are finite; a program needn't handle non-finite values.
Results may differ from the reference program's by a relative error of at most 0.017.
Values may be sent and summed in bfloat16 or wider, within the bound.
A program may use at most 128 MiB of HBM per device.

```python
import math
import jax
import jax.numpy as jnp
from jax import lax

D = 2304
FF = 20480
NB = 32
TOKENS = 4096
N_POL = 4
N_FSDP = 32


def slope_profile(span_log):
    position = jnp.arange(FF, dtype=jnp.float32) / (FF - 1) - 0.5
    parity = jnp.arange(N_POL) % 2
    direction = jnp.where(parity == 0, 1.0, -1.0).astype(jnp.float32)
    return jnp.exp(direction[:, None] * position[None, :] * span_log)


def draw_up_pre(key, part):
    key_base, key_rows, key_cols = jax.random.split(key, 3)
    key_order = jax.random.fold_in(key, 11)
    key_jitter = jax.random.fold_in(key, 13)
    row_scale = jnp.exp(jax.random.uniform(key_rows, (N_POL, TOKENS, 1), jnp.float32, math.log(0.9), math.log(1.1)))
    base = jnp.clip(jax.random.normal(key_base, (N_POL, TOKENS, FF), jnp.float32), -4.0, 4.0)
    profile = slope_profile(math.log(3.0))
    col_scale = profile[:, None, :] * jnp.exp(jax.random.uniform(key_cols, (N_POL, 1, FF), jnp.float32, math.log(0.1), 0.0))
    order = jax.random.permutation(key_order, N_POL).astype(jnp.float32)
    exponent = -2.0 + 3.0 * order / (N_POL - 1)
    jitter = jax.random.uniform(key_jitter, (N_POL,), jnp.float32, -0.18, 0.18)
    policy_scale = jnp.exp(exponent * math.log(4.0) + jitter)[:, None, None]
    return (base * row_scale * col_scale * policy_scale).astype(jnp.bfloat16)


def draw_task(key, part):
    key_base, key_rows, key_cols = jax.random.split(key, 3)
    base = jnp.clip(jax.random.normal(key_base, (N_POL, FF, D), jnp.float32), -4.0, 4.0)
    profile = slope_profile(math.log(3.0))
    row_scale = profile[:, :, None] * jnp.exp(jax.random.uniform(key_rows, (N_POL, FF, 1), jnp.float32, math.log(0.1), 0.0))
    col_scale = jnp.exp(jax.random.uniform(key_cols, (N_POL, 1, D), jnp.float32, math.log(0.3), math.log(3.0)))
    return (base * row_scale * col_scale).astype(jnp.bfloat16)


def set_ends(values, key, least, high):
    shape = values.shape
    place = [jax.random.randint(jax.random.fold_in(key, axis), (), 0, shape[axis]) for axis in range(len(shape))]
    values = values.at[tuple(place)].set(least)
    longest = shape.index(max(shape))
    place[longest] = (place[longest] + 1) % shape[longest]
    return values.at[tuple(place)].set(high)


def levels(key, dims, cuts, smallest, largest):
    def one(dim, shards_of):
        draws = jax.random.uniform(jax.random.fold_in(jax.random.fold_in(key, 6), dim), (shards_of,), jnp.float32, smallest / len(cuts), largest / len(cuts))
        return jnp.repeat(jnp.exp(draws), dims[dim] // shards_of).reshape((-1,) + (1,) * (len(dims) - dim - 1))

    factor_of = one(*cuts[0])
    for cut in cuts[1:]:
        factor_of = factor_of * one(*cut)
    return factor_of


def normal_values(rng, dims, deviation, reach, cuts=(), kind=jnp.bfloat16):
    result = jax.random.normal(rng, dims, jnp.float32) * deviation
    if len(cuts) > 0:
        result = levels(rng, dims, cuts, -0.22, 0.18) * result
    return jnp.clip(result, min=-reach, max=reach).astype(kind)


def setup_inputs(seed: int = 0) -> dict:
    streams_of = jax.random.split(jax.random.key(seed), 8)
    return {
        "gate_pre": normal_values(streams_of[0], (N_POL, TOKENS, FF), 1.0, 6.0, ((0, 4), (2, 32))),
        "up_pre": draw_up_pre(jax.random.fold_in(streams_of[7], 71), 0),
        "lag": normal_values(streams_of[2], (N_POL, FF, D), 1.0, 6.0, ((0, 4), (1, 32))),
        "task": draw_task(jax.random.fold_in(streams_of[7], 71), 0),
        "cotangent": normal_values(streams_of[4], (N_POL, TOKENS, D), 1.0, 6.0, ((0, 4), (1, 32))),
        "buckets": set_ends(jax.random.randint(streams_of[5], (N_POL, TOKENS), 0, NB), jax.random.fold_in(streams_of[5], 1), 0, NB - 1).astype(jnp.int32),
        "advantages": normal_values(streams_of[6], (N_POL, NB), 1.0, 4.0, ((0, 4),), jnp.float32),
    }


kl_coef = 0.5
clip_level = 0.15
step_rate = 8.0
ema_rate = 0.1

def slerp_weights(first_sq, second_sq, cross_dot):
    norm_first = jnp.sqrt(first_sq)
    norm_second = jnp.sqrt(second_sq)
    blend = norm_second / (norm_first + norm_second)
    cosine = jnp.clip(cross_dot / (norm_first * norm_second), -1.0, 1.0)
    opening = jnp.arccos(cosine)
    sine_val = jnp.sin(opening)
    weight_first = jnp.sin((1.0 - blend) * opening) / sine_val
    weight_second = jnp.sin(blend * opening) / sine_val
    return (weight_first, weight_second)

def reference(gate_pre, up_pre, lag, task, cotangent, buckets, advantages):
    ff_local = FF // N_FSDP
    inv_root = 1.0 / math.sqrt(FF)
    lag_outs = []
    deltas = []
    for policy in range(N_POL):
        hidden = (jax.nn.gelu(gate_pre[policy].astype(jnp.float32), approximate=True) * up_pre[policy].astype(jnp.float32)).astype(jnp.bfloat16)
        blocks_h = hidden.reshape(TOKENS, N_FSDP, ff_local).transpose(1, 0, 2)
        blocks_l = lag[policy].reshape(N_FSDP, ff_local, D)

        def add_block(summed, operands):
            part_val = (jnp.dot(operands[0], operands[1], preferred_element_type=jnp.float32) * inv_root).astype(jnp.bfloat16)
            part_val = lax.optimization_barrier(part_val)
            return (summed + part_val.astype(jnp.float32), None)
        kl_gap, _ = lax.scan(add_block, jnp.zeros((TOKENS, D), jnp.float32), (blocks_h, blocks_l))
        adv_tok = advantages[policy][buckets[policy]]
        signal = (adv_tok[:, None] * cotangent[policy].astype(jnp.float32) + kl_coef * kl_gap).astype(jnp.bfloat16)
        gradient = (jnp.dot(hidden.T, signal, preferred_element_type=jnp.float32) * inv_root).astype(jnp.bfloat16)
        grad_float = gradient.astype(jnp.float32)
        grad_sq = jnp.sum(grad_float * grad_float)
        factor = jnp.minimum(1.0, clip_level / (jnp.sqrt(grad_sq / (FF * D)) + 1e-06))
        update = step_rate * factor * grad_float
        lag_outs.append(((1.0 - ema_rate) * (lag[policy].astype(jnp.float32) - update)).astype(jnp.bfloat16))
        deltas.append(task[policy].astype(jnp.float32) - update)
    merged_list = []
    for policy in range(N_POL):
        lower = min(policy, policy ^ 1)
        upper = max(policy, policy ^ 1)
        first = deltas[lower]
        second = deltas[upper]
        weight_first, weight_second = slerp_weights(jnp.sum(first * first), jnp.sum(second * second), jnp.sum(first * second))
        merged_list.append((weight_first * first + weight_second * second).astype(jnp.bfloat16))
    return (jnp.stack(lag_outs), jnp.stack(merged_list))
```

```python
import functools
import math

import jax
import jax.numpy as jnp
from jax import lax
from jax.experimental import pallas as pl
from jax.experimental.pallas import tpu as pltpu
from jax.sharding import PartitionSpec as P

D = 2304
FF = 20480

kl_coef = 0.5
clip_level = 0.15
step_rate = 8.0
ema_rate = 0.1

MESH = pl.DeviceIdType.MESH
VMEM_BYTES = 67_000_000
RING = 4
BLOCKS = 32


def from_partner(block, axis, distance):
    count = lax.axis_size(axis)
    route = []
    for low in range(count):
        high = low | 1 << distance
        if high != low and high < count:
            route += [(low, high), (high, low)]
    return lax.ppermute(block, axis, route)


def copy_for_each(array, axis):
    length = lax.axis_size(axis)
    return lax.all_to_all(
        jnp.broadcast_to(array[None], (length, *array.shape)), axis, 0, 0, tiled=True
    )


def taken_together(array, axis):
    return copy_for_each(array, axis).sum(axis=0)


def in_one(arrays, axis):
    ends = [0]
    for a in arrays:
        ends.append(ends[-1] + a.size)
    total = taken_together(jnp.concatenate([a.ravel() for a in arrays]), axis)
    return tuple((total[b:e].reshape(a.shape) for a, b, e in zip(arrays, ends, ends[1:])))


def slerp_weights(first_sq, second_sq, cross_dot):
    norm_first = jnp.sqrt(first_sq)
    norm_second = jnp.sqrt(second_sq)
    blend = norm_second / (norm_first + norm_second)
    cosine = jnp.clip(cross_dot / (norm_first * norm_second), -1.0, 1.0)
    opening = jnp.arccos(cosine)
    sine_val = jnp.sin(opening)
    weight_first = jnp.sin((1.0 - blend) * opening) / sine_val
    weight_second = jnp.sin(blend * opening) / sine_val
    return (weight_first, weight_second)


def clip_factor(grad_sq):
    return jnp.minimum(1.0, clip_level / (jnp.sqrt(grad_sq / (FF * D)) + 1e-06))


def position():
    me = lax.axis_index("fsdp")
    return lax.div(me, 16), lax.rem(lax.div(me, 4), 4), lax.rem(me, 4)


def wrap(value):
    return lax.rem(value + 2 * RING, RING)


def flat(y, z, x):
    return y * 16 + z * 4 + x


def far_first(index):
    return jnp.where(index == 0, 2, jnp.where(index == 1, 3, jnp.where(index == 2, 1, 0)))


def near_first(index):
    return jnp.where(index == 2, 3, jnp.where(index == 3, 2, index))


def each(count, body):
    lax.fori_loop(0, count, lambda i, _: (body(i), None)[1], None)


def meet_neighbours():
    y, z, x = position()
    barrier = pltpu.get_barrier_semaphore()
    for target in (
        flat(y, z, wrap(x + 1)),
        flat(y, z, wrap(x - 1)),
        flat(y, wrap(z + 1), x),
        flat(y, wrap(z - 1), x),
        flat(1 - y, z, x),
    ):
        pl.semaphore_signal(
            barrier,
            inc=1,
            device_id=(lax.axis_index("pol"), target),
            device_id_type=MESH,
        )
    pl.semaphore_wait(barrier, 5)


def remote(src, dst, send_sem, recv_sem, target):
    return pltpu.make_async_remote_copy(
        src_ref=src,
        dst_ref=dst,
        send_sem=send_sem,
        recv_sem=recv_sem,
        device_id=(lax.axis_index("pol"), target),
        device_id_type=MESH,
    )


def axes_of(color):
    _, z, x = position()
    first = jnp.where(color == 0, x, z)
    second = jnp.where(color == 0, z, x)
    return 1 + 3 * color, 4 - 3 * color, first, second


def reduce_kernel(
    gate, up, lag_in, adv, cot,
    hid_out, wide_out, slim_out,
    gate_buf, up_buf, lag, hid, wide, slim, wide_in, slim_in,
    load_sem, lag_sem, out_sem, wide_send, slim_send, wide_recv, slim_recv,
):
    y, z, x = position()
    ff = lag.shape[0]
    rows = gate_buf.shape[1]
    half = rows // 2
    wcols, scols = wide.shape[2], slim.shape[2]
    inv_root = 1.0 / math.sqrt(FF)
    lag_copy = pltpu.make_async_copy(lag_in, lag, lag_sem)
    lag_copy.start()

    def place(j):
        ey = 1 - lax.rem(j, 2)
        m = lax.div(j, 2)
        ez = far_first(lax.div(m, 4))
        ex = far_first(lax.rem(m, 4))
        block = flat(lax.rem(y + ey, 2), wrap(z + ez), wrap(x + ex))
        return ey, ez, ex, block

    def loads(j):
        slot = lax.rem(j, 2)
        start = pl.multiple_of(place(j)[3] * rows, rows)
        return (
            pltpu.make_async_copy(gate.at[pl.ds(start, rows)], gate_buf.at[slot], load_sem.at[slot, 0]),
            pltpu.make_async_copy(up.at[pl.ds(start, rows)], up_buf.at[slot], load_sem.at[slot, 1]),
        )

    for copy in loads(0):
        copy.start()
    meet_neighbours()

    def send_wide(cv, block, target, slot):
        color, part = lax.div(cv, 2), lax.rem(cv, 2)
        start = pl.multiple_of(block * rows + part * half, half)
        remote(
            wide.at[color, pl.ds(start, half)], wide_in.at[cv, slot], wide_send, wide_recv.at[cv, slot], target
        ).start()

    def send_slim(cv, block, target, slot):
        color, part = lax.div(cv, 2), lax.rem(cv, 2)
        start = pl.multiple_of(block * rows + part * half, half)
        remote(
            slim.at[color, pl.ds(start, half)], slim_in.at[cv, slot], slim_send, slim_recv.at[cv, slot], target
        ).start()

    def compute(j):
        ey, ez, ex, block = place(j)
        slot = lax.rem(j, 2)

        @pl.when(j + 1 < BLOCKS)
        def _():
            for copy in loads(j + 1):
                copy.start()

        for copy in loads(j):
            copy.wait()
        start = pl.multiple_of(block * rows, rows)
        here = pl.ds(start, rows)
        hidden = (
            jax.nn.gelu(gate_buf[slot].astype(jnp.float32), approximate=True)
            * up_buf[slot].astype(jnp.float32)
        ).astype(jnp.bfloat16)
        hid[:, here] = hidden.T
        pltpu.make_async_copy(hid.at[:, here], hid_out.at[:, here], out_sem).start()

        @pl.when(j == 0)
        def _():
            lag_copy.wait()

        for color in range(2):
            wide[color, here, :] = (
                jnp.dot(
                    hidden, lag[:, color * wcols : (color + 1) * wcols], preferred_element_type=jnp.float32
                )
                * inv_root
            ).astype(jnp.bfloat16)
        for color in range(2):
            begin = 2 * wcols + color * scols
            slim[color, here, :] = (
                jnp.dot(hidden, lag[:, begin : begin + scols], preferred_element_type=jnp.float32) * inv_root
            ).astype(jnp.bfloat16)

        def leaf_wide(cv):
            color, s = lax.div(cv, 2), 1 - 2 * lax.rem(cv, 2)
            sp, sq, p, q = axes_of(color)
            ep = jnp.where(color == 0, ex, ez)
            eq = jnp.where(color == 0, ez, ex)
            u = wrap(s * ep)

            @pl.when(u >= 2)
            def _():
                step = jnp.where(u == 2, s, -s)
                target = y * 16 + wrap(p + step) * sp + q * sq
                send_wide(cv, block, target, jnp.where(u == 2, 0, 16) + eq * 2 + ey)

        each(4, leaf_wide)

        @pl.when(ey == 1)
        def _():
            def leaf_slim(cv):
                color = lax.div(cv, 2)
                eq = jnp.where(color == 0, ex, ez)
                er = jnp.where(color == 0, ez, ex)
                send_slim(cv, block, flat(1 - y, z, x), eq * 4 + er)

            each(4, leaf_slim)

    each(BLOCKS, compute)

    def gather(total, parts):
        def tile(i):
            at = pl.ds(pl.multiple_of(i * 16, 16), 16)
            value = total[at, :].astype(jnp.float32)
            for part in parts:
                value = value + part[at, :].astype(jnp.float32)
            total[at, :] = value.astype(jnp.bfloat16)

        each(half // 16, tile)

    def take_wide(cv, block, slots):
        color, part = lax.div(cv, 2), lax.rem(cv, 2)
        start = pl.multiple_of(block * rows + part * half, half)
        for slot in slots:
            remote(
                wide_in.at[cv, slot], wide_in.at[cv, slot], wide_send, wide_recv.at[cv, slot], flat(1 - y, z, x)
            ).wait_recv()
        gather(wide.at[color, pl.ds(start, half)], [wide_in.at[cv, slot] for slot in slots])

    def take_slim(cv, block, slots):
        color, part = lax.div(cv, 2), lax.rem(cv, 2)
        start = pl.multiple_of(block * rows + part * half, half)
        for slot in slots:
            remote(
                slim_in.at[cv, slot], slim_in.at[cv, slot], slim_send, slim_recv.at[cv, slot], flat(1 - y, z, x)
            ).wait_recv()
        gather(slim.at[color, pl.ds(start, half)], [slim_in.at[cv, slot] for slot in slots])

    def wide_middle(cv, k):
        color, s = lax.div(cv, 2), 1 - 2 * lax.rem(cv, 2)
        sp, sq, p, q = axes_of(color)
        eq, ey = far_first(lax.div(k, 2)), 1 - lax.rem(k, 2)
        block = lax.rem(y + ey, 2) * 16 + wrap(p + s) * sp + wrap(q + eq) * sq
        take_wide(cv, block, (eq * 2 + ey,))
        send_wide(cv, block, y * 16 + wrap(p + s) * sp + q * sq, 8 + eq * 2 + ey)

    def wide_root(cv, k):
        color, s = lax.div(cv, 2), 1 - 2 * lax.rem(cv, 2)
        sp, sq, p, q = axes_of(color)
        eq, ey = far_first(lax.div(k, 2)), 1 - lax.rem(k, 2)
        v = wrap(s * eq)
        block = lax.rem(y + ey, 2) * 16 + p * sp + wrap(q + eq) * sq
        take_wide(cv, block, (8 + eq * 2 + ey, 16 + eq * 2 + ey))

        @pl.when(v == 1)
        def _():
            take_wide(cv, block, (24 + ey,))

        @pl.when(v == 0)
        def _():
            take_wide(cv, block, (26 + ey, 28 + ey))

        @pl.when(v != 0)
        def _():
            step = jnp.where(v == 3, -s, s)
            slot = jnp.where(v == 2, 24, jnp.where(v == 3, 28, 26)) + ey
            send_wide(cv, block, y * 16 + p * sp + wrap(q + step) * sq, slot)

        @pl.when((v == 0) & (ey == 1))
        def _():
            send_wide(cv, block, flat(1 - y, z, x), 30)

        @pl.when((v == 0) & (ey == 0))
        def _():
            take_wide(cv, block, (30,))

    def slim_step(cv, t):
        color, s = lax.div(cv, 2), 1 - 2 * lax.rem(cv, 2)
        sq, sr, q, r = axes_of(color)
        er, eq = far_first(lax.div(t, 4)), far_first(lax.rem(t, 4))
        v, w = wrap(s * eq), wrap(s * er)
        block = y * 16 + wrap(q + eq) * sq + wrap(r + er) * sr
        take_slim(cv, block, (eq * 4 + er,))

        @pl.when(v == 1)
        def _():
            take_slim(cv, block, (16 + er,))

        @pl.when(v == 0)
        def _():
            take_slim(cv, block, (20 + er, 24 + er))

        @pl.when((v == 0) & (w == 1))
        def _():
            take_slim(cv, block, (28,))

        @pl.when((v == 0) & (w == 0))
        def _():
            take_slim(cv, block, (29, 30))

        @pl.when((v != 0) | (w != 0))
        def _():
            step_q = jnp.where(v == 0, 0, jnp.where(v == 3, -s, s))
            step_r = jnp.where(v == 0, jnp.where(w == 3, -s, s), 0)
            slot_q = jnp.where(v == 2, 16, jnp.where(v == 3, 24, 20)) + er
            slot_r = jnp.where(w == 2, 28, jnp.where(w == 3, 30, 29))
            target = y * 16 + wrap(q + step_q) * sq + wrap(r + step_r) * sr
            send_slim(cv, block, target, jnp.where(v == 0, slot_r, slot_q))

    def wave(k):
        @pl.when(k < 8)
        def _():
            each(4, lambda cv: wide_middle(cv, k))

        @pl.when(k > 0)
        def _():
            each(4, lambda cv: slim_step(cv, 2 * k - 1))

        @pl.when(k < 8)
        def _():
            each(4, lambda cv: slim_step(cv, 2 * k))

        @pl.when(k > 0)
        def _():
            each(4, lambda cv: wide_root(cv, k - 1))

    each(9, wave)

    own = pl.ds(pl.multiple_of(flat(y, z, x) * rows, rows), rows)
    scale = adv[...]

    def finish(source, out, color, begin, width):
        for i in range(width // 128):
            lanes = slice(i * 128, (i + 1) * 128)
            weighted = scale * cot[:, begin + i * 128 : begin + (i + 1) * 128].astype(jnp.float32)
            gap = source[color, own, lanes].astype(jnp.float32)
            out[color, :, lanes] = (weighted + kl_coef * gap).astype(jnp.bfloat16)

    for color in range(2):
        finish(wide, wide_out, color, color * wcols, wcols)
        finish(slim, slim_out, color, 2 * wcols + color * scols, scols)

    pltpu.make_async_copy(hid, hid_out, out_sem).wait()
    remote(wide_in, wide_in, wide_send, wide_recv.at[0, 0], flat(1 - y, z, x)).wait_send()
    remote(slim_in, slim_in, slim_send, slim_recv.at[0, 0], flat(1 - y, z, x)).wait_send()


def spread_kernel(
    hid_in, wide_own, slim_own,
    grad,
    hid, wide, slim, total,
    hid_sem, own_sem, wide_send, slim_send, wide_recv, slim_recv,
):
    y, z, x = position()
    me = flat(y, z, x)
    rows = wide_own.shape[1]
    half = rows // 2
    wcols, scols = wide.shape[2], slim.shape[2]
    inv_root = 1.0 / math.sqrt(FF)
    hid_copy = pltpu.make_async_copy(hid_in, hid, hid_sem)
    hid_copy.start()
    own = pl.ds(pl.multiple_of(me * rows, rows), rows)
    own_copies = []
    for color in range(2):
        own_copies.append(pltpu.make_async_copy(wide_own.at[color], wide.at[color, own], own_sem.at[color]))
        own_copies.append(pltpu.make_async_copy(slim_own.at[color], slim.at[color, own], own_sem.at[2 + color]))
    for copy in own_copies:
        copy.start()
    total[...] = jnp.zeros_like(total)
    for copy in own_copies:
        copy.wait()
    meet_neighbours()

    def piece(ref, cv, block):
        color, part = lax.div(cv, 2), lax.rem(cv, 2)
        start = pl.multiple_of(block * rows + part * half, half)
        return ref.at[color, pl.ds(start, half)]

    def send_wide(cv, block, target, slot):
        here = piece(wide, cv, block)
        remote(here, here, wide_send, wide_recv.at[cv, slot], target).start()

    def send_slim(cv, block, target, slot):
        here = piece(slim, cv, block)
        remote(here, here, slim_send, slim_recv.at[cv, slot], target).start()

    def wait_wide(cv, block, slot):
        here = piece(wide, cv, block)
        remote(here, here, wide_send, wide_recv.at[cv, slot], flat(1 - y, z, x)).wait_recv()

    def wait_slim(cv, block, slot):
        here = piece(slim, cv, block)
        remote(here, here, slim_send, slim_recv.at[cv, slot], flat(1 - y, z, x)).wait_recv()

    def wide_root(cv, n):
        color, s = lax.div(cv, 2), 1 - 2 * lax.rem(cv, 2)
        sp, sq, p, q = axes_of(color)
        oq, oy = near_first(lax.div(n, 2)), lax.rem(n, 2)
        b = wrap(s * oq)
        block = lax.rem(y + oy, 2) * 16 + p * sp + wrap(q - oq) * sq
        slot = oy * 16 + oq * 4

        @pl.when(n > 0)
        def _():
            wait_wide(cv, block, slot)

        @pl.when(n == 0)
        def _():
            send_wide(cv, block, flat(1 - y, z, x), 16)

        @pl.when(b <= 1)
        def _():
            send_wide(cv, block, y * 16 + p * sp + wrap(q + s) * sq, oy * 16 + wrap(oq + s) * 4)

        @pl.when(b == 0)
        def _():
            send_wide(cv, block, y * 16 + p * sp + wrap(q - s) * sq, oy * 16 + wrap(oq - s) * 4)

        send_wide(cv, block, y * 16 + wrap(p + s) * sp + q * sq, slot + wrap(s))
        send_wide(cv, block, y * 16 + wrap(p - s) * sp + q * sq, slot + wrap(-s))

    def wide_middle(cv, n):
        color, s = lax.div(cv, 2), 1 - 2 * lax.rem(cv, 2)
        sp, sq, p, q = axes_of(color)
        oq, oy = near_first(lax.div(n, 2)), lax.rem(n, 2)
        block = lax.rem(y + oy, 2) * 16 + wrap(p - s) * sp + wrap(q - oq) * sq
        slot = oy * 16 + oq * 4
        wait_wide(cv, block, slot + wrap(s))
        send_wide(cv, block, y * 16 + wrap(p + s) * sp + q * sq, slot + 2)

    def wide_leaf(cv, n):
        color, s = lax.div(cv, 2), 1 - 2 * lax.rem(cv, 2)
        sp, sq, p, q = axes_of(color)
        oq, oy = near_first(lax.div(n, 2)), lax.rem(n, 2)
        slot = oy * 16 + oq * 4
        base = lax.rem(y + oy, 2) * 16 + wrap(q - oq) * sq
        wait_wide(cv, base + wrap(p + s) * sp, slot + wrap(-s))
        wait_wide(cv, base + wrap(p + 2) * sp, slot + 2)

    def slim_step(cv, t):
        color, s = lax.div(cv, 2), 1 - 2 * lax.rem(cv, 2)
        sq, sr, q, r = axes_of(color)
        orr, oq = near_first(lax.div(t, 4)), near_first(lax.rem(t, 4))
        b, c = wrap(s * oq), wrap(s * orr)
        block = y * 16 + wrap(q - oq) * sq + wrap(r - orr) * sr
        slot = orr * 4 + oq

        @pl.when(t > 0)
        def _():
            wait_slim(cv, block, slot)

        send_slim(cv, block, flat(1 - y, z, x), 16 + slot)

        @pl.when((b == 0) & (c <= 1))
        def _():
            send_slim(cv, block, y * 16 + q * sq + wrap(r + s) * sr, wrap(orr + s) * 4)

        @pl.when((b == 0) & (c == 0))
        def _():
            send_slim(cv, block, y * 16 + q * sq + wrap(r - s) * sr, wrap(orr - s) * 4)

        @pl.when(b <= 1)
        def _():
            send_slim(cv, block, y * 16 + wrap(q + s) * sq + r * sr, orr * 4 + wrap(oq + s))

        @pl.when(b == 0)
        def _():
            send_slim(cv, block, y * 16 + wrap(q - s) * sq + r * sr, orr * 4 + wrap(oq - s))

    def slim_leaf(cv, n):
        color = lax.div(cv, 2)
        sq, sr, q, r = axes_of(color)
        orr, oy = near_first(lax.div(n, 2)), lax.rem(n, 2)

        @pl.when(oy == 1)
        def _():
            def one(oq):
                block = (1 - y) * 16 + wrap(q - oq) * sq + wrap(r - orr) * sr
                wait_slim(cv, block, 16 + orr * 4 + oq)

            each(4, one)

    def multiply(n):
        each(4, lambda cv: wide_leaf(cv, n))
        each(4, lambda cv: slim_leaf(cv, n))
        oo, oy = near_first(lax.div(n, 2)), lax.rem(n, 2)
        yy = lax.rem(y + oy, 2)
        for color in range(2):
            wide_at = color * wcols
            slim_at = 2 * wcols + color * scols
            if color == 0:
                start = pl.multiple_of((yy * 4 + wrap(z - oo)) * 4 * rows, 4 * rows)
                at = [pl.ds(start, 4 * rows)]
            else:
                start = yy * 16 + wrap(x - oo)
                at = [pl.ds(pl.multiple_of((start + 4 * i) * rows, rows), rows) for i in range(4)]
            left = jnp.concatenate([hid[:, a] for a in at], axis=1)
            right = jnp.concatenate([wide[color, a, :] for a in at], axis=0)
            total[:, wide_at : wide_at + wcols] += jnp.dot(left, right, preferred_element_type=jnp.float32)
            right = jnp.concatenate([slim[color, a, :] for a in at], axis=0)
            total[:, slim_at : slim_at + scols] += jnp.dot(left, right, preferred_element_type=jnp.float32)

    def wave(n):
        @pl.when(n < 8)
        def _():
            each(4, lambda cv: wide_root(cv, n))

        @pl.when((n > 0) & (n < 9))
        def _():
            each(4, lambda cv: slim_step(cv, 2 * n - 1))

        @pl.when(n < 8)
        def _():
            each(4, lambda cv: slim_step(cv, 2 * n))

        @pl.when((n > 0) & (n < 9))
        def _():
            each(4, lambda cv: wide_middle(cv, n - 1))

        @pl.when(n == 1)
        def _():
            hid_copy.wait()

        @pl.when(n > 1)
        def _():
            multiply(n - 2)

    each(10, wave)
    grad[...] = (total[...] * inv_root).astype(jnp.bfloat16)
    sent = pl.ds(0, (BLOCKS - 1) * rows)
    remote(wide.at[:, sent], wide.at[:, sent], wide_send, wide_recv.at[0, 0], flat(1 - y, z, x)).wait_send()
    remote(slim.at[:, sent], slim.at[:, sent], slim_send, slim_recv.at[0, 0], flat(1 - y, z, x)).wait_send()


def shards(gate_pre, up_pre, lag, task, cotangent, buckets, advantages):
    task_own = task[0]
    lag_own = lag[0]
    pol_index = lax.axis_index("pol")
    is_first = pol_index % 2 == 0
    partner_task = from_partner(task_own, "pol", 0)
    tokens, ff = gate_pre.shape[1:]
    cols = lag.shape[2]
    rows = tokens // BLOCKS
    half = rows // 2
    wcols, scols = cols // 3, cols // 6
    chosen = (buckets[0][:, None] == jnp.arange(advantages.shape[1])[None, :]).astype(jnp.float32)
    adv_tok = jnp.dot(chosen, advantages[0], precision=lax.Precision.HIGHEST)
    adv_wide = jnp.broadcast_to(adv_tok[:, None], (rows, 128))
    any_spec = pl.BlockSpec(memory_space=pl.ANY)
    vmem_spec = pl.BlockSpec(memory_space=pltpu.VMEM)
    bf16 = jnp.bfloat16
    per_stream = [
        pltpu.SemaphoreType.DMA,
        pltpu.SemaphoreType.DMA,
        pltpu.SemaphoreType.DMA((4, BLOCKS)),
        pltpu.SemaphoreType.DMA((4, BLOCKS)),
    ]
    hidden, wide_own, slim_own = pl.pallas_call(
        reduce_kernel,
        name="gap_reduce",
        out_shape=(
            jax.ShapeDtypeStruct((ff, tokens), bf16),
            jax.ShapeDtypeStruct((2, rows, wcols), bf16),
            jax.ShapeDtypeStruct((2, rows, scols), bf16),
        ),
        in_specs=[any_spec, any_spec, any_spec, vmem_spec, vmem_spec],
        out_specs=(any_spec, vmem_spec, vmem_spec),
        scratch_shapes=[
            pltpu.VMEM((2, rows, ff), bf16),
            pltpu.VMEM((2, rows, ff), bf16),
            pltpu.VMEM((ff, cols), bf16),
            pltpu.VMEM((ff, tokens), bf16),
            pltpu.VMEM((2, tokens, wcols), bf16),
            pltpu.VMEM((2, tokens, scols), bf16),
            pltpu.VMEM((4, BLOCKS - 1, half, wcols), bf16),
            pltpu.VMEM((4, BLOCKS - 1, half, scols), bf16),
            pltpu.SemaphoreType.DMA((2, 2)),
            pltpu.SemaphoreType.DMA,
            pltpu.SemaphoreType.DMA,
            *per_stream,
        ],
        compiler_params=pltpu.CompilerParams(
            collective_id=0, has_side_effects=True, vmem_limit_bytes=VMEM_BYTES
        ),
        cost_estimate=pl.CostEstimate(
            flops=2 * tokens * ff * cols, bytes_accessed=6 * tokens * ff, transcendentals=tokens * ff
        ),
    )(gate_pre[0], up_pre[0], lag_own, adv_wide, cotangent[0])
    gradient = pl.pallas_call(
        spread_kernel,
        name="signal_spread",
        out_shape=jax.ShapeDtypeStruct((ff, cols), bf16),
        in_specs=[any_spec, any_spec, any_spec],
        out_specs=vmem_spec,
        scratch_shapes=[
            pltpu.VMEM((ff, tokens), bf16),
            pltpu.VMEM((2, tokens, wcols), bf16),
            pltpu.VMEM((2, tokens, scols), bf16),
            pltpu.VMEM((ff, cols), jnp.float32),
            pltpu.SemaphoreType.DMA,
            pltpu.SemaphoreType.DMA((4,)),
            *per_stream,
        ],
        compiler_params=pltpu.CompilerParams(
            collective_id=1, has_side_effects=True, vmem_limit_bytes=VMEM_BYTES
        ),
        cost_estimate=pl.CostEstimate(
            flops=2 * tokens * ff * cols, bytes_accessed=2 * tokens * ff, transcendentals=0
        ),
    )(hidden, wide_own, slim_own)
    grad_float = gradient.astype(jnp.float32)
    task_float = task_own.astype(jnp.float32)
    partner_grad = from_partner(gradient, "pol", 0)
    part_grad_float = partner_grad.astype(jnp.float32)
    part_task_float = partner_task.astype(jnp.float32)
    dot_sums = in_one(
        (
            jnp.sum(grad_float * grad_float),
            jnp.sum(part_grad_float * part_grad_float),
            jnp.sum(grad_float * part_grad_float),
            jnp.sum(task_float * task_float),
            jnp.sum(part_task_float * part_task_float),
            jnp.sum(task_float * part_task_float),
            jnp.sum(task_float * grad_float),
            jnp.sum(task_float * part_grad_float),
            jnp.sum(part_task_float * grad_float),
            jnp.sum(part_task_float * part_grad_float),
        ),
        "fsdp",
    )
    grad_oo, grad_pp, grad_op, task_oo, task_pp, task_op, tgrad_oo, tgrad_op, tgrad_po, tgrad_pp = (
        dot_sums
    )
    factor_own = clip_factor(grad_oo)
    factor_part = clip_factor(grad_pp)
    scale_own = step_rate * factor_own
    scale_part = step_rate * factor_part
    update_own = scale_own * grad_float
    delta_own = task_float - update_own
    delta_part = part_task_float - scale_part * part_grad_float
    own_total = task_oo - 2.0 * scale_own * tgrad_oo + scale_own * scale_own * grad_oo
    part_total = task_pp - 2.0 * scale_part * tgrad_pp + scale_part * scale_part * grad_pp
    cross_dot = (
        task_op - scale_part * tgrad_op - scale_own * tgrad_po + scale_own * scale_part * grad_op
    )
    first_sq = jnp.where(is_first, own_total, part_total)
    second_sq = jnp.where(is_first, part_total, own_total)
    weight_first, weight_second = slerp_weights(first_sq, second_sq, cross_dot)
    weight_own = jnp.where(is_first, weight_first, weight_second)
    weight_part = jnp.where(is_first, weight_second, weight_first)
    merged = (weight_own * delta_own + weight_part * delta_part).astype(jnp.bfloat16)
    new_lag = ((1.0 - ema_rate) * (lag_own.astype(jnp.float32) - update_own)).astype(jnp.bfloat16)
    return (new_lag[None], merged[None])


def solution(mesh):
    return jax.shard_map(
        shards,
        mesh=mesh,
        in_specs=(
            P("pol", None, "fsdp"),
            P("pol", None, "fsdp"),
            P("pol", "fsdp", None),
            P("pol", "fsdp", None),
            P("pol", "fsdp", None),
            P("pol", "fsdp"),
            P("pol", None),
        ),
        out_specs=(P("pol", "fsdp", None), P("pol", "fsdp", None)),
        check_vma=False,
    )
```

```python
import functools
import math

import jax
import jax.numpy as jnp
from jax import lax
from jax.experimental import pallas as pl
from jax.experimental.pallas import tpu as pltpu
from jax.sharding import PartitionSpec as P

D = 2304
FF = 20480

kl_coef = 0.5
clip_level = 0.15
step_rate = 8.0
ema_rate = 0.1

MESH = pl.DeviceIdType.MESH
VMEM_BYTES = 67_000_000
RING = 4
BLOCKS = 32


def from_partner(block, axis, distance):
    count = lax.axis_size(axis)
    route = []
    for low in range(count):
        high = low | 1 << distance
        if high != low and high < count:
            route += [(low, high), (high, low)]
    return lax.ppermute(block, axis, route)


def slerp_weights(first_sq, second_sq, cross_dot):
    norm_first = jnp.sqrt(first_sq)
    norm_second = jnp.sqrt(second_sq)
    blend = norm_second / (norm_first + norm_second)
    cosine = jnp.clip(cross_dot / (norm_first * norm_second), -1.0, 1.0)
    opening = jnp.arccos(cosine)
    sine_val = jnp.sin(opening)
    weight_first = jnp.sin((1.0 - blend) * opening) / sine_val
    weight_second = jnp.sin(blend * opening) / sine_val
    return (weight_first, weight_second)


def clip_factor(grad_sq):
    return jnp.minimum(1.0, clip_level / (jnp.sqrt(grad_sq / (FF * D)) + 1e-06))


def position():
    me = lax.axis_index("fsdp")
    return lax.div(me, 16), lax.rem(lax.div(me, 4), 4), lax.rem(me, 4)


def wrap(value):
    return lax.rem(value + 2 * RING, RING)


def flat(y, z, x):
    return y * 16 + z * 4 + x


def far_first(index):
    return jnp.where(index == 0, 2, jnp.where(index == 1, 3, jnp.where(index == 2, 1, 0)))


def near_first(index):
    return jnp.where(index == 2, 3, jnp.where(index == 3, 2, index))


def each(count, body):
    lax.fori_loop(0, count, lambda i, _: (body(i), None)[1], None)


def partner():
    pol = lax.axis_index("pol")
    return pol + 1 - 2 * lax.rem(pol, 2)


def neighbours():
    y, z, x = position()
    pol = lax.axis_index("pol")
    return [
        (pol, flat(y, z, wrap(x + 1))),
        (pol, flat(y, z, wrap(x - 1))),
        (pol, flat(y, wrap(z + 1), x)),
        (pol, flat(y, wrap(z - 1), x)),
        (pol, flat(1 - y, z, x)),
    ]


def farther():
    y, z, x = position()
    pol = lax.axis_index("pol")
    return [
        (pol, flat(y, z, wrap(x + 2))),
        (pol, flat(y, wrap(z + 2), x)),
        (partner(), flat(y, z, x)),
        (partner(), flat(1 - y, z, x)),
    ]


def meet(devices):
    barrier = pltpu.get_barrier_semaphore()
    for device in devices:
        pl.semaphore_signal(barrier, inc=1, device_id=device, device_id_type=MESH)
    pl.semaphore_wait(barrier, len(devices))


def remote(src, dst, send_sem, recv_sem, target):
    return remote_to(src, dst, send_sem, recv_sem, (lax.axis_index("pol"), target))


def remote_to(src, dst, send_sem, recv_sem, device):
    return pltpu.make_async_remote_copy(
        src_ref=src,
        dst_ref=dst,
        send_sem=send_sem,
        recv_sem=recv_sem,
        device_id=device,
        device_id_type=MESH,
    )


def axes_of(color):
    _, z, x = position()
    first = jnp.where(color == 0, x, z)
    second = jnp.where(color == 0, z, x)
    return 1 + 3 * color, 4 - 3 * color, first, second


def reduce_kernel(
    gate, up, lag_in, adv, cot,
    hid_out, wide_out, slim_out,
    gate_buf, up_buf, active, lag, hid, wide, slim, wide_in, slim_in,
    load_sem, lag_sem, out_sem, wide_send, slim_send, wide_recv, slim_recv,
):
    y, z, x = position()
    ff = lag.shape[0]
    rows = gate_buf.shape[1] // 2
    half = rows // 2
    wcols, scols = wide.shape[2], slim.shape[2]
    inv_root = 1.0 / math.sqrt(FF)
    lag_copy = pltpu.make_async_copy(lag_in, lag, lag_sem)
    lag_copy.start()

    def place(j):
        ez, ex = far_first(lax.div(j, 4)), far_first(lax.rem(j, 4))
        return ez, ex, flat(1 - y, wrap(z + ez), wrap(x + ex)), flat(y, wrap(z + ez), wrap(x + ex))

    def loads(j):
        slot = lax.rem(j, 2)
        copies = []
        for i, block in enumerate(place(j)[2:]):
            start = pl.multiple_of(block * rows, rows)
            there = pl.ds(i * rows, rows)
            copies.append(
                pltpu.make_async_copy(gate.at[pl.ds(start, rows)], gate_buf.at[slot, there], load_sem.at[slot, i])
            )
            copies.append(
                pltpu.make_async_copy(up.at[pl.ds(start, rows)], up_buf.at[slot, there], load_sem.at[slot, 2 + i])
            )
        return copies

    def activate(j):
        slot = lax.rem(j, 2)
        for copy in loads(j):
            copy.wait()
        active[slot] = (
            jax.nn.gelu(gate_buf[slot].astype(jnp.float32), approximate=True)
            * up_buf[slot].astype(jnp.float32)
        ).astype(jnp.bfloat16)

    for j in range(2):
        for copy in loads(j):
            copy.start()
    activate(0)
    meet(neighbours())

    def send_wide(cv, block, target, slot):
        color, part = lax.div(cv, 2), lax.rem(cv, 2)
        start = pl.multiple_of(block * rows + part * half, half)
        remote(
            wide.at[color, pl.ds(start, half)], wide_in.at[cv, slot], wide_send, wide_recv.at[cv, slot], target
        ).start()

    def send_slim(cv, block, target, slot):
        color, part = lax.div(cv, 2), lax.rem(cv, 2)
        start = pl.multiple_of(block * rows + part * half, half)
        remote(
            slim.at[color, pl.ds(start, half)], slim_in.at[cv, slot], slim_send, slim_recv.at[cv, slot], target
        ).start()

    def compute(j):
        ez, ex, other, mine = place(j)
        slot = lax.rem(j, 2)

        @pl.when(j + 2 < BLOCKS // 2)
        def _():
            for copy in loads(j + 2):
                copy.start()

        @pl.when(j + 1 < BLOCKS // 2)
        def _():
            for copy in loads(j + 1):
                copy.wait()

        later = 1 - slot
        active[later] = (
            jax.nn.gelu(gate_buf[later].astype(jnp.float32), approximate=True)
            * up_buf[later].astype(jnp.float32)
        ).astype(jnp.bfloat16)
        hidden = active[slot]
        places = [pl.ds(pl.multiple_of(block * rows, rows), rows) for block in (other, mine)]

        def product(begin, width):
            return (
                jnp.dot(hidden, lag[:, begin : begin + width], preferred_element_type=jnp.float32) * inv_root
            ).astype(jnp.bfloat16)

        for color in range(2):
            value = product(color * wcols, wcols)
            for i, here in enumerate(places):
                wide[color, here, :] = value[i * rows : (i + 1) * rows]
        for color in range(2):
            value = product(2 * wcols + color * scols, scols)
            for i, here in enumerate(places):
                slim[color, here, :] = value[i * rows : (i + 1) * rows]
        for i, here in enumerate(places):
            hid[:, here] = hidden[i * rows : (i + 1) * rows].T
            pltpu.make_async_copy(hid.at[:, here], hid_out.at[:, here], out_sem).start()

        def leaf(cv):
            color, s = lax.div(cv, 2), 1 - 2 * lax.rem(cv, 2)
            sp, sq, p, q = axes_of(color)
            ep = jnp.where(color == 0, ex, ez)
            eq = jnp.where(color == 0, ez, ex)
            u = wrap(s * ep)
            send_slim(cv, other, flat(1 - y, z, x), ep * 4 + eq)

            @pl.when(u >= 2)
            def _():
                step = jnp.where(u == 2, s, -s)
                target = y * 16 + wrap(p + step) * sp + q * sq
                slot_of = jnp.where(u == 2, 0, 16) + eq * 2
                send_wide(cv, other, target, slot_of + 1)
                send_wide(cv, mine, target, slot_of)

        each(4, leaf)

    lag_copy.wait()
    each(BLOCKS // 2, compute)

    def gather(total, parts):
        def tile(i):
            at = pl.ds(pl.multiple_of(i * 16, 16), 16)
            value = total[at, :].astype(jnp.float32)
            for part in parts:
                value = value + part[at, :].astype(jnp.float32)
            total[at, :] = value.astype(jnp.bfloat16)

        each(half // 16, tile)

    def take_wide(cv, block, slots):
        color, part = lax.div(cv, 2), lax.rem(cv, 2)
        start = pl.multiple_of(block * rows + part * half, half)
        for slot in slots:
            remote(
                wide_in.at[cv, slot], wide_in.at[cv, slot], wide_send, wide_recv.at[cv, slot], flat(1 - y, z, x)
            ).wait_recv()
        gather(wide.at[color, pl.ds(start, half)], [wide_in.at[cv, slot] for slot in slots])

    def take_slim(cv, block, slots):
        color, part = lax.div(cv, 2), lax.rem(cv, 2)
        start = pl.multiple_of(block * rows + part * half, half)
        for slot in slots:
            remote(
                slim_in.at[cv, slot], slim_in.at[cv, slot], slim_send, slim_recv.at[cv, slot], flat(1 - y, z, x)
            ).wait_recv()
        gather(slim.at[color, pl.ds(start, half)], [slim_in.at[cv, slot] for slot in slots])

    def wide_middle(cv, k):
        color, s = lax.div(cv, 2), 1 - 2 * lax.rem(cv, 2)
        sp, sq, p, q = axes_of(color)
        eq, ey = far_first(lax.div(k, 2)), 1 - lax.rem(k, 2)
        block = lax.rem(y + ey, 2) * 16 + wrap(p + s) * sp + wrap(q + eq) * sq
        take_wide(cv, block, (eq * 2 + ey,))
        send_wide(cv, block, y * 16 + wrap(p + s) * sp + q * sq, 8 + eq * 2 + ey)

    def wide_root(cv, k):
        color, s = lax.div(cv, 2), 1 - 2 * lax.rem(cv, 2)
        sp, sq, p, q = axes_of(color)
        eq, ey = far_first(lax.div(k, 2)), 1 - lax.rem(k, 2)
        v = wrap(s * eq)
        block = lax.rem(y + ey, 2) * 16 + p * sp + wrap(q + eq) * sq
        take_wide(cv, block, (8 + eq * 2 + ey, 16 + eq * 2 + ey))

        @pl.when(v == 1)
        def _():
            take_wide(cv, block, (24 + ey,))

        @pl.when(v == 0)
        def _():
            take_wide(cv, block, (26 + ey, 28 + ey))

        @pl.when(v != 0)
        def _():
            step = jnp.where(v == 3, -s, s)
            slot = jnp.where(v == 2, 24, jnp.where(v == 3, 28, 26)) + ey
            send_wide(cv, block, y * 16 + p * sp + wrap(q + step) * sq, slot)

        @pl.when((v == 0) & (ey == 1))
        def _():
            send_wide(cv, block, flat(1 - y, z, x), 30)

        @pl.when((v == 0) & (ey == 0))
        def _():
            take_wide(cv, block, (30,))

    def slim_step(cv, t):
        color, s = lax.div(cv, 2), 1 - 2 * lax.rem(cv, 2)
        sq, sr, q, r = axes_of(color)
        er, eq = far_first(lax.div(t, 4)), far_first(lax.rem(t, 4))
        v, w = wrap(s * eq), wrap(s * er)
        block = y * 16 + wrap(q + eq) * sq + wrap(r + er) * sr
        take_slim(cv, block, (eq * 4 + er,))

        @pl.when(v == 1)
        def _():
            take_slim(cv, block, (16 + er,))

        @pl.when(v == 0)
        def _():
            take_slim(cv, block, (20 + er, 24 + er))

        @pl.when((v == 0) & (w == 1))
        def _():
            take_slim(cv, block, (28,))

        @pl.when((v == 0) & (w == 0))
        def _():
            take_slim(cv, block, (29, 30))

        @pl.when((v != 0) | (w != 0))
        def _():
            step_q = jnp.where(v == 0, 0, jnp.where(v == 3, -s, s))
            step_r = jnp.where(v == 0, jnp.where(w == 3, -s, s), 0)
            slot_q = jnp.where(v == 2, 16, jnp.where(v == 3, 24, 20)) + er
            slot_r = jnp.where(w == 2, 28, jnp.where(w == 3, 30, 29))
            target = y * 16 + wrap(q + step_q) * sq + wrap(r + step_r) * sr
            send_slim(cv, block, target, jnp.where(v == 0, slot_r, slot_q))

    def wave(k):
        @pl.when(k < 8)
        def _():
            each(4, lambda cv: wide_middle(cv, k))

        @pl.when(k > 0)
        def _():
            each(4, lambda cv: slim_step(cv, 2 * k - 1))

        @pl.when(k < 8)
        def _():
            each(4, lambda cv: slim_step(cv, 2 * k))

        @pl.when(k > 0)
        def _():
            each(4, lambda cv: wide_root(cv, k - 1))

    each(9, wave)

    own = pl.ds(pl.multiple_of(flat(y, z, x) * rows, rows), rows)
    scale = adv[...]

    def finish(source, out, color, begin, width):
        for i in range(width // 128):
            lanes = slice(i * 128, (i + 1) * 128)
            weighted = scale * cot[:, begin + i * 128 : begin + (i + 1) * 128].astype(jnp.float32)
            gap = source[color, own, lanes].astype(jnp.float32)
            out[color, :, lanes] = (weighted + kl_coef * gap).astype(jnp.bfloat16)

    for color in range(2):
        finish(wide, wide_out, color, color * wcols, wcols)
        finish(slim, slim_out, color, 2 * wcols + color * scols, scols)

    pltpu.make_async_copy(hid, hid_out, out_sem).wait()
    remote(wide_in, wide_in, wide_send, wide_recv.at[0, 0], flat(1 - y, z, x)).wait_send()
    remote(slim_in, slim_in, slim_send, slim_recv.at[0, 0], flat(1 - y, z, x)).wait_send()


def spread_kernel(
    hid_in, wide_own, slim_own, task_in, other_task_in,
    grad_out, other_grad_out, sums_out,
    hid, wide, slim, total, task, other_task, grad, other_grad, sums, sums_in,
    hid_sem, own_sem, wide_send, slim_send, wide_recv, slim_recv,
    task_sem, grad_send, grad_recv, out_sem, sums_send, sums_recv,
):
    y, z, x = position()
    me = flat(y, z, x)
    rows = wide_own.shape[1]
    half = rows // 2
    wcols, scols = wide.shape[2], slim.shape[2]
    inv_root = 1.0 / math.sqrt(FF)
    hid_copy = pltpu.make_async_copy(hid_in, hid, hid_sem)
    hid_copy.start()
    task_copies = [
        pltpu.make_async_copy(task_in, task, task_sem.at[0]),
        pltpu.make_async_copy(other_task_in, other_task, task_sem.at[1]),
    ]
    own = pl.ds(pl.multiple_of(me * rows, rows), rows)
    own_copies = []
    for color in range(2):
        own_copies.append(pltpu.make_async_copy(wide_own.at[color], wide.at[color, own], own_sem.at[color]))
        own_copies.append(pltpu.make_async_copy(slim_own.at[color], slim.at[color, own], own_sem.at[2 + color]))
    for copy in own_copies:
        copy.start()
    for copy in task_copies:
        copy.start()
    total[...] = jnp.zeros_like(total)
    for copy in own_copies:
        copy.wait()
    meet(neighbours() + farther())

    def piece(ref, cv, block):
        color, part = lax.div(cv, 2), lax.rem(cv, 2)
        start = pl.multiple_of(block * rows + part * half, half)
        return ref.at[color, pl.ds(start, half)]

    def send_wide(cv, block, target, slot):
        here = piece(wide, cv, block)
        remote(here, here, wide_send, wide_recv.at[cv, slot], target).start()

    def send_slim(cv, block, target, slot):
        here = piece(slim, cv, block)
        remote(here, here, slim_send, slim_recv.at[cv, slot], target).start()

    def wait_wide(cv, block, slot):
        here = piece(wide, cv, block)
        remote(here, here, wide_send, wide_recv.at[cv, slot], flat(1 - y, z, x)).wait_recv()

    def wait_slim(cv, block, slot):
        here = piece(slim, cv, block)
        remote(here, here, slim_send, slim_recv.at[cv, slot], flat(1 - y, z, x)).wait_recv()

    def wide_root(cv, n):
        color, s = lax.div(cv, 2), 1 - 2 * lax.rem(cv, 2)
        sp, sq, p, q = axes_of(color)
        oq, oy = near_first(lax.div(n, 2)), lax.rem(n, 2)
        b = wrap(s * oq)
        block = lax.rem(y + oy, 2) * 16 + p * sp + wrap(q - oq) * sq
        slot = oy * 16 + oq * 4

        @pl.when(n > 0)
        def _():
            wait_wide(cv, block, slot)

        @pl.when(n == 0)
        def _():
            send_wide(cv, block, flat(1 - y, z, x), 16)

        @pl.when(b <= 1)
        def _():
            send_wide(cv, block, y * 16 + p * sp + wrap(q + s) * sq, oy * 16 + wrap(oq + s) * 4)

        @pl.when(b == 0)
        def _():
            send_wide(cv, block, y * 16 + p * sp + wrap(q - s) * sq, oy * 16 + wrap(oq - s) * 4)

        send_wide(cv, block, y * 16 + wrap(p + s) * sp + q * sq, slot + wrap(s))
        send_wide(cv, block, y * 16 + wrap(p - s) * sp + q * sq, slot + wrap(-s))

    def wide_middle(cv, n):
        color, s = lax.div(cv, 2), 1 - 2 * lax.rem(cv, 2)
        sp, sq, p, q = axes_of(color)
        oq, oy = near_first(lax.div(n, 2)), lax.rem(n, 2)
        block = lax.rem(y + oy, 2) * 16 + wrap(p - s) * sp + wrap(q - oq) * sq
        slot = oy * 16 + oq * 4
        wait_wide(cv, block, slot + wrap(s))
        send_wide(cv, block, y * 16 + wrap(p + s) * sp + q * sq, slot + 2)

    def wide_leaf(cv, n):
        color, s = lax.div(cv, 2), 1 - 2 * lax.rem(cv, 2)
        sp, sq, p, q = axes_of(color)
        oq, oy = near_first(lax.div(n, 2)), lax.rem(n, 2)
        slot = oy * 16 + oq * 4
        base = lax.rem(y + oy, 2) * 16 + wrap(q - oq) * sq
        wait_wide(cv, base + wrap(p + s) * sp, slot + wrap(-s))
        wait_wide(cv, base + wrap(p + 2) * sp, slot + 2)

    def slim_step(cv, t):
        color, s = lax.div(cv, 2), 1 - 2 * lax.rem(cv, 2)
        sq, sr, q, r = axes_of(color)
        orr, oq = near_first(lax.div(t, 4)), near_first(lax.rem(t, 4))
        b, c = wrap(s * oq), wrap(s * orr)
        block = y * 16 + wrap(q - oq) * sq + wrap(r - orr) * sr
        slot = orr * 4 + oq

        @pl.when(t > 0)
        def _():
            wait_slim(cv, block, slot)

        send_slim(cv, block, flat(1 - y, z, x), 16 + slot)

        @pl.when((b == 0) & (c <= 1))
        def _():
            send_slim(cv, block, y * 16 + q * sq + wrap(r + s) * sr, wrap(orr + s) * 4)

        @pl.when((b == 0) & (c == 0))
        def _():
            send_slim(cv, block, y * 16 + q * sq + wrap(r - s) * sr, wrap(orr - s) * 4)

        @pl.when(b <= 1)
        def _():
            send_slim(cv, block, y * 16 + wrap(q + s) * sq + r * sr, orr * 4 + wrap(oq + s))

        @pl.when(b == 0)
        def _():
            send_slim(cv, block, y * 16 + wrap(q - s) * sq + r * sr, orr * 4 + wrap(oq - s))

    def slim_leaf(cv, n):
        color = lax.div(cv, 2)
        sq, sr, q, r = axes_of(color)
        orr, oy = near_first(lax.div(n, 2)), lax.rem(n, 2)

        @pl.when(oy == 1)
        def _():
            def one(oq):
                block = (1 - y) * 16 + wrap(q - oq) * sq + wrap(r - orr) * sr
                wait_slim(cv, block, 16 + orr * 4 + oq)

            each(4, one)

    def multiply(n):
        each(4, lambda cv: wide_leaf(cv, n))
        each(4, lambda cv: slim_leaf(cv, n))
        oo, oy = near_first(lax.div(n, 2)), lax.rem(n, 2)
        yy = lax.rem(y + oy, 2)
        for color in range(2):
            wide_at = color * wcols
            slim_at = 2 * wcols + color * scols
            if color == 0:
                start = pl.multiple_of((yy * 4 + wrap(z - oo)) * 4 * rows, 4 * rows)
                at = [pl.ds(start, 4 * rows)]
            else:
                start = yy * 16 + wrap(x - oo)
                at = [pl.ds(pl.multiple_of((start + 4 * i) * rows, rows), rows) for i in range(4)]
            left = jnp.concatenate([hid[:, a] for a in at], axis=1)
            right = jnp.concatenate([wide[color, a, :] for a in at], axis=0)
            total[:, wide_at : wide_at + wcols] += jnp.dot(left, right, preferred_element_type=jnp.float32)
            right = jnp.concatenate([slim[color, a, :] for a in at], axis=0)
            total[:, slim_at : slim_at + scols] += jnp.dot(left, right, preferred_element_type=jnp.float32)

    def wave(n):
        @pl.when(n < 8)
        def _():
            each(4, lambda cv: wide_root(cv, n))

        @pl.when((n > 0) & (n < 9))
        def _():
            each(4, lambda cv: slim_step(cv, 2 * n - 1))

        @pl.when(n < 8)
        def _():
            each(4, lambda cv: slim_step(cv, 2 * n))

        @pl.when((n > 0) & (n < 9))
        def _():
            each(4, lambda cv: wide_middle(cv, n - 1))

        @pl.when(n == 1)
        def _():
            hid_copy.wait()
            for copy in task_copies:
                copy.wait()

        @pl.when(n > 1)
        def _():
            multiply(n - 2)

    each(10, wave)

    ff, cols = grad.shape
    band = 128
    tile = 16
    zero = jnp.zeros((tile, 128), jnp.float32)

    def products(pairs, sums_of, at):
        done = list(sums_of)
        for i in range(cols // 128):
            lanes = slice(i * 128, (i + 1) * 128)
            read = {}
            for k, (one, two) in enumerate(pairs):
                for ref in (one, two):
                    if id(ref) not in read:
                        read[id(ref)] = ref[at, lanes].astype(jnp.float32)
                done[k] = done[k] + read[id(one)] * read[id(two)]
        return tuple(done)

    def tile_at(i):
        return pl.ds(pl.multiple_of(i * tile, tile), tile)

    def grad_copy(i):
        at = pl.ds(i * band, band)
        return remote_to(grad.at[at], other_grad.at[at], grad_send, grad_recv.at[i], (partner(), me))

    kept = (zero, zero, zero)
    for i in range(ff // band):

        def settle(k, sums_of):
            at = tile_at(k)
            grad[at, :] = (total[at, :] * inv_root).astype(jnp.bfloat16)
            return products(((grad, grad), (task, grad), (other_task, grad)), sums_of, at)

        kept = lax.fori_loop(i * (band // tile), (i + 1) * (band // tile), settle, kept)
        grad_copy(i).start()
        at = pl.ds(i * band, band)
        pltpu.make_async_copy(grad.at[at], grad_out.at[at], out_sem.at[0]).start()
    tasks = lax.fori_loop(
        0,
        ff // tile,
        lambda k, sums_of: products(((task, task), (task, other_task)), sums_of, tile_at(k)),
        (zero, zero),
    )
    crossed = (zero,)
    for i in range(ff // band):
        grad_copy(i).wait_recv()
        at = pl.ds(i * band, band)
        pltpu.make_async_copy(other_grad.at[at], other_grad_out.at[at], out_sem.at[1]).start()
        crossed = lax.fori_loop(
            i * (band // tile),
            (i + 1) * (band // tile),
            lambda k, sums_of: products(((grad, other_grad),), sums_of, tile_at(k)),
            crossed,
        )
    for i, value in enumerate(kept + tasks + crossed):
        sums[0, i : i + 1, :] = jnp.sum(value, axis=0, keepdims=True)
    sums[0, 6:8, :] = jnp.zeros((2, 128), jnp.float32)

    def exchange(source, slots, devices):
        copies = [
            remote_to(sums.at[source], sums_in.at[slot], sums_send, sums_recv.at[slot], device)
            for slot, device in zip(slots, devices)
        ]
        for copy in copies:
            copy.start()
        for copy in copies:
            copy.wait_recv()

    pol = lax.axis_index("pol")
    exchange(0, (0, 1, 2), [(pol, flat(y, z, wrap(x + i))) for i in (1, 2, 3)])
    sums[1] = sums[0] + sums_in[0] + sums_in[1] + sums_in[2]
    exchange(1, (3, 4, 5), [(pol, flat(y, wrap(z + i), x)) for i in (1, 2, 3)])
    sums[2] = sums[1] + sums_in[3] + sums_in[4] + sums_in[5]
    exchange(2, (6, 7, 8), [(pol, flat(1 - y, z, x)), (partner(), me), (partner(), flat(1 - y, z, x))])
    sums_out[0] = jnp.broadcast_to(jnp.sum(sums[2] + sums_in[6], axis=1, keepdims=True), (8, 128))
    sums_out[1] = jnp.broadcast_to(jnp.sum(sums_in[7] + sums_in[8], axis=1, keepdims=True), (8, 128))

    pltpu.make_async_copy(grad, grad_out, out_sem.at[0]).wait()
    pltpu.make_async_copy(other_grad, other_grad_out, out_sem.at[1]).wait()
    remote_to(grad, other_grad, grad_send, grad_recv.at[0], (partner(), me)).wait_send()
    remote_to(sums_in, sums_in, sums_send, sums_recv.at[0], (partner(), me)).wait_send()
    sent = pl.ds(0, (BLOCKS - 1) * rows)
    remote(wide.at[:, sent], wide.at[:, sent], wide_send, wide_recv.at[0, 0], flat(1 - y, z, x)).wait_send()
    remote(slim.at[:, sent], slim.at[:, sent], slim_send, slim_recv.at[0, 0], flat(1 - y, z, x)).wait_send()


def shards(gate_pre, up_pre, lag, task, cotangent, buckets, advantages):
    task_own = task[0]
    lag_own = lag[0]
    pol_index = lax.axis_index("pol")
    is_first = pol_index % 2 == 0
    partner_task = from_partner(task_own, "pol", 0)
    tokens, ff = gate_pre.shape[1:]
    cols = lag.shape[2]
    rows = tokens // BLOCKS
    half = rows // 2
    wcols, scols = cols // 3, cols // 6
    chosen = (buckets[0][:, None] == jnp.arange(advantages.shape[1])[None, :]).astype(jnp.float32)
    adv_tok = jnp.dot(chosen, advantages[0], precision=lax.Precision.HIGHEST)
    adv_wide = jnp.broadcast_to(adv_tok[:, None], (rows, 128))
    any_spec = pl.BlockSpec(memory_space=pl.ANY)
    vmem_spec = pl.BlockSpec(memory_space=pltpu.VMEM)
    bf16 = jnp.bfloat16
    per_stream = [
        pltpu.SemaphoreType.DMA,
        pltpu.SemaphoreType.DMA,
        pltpu.SemaphoreType.DMA((4, BLOCKS)),
        pltpu.SemaphoreType.DMA((4, BLOCKS)),
    ]
    hidden, wide_own, slim_own = pl.pallas_call(
        reduce_kernel,
        name="gap_reduce",
        out_shape=(
            jax.ShapeDtypeStruct((ff, tokens), bf16),
            jax.ShapeDtypeStruct((2, rows, wcols), bf16),
            jax.ShapeDtypeStruct((2, rows, scols), bf16),
        ),
        in_specs=[any_spec, any_spec, any_spec, vmem_spec, vmem_spec],
        out_specs=(any_spec, vmem_spec, vmem_spec),
        scratch_shapes=[
            pltpu.VMEM((2, 2 * rows, ff), bf16),
            pltpu.VMEM((2, 2 * rows, ff), bf16),
            pltpu.VMEM((2, 2 * rows, ff), bf16),
            pltpu.VMEM((ff, cols), bf16),
            pltpu.VMEM((ff, tokens), bf16),
            pltpu.VMEM((2, tokens, wcols), bf16),
            pltpu.VMEM((2, tokens, scols), bf16),
            pltpu.VMEM((4, BLOCKS - 1, half, wcols), bf16),
            pltpu.VMEM((4, BLOCKS - 1, half, scols), bf16),
            pltpu.SemaphoreType.DMA((2, 4)),
            pltpu.SemaphoreType.DMA,
            pltpu.SemaphoreType.DMA,
            *per_stream,
        ],
        compiler_params=pltpu.CompilerParams(
            collective_id=0, has_side_effects=True, vmem_limit_bytes=VMEM_BYTES
        ),
        cost_estimate=pl.CostEstimate(
            flops=2 * tokens * ff * cols, bytes_accessed=6 * tokens * ff, transcendentals=tokens * ff
        ),
    )(gate_pre[0], up_pre[0], lag_own, adv_wide, cotangent[0])
    gradient, partner_grad, sums = pl.pallas_call(
        spread_kernel,
        name="signal_spread",
        out_shape=(
            jax.ShapeDtypeStruct((ff, cols), bf16),
            jax.ShapeDtypeStruct((ff, cols), bf16),
            jax.ShapeDtypeStruct((2, 8, 128), jnp.float32),
        ),
        in_specs=[any_spec] * 5,
        out_specs=(any_spec, any_spec, vmem_spec),
        scratch_shapes=[
            pltpu.VMEM((ff, tokens), bf16),
            pltpu.VMEM((2, tokens, wcols), bf16),
            pltpu.VMEM((2, tokens, scols), bf16),
            pltpu.VMEM((ff, cols), jnp.float32),
            *[pltpu.VMEM((ff, cols), bf16)] * 4,
            pltpu.VMEM((3, 8, 128), jnp.float32),
            pltpu.VMEM((9, 8, 128), jnp.float32),
            pltpu.SemaphoreType.DMA,
            pltpu.SemaphoreType.DMA((4,)),
            *per_stream,
            pltpu.SemaphoreType.DMA((2,)),
            pltpu.SemaphoreType.DMA,
            pltpu.SemaphoreType.DMA((ff // 128,)),
            pltpu.SemaphoreType.DMA((2,)),
            pltpu.SemaphoreType.DMA,
            pltpu.SemaphoreType.DMA((9,)),
        ],
        compiler_params=pltpu.CompilerParams(
            collective_id=1, has_side_effects=True, vmem_limit_bytes=VMEM_BYTES
        ),
        cost_estimate=pl.CostEstimate(
            flops=2 * tokens * ff * cols, bytes_accessed=2 * tokens * ff, transcendentals=0
        ),
    )(hidden, wide_own, slim_own, task_own, partner_task)
    grad_float = gradient.astype(jnp.float32)
    task_float = task_own.astype(jnp.float32)
    part_grad_float = partner_grad.astype(jnp.float32)
    part_task_float = partner_task.astype(jnp.float32)
    grad_oo, tgrad_oo, tgrad_po, task_oo, task_op, grad_op = (sums[0, i] for i in range(6))
    grad_pp, tgrad_pp, tgrad_op, task_pp = (sums[1, i] for i in range(4))
    factor_own = clip_factor(grad_oo)
    factor_part = clip_factor(grad_pp)
    scale_own = step_rate * factor_own
    scale_part = step_rate * factor_part
    own_total = task_oo - 2.0 * scale_own * tgrad_oo + scale_own * scale_own * grad_oo
    part_total = task_pp - 2.0 * scale_part * tgrad_pp + scale_part * scale_part * grad_pp
    cross_dot = (
        task_op - scale_part * tgrad_op - scale_own * tgrad_po + scale_own * scale_part * grad_op
    )
    first_sq = jnp.where(is_first, own_total, part_total)
    second_sq = jnp.where(is_first, part_total, own_total)
    weight_first, weight_second = slerp_weights(first_sq, second_sq, cross_dot)
    weight_own = jnp.where(is_first, weight_first, weight_second)
    weight_part = jnp.where(is_first, weight_second, weight_first)
    scalars = lax.optimization_barrier(jnp.stack([weight_own, weight_part, scale_own, scale_part]))
    weight_own, weight_part, scale_own, scale_part = (scalars[i, 0] for i in range(4))
    update_own = scale_own * grad_float
    delta_own = task_float - update_own
    delta_part = part_task_float - scale_part * part_grad_float
    merged = (weight_own * delta_own + weight_part * delta_part).astype(jnp.bfloat16)
    new_lag = ((1.0 - ema_rate) * (lag_own.astype(jnp.float32) - update_own)).astype(jnp.bfloat16)
    return (new_lag[None], merged[None])


def solution(mesh):
    return jax.shard_map(
        shards,
        mesh=mesh,
        in_specs=(
            P("pol", None, "fsdp"),
            P("pol", None, "fsdp"),
            P("pol", "fsdp", None),
            P("pol", "fsdp", None),
            P("pol", "fsdp", None),
            P("pol", "fsdp"),
            P("pol", None),
        ),
        out_specs=(P("pol", "fsdp", None), P("pol", "fsdp", None)),
        check_vma=False,
    )
```

```python
import functools
import math

import jax
import jax.numpy as jnp
from jax import lax
from jax.experimental import pallas as pl
from jax.experimental.pallas import tpu as pltpu
from jax.sharding import PartitionSpec as P

D = 2304
FF = 20480

kl_coef = 0.5
clip_level = 0.15
step_rate = 8.0
ema_rate = 0.1

MESH = pl.DeviceIdType.MESH
VMEM_BYTES = 67_000_000
RING = 4
BLOCKS = 32


def from_partner(block, axis, distance):
    count = lax.axis_size(axis)
    route = []
    for low in range(count):
        high = low | 1 << distance
        if high != low and high < count:
            route += [(low, high), (high, low)]
    return lax.ppermute(block, axis, route)


def slerp_weights(first_sq, second_sq, cross_dot):
    norm_first = jnp.sqrt(first_sq)
    norm_second = jnp.sqrt(second_sq)
    blend = norm_second / (norm_first + norm_second)
    cosine = jnp.clip(cross_dot / (norm_first * norm_second), -1.0, 1.0)
    opening = jnp.arctan2(jnp.sqrt((1.0 - cosine) * (1.0 + cosine)), cosine)
    sine_val = jnp.sin(opening)
    weight_first = jnp.sin((1.0 - blend) * opening) / sine_val
    weight_second = jnp.sin(blend * opening) / sine_val
    return (weight_first, weight_second)


def clip_factor(grad_sq):
    return jnp.minimum(1.0, clip_level / (jnp.sqrt(grad_sq / (FF * D)) + 1e-06))


def position():
    me = lax.axis_index("fsdp")
    return lax.div(me, 16), lax.rem(lax.div(me, 4), 4), lax.rem(me, 4)


def wrap(value):
    return lax.rem(value + 2 * RING, RING)


def flat(y, z, x):
    return y * 16 + z * 4 + x


FAR = (2, 3, 1, 0)
NEAR = (0, 1, 3, 2)

REDUCE_ORDER = ("s0 s4 m0 m1", "m2 m3 m4 m5", "m6 m7 s1 s2", "r0 r1 s5 s6", "s8 s12 s3 r2", "r3 r4 r5 s9", "s7 s10 s13 r6", "s14 s11 r7 s15")
SPREAD_ORDER = (
    ("s0 r0 s1 s2", "s4 s8 r1 m0", "s3 r2 s6 s5", "r4 s9 s10 s12", "m1 r3"),
    ("m2 r5 s7 m4", "s11 s14"),
    ("m3 s13 r6",),
    ("m5 r7 s15",),
    ("m6",),
    (),
    ("m7",),
    (),
)


def far_first(index):
    return jnp.where(index == 0, 2, jnp.where(index == 1, 3, jnp.where(index == 2, 1, 0)))


def near_first(index):
    return jnp.where(index == 2, 3, jnp.where(index == 3, 2, index))


def steps_of(order, bodies):
    for step in " ".join(order).split():
        body, index = bodies[step[0]], int(step[1:])
        each(4, functools.partial(body, index))


def each(count, body):
    lax.fori_loop(0, count, lambda i, _: (body(i), None)[1], None)


def partner():
    pol = lax.axis_index("pol")
    return pol + 1 - 2 * lax.rem(pol, 2)


def neighbours():
    y, z, x = position()
    pol = lax.axis_index("pol")
    return [
        (pol, flat(y, z, wrap(x + 1))),
        (pol, flat(y, z, wrap(x - 1))),
        (pol, flat(y, wrap(z + 1), x)),
        (pol, flat(y, wrap(z - 1), x)),
        (pol, flat(1 - y, z, x)),
    ]


def farther():
    y, z, x = position()
    pol = lax.axis_index("pol")
    return [
        (pol, flat(y, z, wrap(x + 2))),
        (pol, flat(y, wrap(z + 2), x)),
        (partner(), flat(y, z, x)),
        (partner(), flat(1 - y, z, x)),
    ]


def meet(devices):
    barrier = pltpu.get_barrier_semaphore()
    for device in devices:
        pl.semaphore_signal(barrier, inc=1, device_id=device, device_id_type=MESH)
    pl.semaphore_wait(barrier, len(devices))


def remote(src, dst, send_sem, recv_sem, target):
    return remote_to(src, dst, send_sem, recv_sem, (lax.axis_index("pol"), target))


def remote_to(src, dst, send_sem, recv_sem, device):
    return pltpu.make_async_remote_copy(
        src_ref=src,
        dst_ref=dst,
        send_sem=send_sem,
        recv_sem=recv_sem,
        device_id=device,
        device_id_type=MESH,
    )


def axes_of(color):
    _, z, x = position()
    first = jnp.where(color == 0, x, z)
    second = jnp.where(color == 0, z, x)
    return 1 + 3 * color, 4 - 3 * color, first, second


def reduce_kernel(
    gate, up, lag_in, adv, cot,
    hid_out, wide_out, slim_out,
    gate_buf, up_buf, active, lag, hid, wide, slim, wide_in, slim_in,
    load_sem, lag_sem, out_sem, wide_send, slim_send, wide_recv, slim_recv,
):
    y, z, x = position()
    ff = lag.shape[0]
    rows = gate_buf.shape[1] // 2
    half = rows // 2
    wcols, scols = wide.shape[2], slim.shape[2]
    inv_root = 1.0 / math.sqrt(FF)
    lag_copy = pltpu.make_async_copy(lag_in, lag, lag_sem)
    lag_copy.start()

    def place(j):
        ez, ex = far_first(lax.div(j, 4)), far_first(lax.rem(j, 4))
        return ez, ex, flat(1 - y, wrap(z + ez), wrap(x + ex)), flat(y, wrap(z + ez), wrap(x + ex))

    def loads(j):
        slot = lax.rem(j, 2)
        copies = []
        for i, block in enumerate(place(j)[2:]):
            start = pl.multiple_of(block * rows, rows)
            there = pl.ds(i * rows, rows)
            copies.append(
                pltpu.make_async_copy(gate.at[pl.ds(start, rows)], gate_buf.at[slot, there], load_sem.at[slot, i])
            )
            copies.append(
                pltpu.make_async_copy(up.at[pl.ds(start, rows)], up_buf.at[slot, there], load_sem.at[slot, 2 + i])
            )
        return copies

    def activate(j):
        slot = lax.rem(j, 2)
        for copy in loads(j):
            copy.wait()
        active[slot] = (
            jax.nn.gelu(gate_buf[slot].astype(jnp.float32), approximate=True)
            * up_buf[slot].astype(jnp.float32)
        ).astype(jnp.bfloat16)

    for j in range(2):
        for copy in loads(j):
            copy.start()
    activate(0)
    meet(neighbours())

    def send_wide(cv, block, target, slot):
        color, part = lax.div(cv, 2), lax.rem(cv, 2)
        start = pl.multiple_of(block * rows + part * half, half)
        remote(
            wide.at[color, pl.ds(start, half)], wide_in.at[cv, slot], wide_send, wide_recv.at[cv, slot], target
        ).start()

    def send_slim(cv, block, target, slot):
        color, part = lax.div(cv, 2), lax.rem(cv, 2)
        start = pl.multiple_of(block * rows + part * half, half)
        remote(
            slim.at[color, pl.ds(start, half)], slim_in.at[cv, slot], slim_send, slim_recv.at[cv, slot], target
        ).start()

    def compute(j):
        ez, ex, other, mine = place(j)
        slot = lax.rem(j, 2)

        @pl.when(j + 2 < BLOCKS // 2)
        def _():
            for copy in loads(j + 2):
                copy.start()

        @pl.when(j + 1 < BLOCKS // 2)
        def _():
            for copy in loads(j + 1):
                copy.wait()

        later = 1 - slot
        active[later] = (
            jax.nn.gelu(gate_buf[later].astype(jnp.float32), approximate=True)
            * up_buf[later].astype(jnp.float32)
        ).astype(jnp.bfloat16)
        hidden = active[slot]
        places = [pl.ds(pl.multiple_of(block * rows, rows), rows) for block in (other, mine)]

        def product(begin, width):
            return (
                jnp.dot(hidden, lag[:, begin : begin + width], preferred_element_type=jnp.float32) * inv_root
            ).astype(jnp.bfloat16)

        for color in range(2):
            value = product(color * wcols, wcols)
            for i, here in enumerate(places):
                wide[color, here, :] = value[i * rows : (i + 1) * rows]
        for color in range(2):
            value = product(2 * wcols + color * scols, scols)
            for i, here in enumerate(places):
                slim[color, here, :] = value[i * rows : (i + 1) * rows]
        for i, here in enumerate(places):
            hid[:, here] = hidden[i * rows : (i + 1) * rows].T
            pltpu.make_async_copy(hid.at[:, here], hid_out.at[:, here], out_sem).start()

        def leaf(cv):
            color, s = lax.div(cv, 2), 1 - 2 * lax.rem(cv, 2)
            sp, sq, p, q = axes_of(color)
            ep = jnp.where(color == 0, ex, ez)
            eq = jnp.where(color == 0, ez, ex)
            u = wrap(s * ep)
            send_slim(cv, other, flat(1 - y, z, x), ep * 4 + eq)

            @pl.when(u >= 2)
            def _():
                step = jnp.where(u == 2, s, -s)
                target = y * 16 + wrap(p + step) * sp + q * sq
                slot_of = jnp.where(u == 2, 0, 16) + eq * 2
                send_wide(cv, other, target, slot_of + 1)
                send_wide(cv, mine, target, slot_of)

        each(4, leaf)

    lag_copy.wait()
    each(BLOCKS // 2, compute)

    def gather(total, parts):
        def tile(i):
            at = pl.ds(pl.multiple_of(i * 16, 16), 16)
            value = total[at, :].astype(jnp.float32)
            for part in parts:
                value = value + part[at, :].astype(jnp.float32)
            total[at, :] = value.astype(jnp.bfloat16)

        each(half // 16, tile)

    def take_wide(cv, block, slots):
        color, part = lax.div(cv, 2), lax.rem(cv, 2)
        start = pl.multiple_of(block * rows + part * half, half)
        for slot in slots:
            remote(
                wide_in.at[cv, slot], wide_in.at[cv, slot], wide_send, wide_recv.at[cv, slot], flat(1 - y, z, x)
            ).wait_recv()
        gather(wide.at[color, pl.ds(start, half)], [wide_in.at[cv, slot] for slot in slots])

    def take_slim(cv, block, slots):
        color, part = lax.div(cv, 2), lax.rem(cv, 2)
        start = pl.multiple_of(block * rows + part * half, half)
        for slot in slots:
            remote(
                slim_in.at[cv, slot], slim_in.at[cv, slot], slim_send, slim_recv.at[cv, slot], flat(1 - y, z, x)
            ).wait_recv()
        gather(slim.at[color, pl.ds(start, half)], [slim_in.at[cv, slot] for slot in slots])

    def wide_middle(k, cv):
        color, s = lax.div(cv, 2), 1 - 2 * lax.rem(cv, 2)
        sp, sq, p, q = axes_of(color)
        eq, ey = FAR[k // 2], 1 - k % 2
        block = lax.rem(y + ey, 2) * 16 + wrap(p + s) * sp + wrap(q + eq) * sq
        take_wide(cv, block, (eq * 2 + ey,))
        send_wide(cv, block, y * 16 + wrap(p + s) * sp + q * sq, 8 + eq * 2 + ey)

    def wide_root(k, cv):
        color, s = lax.div(cv, 2), 1 - 2 * lax.rem(cv, 2)
        sp, sq, p, q = axes_of(color)
        eq, ey = FAR[k // 2], 1 - k % 2
        v = wrap(s * eq)
        block = lax.rem(y + ey, 2) * 16 + p * sp + wrap(q + eq) * sq
        arrived = (8 + eq * 2 + ey, 16 + eq * 2 + ey)
        if eq == 0:
            take_wide(cv, block, arrived + (26 + ey, 28 + ey) + ((30,) if ey == 0 else ()))
            if ey == 1:
                send_wide(cv, block, flat(1 - y, z, x), 30)
            return
        take_wide(cv, block, arrived)
        if eq != 2:

            @pl.when(v == 1)
            def _():
                take_wide(cv, block, (24 + ey,))

        step = jnp.where(v == 3, -s, s)
        slot = jnp.where(v == 2, 24, jnp.where(v == 3, 28, 26)) + ey
        send_wide(cv, block, y * 16 + p * sp + wrap(q + step) * sq, slot)

    def slim_step(t, cv):
        color, s = lax.div(cv, 2), 1 - 2 * lax.rem(cv, 2)
        sq, sr, q, r = axes_of(color)
        er, eq = FAR[t // 4], FAR[t % 4]
        v, w = wrap(s * eq), wrap(s * er)
        block = y * 16 + wrap(q + eq) * sq + wrap(r + er) * sr
        if eq != 0:
            take_slim(cv, block, (eq * 4 + er,))
            if eq != 2:

                @pl.when(v == 1)
                def _():
                    take_slim(cv, block, (16 + er,))

            step = jnp.where(v == 3, -s, s)
            slot = jnp.where(v == 2, 16, jnp.where(v == 3, 24, 20)) + er
            send_slim(cv, block, y * 16 + wrap(q + step) * sq + r * sr, slot)
            return
        take_slim(cv, block, (er, 20 + er, 24 + er) + ((29, 30) if er == 0 else ()))
        if er in (1, 3):

            @pl.when(w == 1)
            def _():
                take_slim(cv, block, (28,))

        if er != 0:
            step = jnp.where(w == 3, -s, s)
            slot = jnp.where(w == 2, 28, jnp.where(w == 3, 30, 29))
            send_slim(cv, block, y * 16 + q * sq + wrap(r + step) * sr, slot)

    steps_of(REDUCE_ORDER, {"m": wide_middle, "r": wide_root, "s": slim_step})

    own = pl.ds(pl.multiple_of(flat(y, z, x) * rows, rows), rows)
    scale = adv[...]

    def finish(source, out, color, begin, width):
        for i in range(width // 128):
            lanes = slice(i * 128, (i + 1) * 128)
            weighted = scale * cot[:, begin + i * 128 : begin + (i + 1) * 128].astype(jnp.float32)
            gap = source[color, own, lanes].astype(jnp.float32)
            out[color, :, lanes] = (weighted + kl_coef * gap).astype(jnp.bfloat16)

    for color in range(2):
        finish(wide, wide_out, color, color * wcols, wcols)
        finish(slim, slim_out, color, 2 * wcols + color * scols, scols)

    pltpu.make_async_copy(hid, hid_out, out_sem).wait()
    remote(wide_in, wide_in, wide_send, wide_recv.at[0, 0], flat(1 - y, z, x)).wait_send()
    remote(slim_in, slim_in, slim_send, slim_recv.at[0, 0], flat(1 - y, z, x)).wait_send()


def spread_kernel(
    hid_in, wide_own, slim_own, task_in, other_task_in, lag_in,
    lag_out, merged_out,
    hid, wide, slim, total, task, other_task, lag, grad, other_grad, sums, sums_in,
    hid_sem, own_sem, wide_send, slim_send, wide_recv, slim_recv,
    task_sem, grad_send, grad_recv, out_sem, sums_send, sums_recv,
):
    y, z, x = position()
    me = flat(y, z, x)
    rows = wide_own.shape[1]
    half = rows // 2
    wcols, scols = wide.shape[2], slim.shape[2]
    inv_root = 1.0 / math.sqrt(FF)
    hid_copy = pltpu.make_async_copy(hid_in, hid, hid_sem)
    hid_copy.start()
    task_copies = [
        pltpu.make_async_copy(task_in, task, task_sem.at[0]),
        pltpu.make_async_copy(other_task_in, other_task, task_sem.at[1]),
        pltpu.make_async_copy(lag_in, lag, task_sem.at[2]),
    ]
    own = pl.ds(pl.multiple_of(me * rows, rows), rows)
    own_copies = []
    for color in range(2):
        own_copies.append(pltpu.make_async_copy(wide_own.at[color], wide.at[color, own], own_sem.at[color]))
        own_copies.append(pltpu.make_async_copy(slim_own.at[color], slim.at[color, own], own_sem.at[2 + color]))
    for copy in own_copies:
        copy.start()
    for copy in task_copies:
        copy.start()
    total[...] = jnp.zeros_like(total)
    for copy in own_copies:
        copy.wait()
    meet(neighbours() + farther())

    def piece(ref, cv, block):
        color, part = lax.div(cv, 2), lax.rem(cv, 2)
        start = pl.multiple_of(block * rows + part * half, half)
        return ref.at[color, pl.ds(start, half)]

    def send_wide(cv, block, target, slot):
        here = piece(wide, cv, block)
        remote(here, here, wide_send, wide_recv.at[cv, slot], target).start()

    def send_slim(cv, block, target, slot):
        here = piece(slim, cv, block)
        remote(here, here, slim_send, slim_recv.at[cv, slot], target).start()

    def wait_wide(cv, block, slot):
        here = piece(wide, cv, block)
        remote(here, here, wide_send, wide_recv.at[cv, slot], flat(1 - y, z, x)).wait_recv()

    def wait_slim(cv, block, slot):
        here = piece(slim, cv, block)
        remote(here, here, slim_send, slim_recv.at[cv, slot], flat(1 - y, z, x)).wait_recv()

    def wide_root(n, cv):
        color, s = lax.div(cv, 2), 1 - 2 * lax.rem(cv, 2)
        sp, sq, p, q = axes_of(color)
        oq, oy = NEAR[n // 2], n % 2
        b = wrap(s * oq)
        block = lax.rem(y + oy, 2) * 16 + p * sp + wrap(q - oq) * sq
        slot = oy * 16 + oq * 4
        if n > 0:
            wait_wide(cv, block, slot)
        else:
            send_wide(cv, block, flat(1 - y, z, x), 16)

        def forward():
            send_wide(cv, block, y * 16 + p * sp + wrap(q + s) * sq, oy * 16 + wrap(oq + s) * 4)

        if oq == 0:
            forward()
            send_wide(cv, block, y * 16 + p * sp + wrap(q - s) * sq, oy * 16 + wrap(oq - s) * 4)
        elif oq != 2:
            pl.when(b == 1)(forward)
        send_wide(cv, block, y * 16 + wrap(p + s) * sp + q * sq, slot + wrap(s))
        send_wide(cv, block, y * 16 + wrap(p - s) * sp + q * sq, slot + wrap(-s))

    def wide_middle(n, cv):
        color, s = lax.div(cv, 2), 1 - 2 * lax.rem(cv, 2)
        sp, sq, p, q = axes_of(color)
        oq, oy = NEAR[n // 2], n % 2
        block = lax.rem(y + oy, 2) * 16 + wrap(p - s) * sp + wrap(q - oq) * sq
        slot = oy * 16 + oq * 4
        wait_wide(cv, block, slot + wrap(s))
        send_wide(cv, block, y * 16 + wrap(p + s) * sp + q * sq, slot + 2)

    def wide_leaf(cv, n):
        color, s = lax.div(cv, 2), 1 - 2 * lax.rem(cv, 2)
        sp, sq, p, q = axes_of(color)
        oq, oy = near_first(lax.div(n, 2)), lax.rem(n, 2)
        slot = oy * 16 + oq * 4
        base = lax.rem(y + oy, 2) * 16 + wrap(q - oq) * sq
        wait_wide(cv, base + wrap(p + s) * sp, slot + wrap(-s))
        wait_wide(cv, base + wrap(p + 2) * sp, slot + 2)

    def slim_step(t, cv):
        color, s = lax.div(cv, 2), 1 - 2 * lax.rem(cv, 2)
        sq, sr, q, r = axes_of(color)
        orr, oq = NEAR[t // 4], NEAR[t % 4]
        b, c = wrap(s * oq), wrap(s * orr)
        block = y * 16 + wrap(q - oq) * sq + wrap(r - orr) * sr
        slot = orr * 4 + oq
        if t > 0:
            wait_slim(cv, block, slot)
        send_slim(cv, block, flat(1 - y, z, x), 16 + slot)

        def forward_third():
            send_slim(cv, block, y * 16 + q * sq + wrap(r + s) * sr, wrap(orr + s) * 4)

        def forward_second():
            send_slim(cv, block, y * 16 + wrap(q + s) * sq + r * sr, orr * 4 + wrap(oq + s))

        if oq == 0:
            if orr == 0:
                forward_third()
                send_slim(cv, block, y * 16 + q * sq + wrap(r - s) * sr, wrap(orr - s) * 4)
            elif orr != 2:
                pl.when(c == 1)(forward_third)
            forward_second()
            send_slim(cv, block, y * 16 + wrap(q - s) * sq + r * sr, orr * 4 + wrap(oq - s))
        elif oq != 2:
            pl.when(b == 1)(forward_second)

    def slim_leaf(cv, n):
        color = lax.div(cv, 2)
        sq, sr, q, r = axes_of(color)
        orr, oy = near_first(lax.div(n, 2)), lax.rem(n, 2)

        @pl.when(oy == 1)
        def _():
            def one(oq):
                block = (1 - y) * 16 + wrap(q - oq) * sq + wrap(r - orr) * sr
                wait_slim(cv, block, 16 + orr * 4 + oq)

            each(4, one)

    def multiply(n):
        each(4, lambda cv: wide_leaf(cv, n))
        each(4, lambda cv: slim_leaf(cv, n))
        oo, oy = near_first(lax.div(n, 2)), lax.rem(n, 2)
        yy = lax.rem(y + oy, 2)
        for color in range(2):
            wide_at = color * wcols
            slim_at = 2 * wcols + color * scols
            if color == 0:
                start = pl.multiple_of((yy * 4 + wrap(z - oo)) * 4 * rows, 4 * rows)
                at = [pl.ds(start, 4 * rows)]
            else:
                start = yy * 16 + wrap(x - oo)
                at = [pl.ds(pl.multiple_of((start + 4 * i) * rows, rows), rows) for i in range(4)]
            left = jnp.concatenate([hid[:, a] for a in at], axis=1)
            right = jnp.concatenate([wide[color, a, :] for a in at], axis=0)
            total[:, wide_at : wide_at + wcols] += jnp.dot(left, right, preferred_element_type=jnp.float32)
            right = jnp.concatenate([slim[color, a, :] for a in at], axis=0)
            total[:, slim_at : slim_at + scols] += jnp.dot(left, right, preferred_element_type=jnp.float32)

    band = 128
    tile = 16
    zero = jnp.zeros((tile, 128), jnp.float32)
    ff, cols = grad.shape

    def products(pairs, sums_of, at):
        done = list(sums_of)
        for i in range(cols // 128):
            lanes = slice(i * 128, (i + 1) * 128)
            read = {}
            for k, (one, two) in enumerate(pairs):
                for ref in (one, two):
                    if id(ref) not in read:
                        read[id(ref)] = ref[at, lanes].astype(jnp.float32)
                done[k] = done[k] + read[id(one)] * read[id(two)]
        return tuple(done)

    def tile_at(i):
        return pl.ds(pl.multiple_of(i * tile, tile), tile)

    def grad_copy(i):
        at = pl.ds(i * band, band)
        return remote_to(grad.at[at], other_grad.at[at], grad_send, grad_recv.at[i], (partner(), me))

    bodies = {"m": wide_middle, "r": wide_root, "s": slim_step}
    steps_of(SPREAD_ORDER[0], bodies)
    hid_copy.wait()
    for copy in task_copies:
        copy.wait()
    tasks = lax.fori_loop(
        0,
        ff // tile,
        lambda k, sums_of: products(((task, task), (task, other_task)), sums_of, tile_at(k)),
        (zero, zero),
    )

    def group(n):
        for i in range(1, len(SPREAD_ORDER)):
            pl.when(n == i)(functools.partial(steps_of, SPREAD_ORDER[i], bodies))
        multiply(n)

    each(8, group)

    kept = (zero, zero, zero)
    for i in range(ff // band):

        def settle(k, sums_of):
            at = tile_at(k)
            grad[at, :] = (total[at, :] * inv_root).astype(jnp.bfloat16)
            return products(((grad, grad), (task, grad), (other_task, grad)), sums_of, at)

        kept = lax.fori_loop(i * (band // tile), (i + 1) * (band // tile), settle, kept)
        grad_copy(i).start()
    crossed = (zero,)
    for i in range(ff // band):
        grad_copy(i).wait_recv()
        crossed = lax.fori_loop(
            i * (band // tile),
            (i + 1) * (band // tile),
            lambda k, sums_of: products(((grad, other_grad),), sums_of, tile_at(k)),
            crossed,
        )
    for i, value in enumerate(kept + tasks + crossed):
        sums[0, i : i + 1, :] = jnp.sum(value, axis=0, keepdims=True)
    sums[0, 6:8, :] = jnp.zeros((2, 128), jnp.float32)

    def exchange(source, slots, devices):
        copies = [
            remote_to(sums.at[source], sums_in.at[slot], sums_send, sums_recv.at[slot], device)
            for slot, device in zip(slots, devices)
        ]
        for copy in copies:
            copy.start()
        for copy in copies:
            copy.wait_recv()

    pol = lax.axis_index("pol")
    exchange(0, (0, 1, 2), [(pol, flat(y, z, wrap(x + i))) for i in (1, 2, 3)])
    sums[1] = sums[0] + sums_in[0] + sums_in[1] + sums_in[2]
    exchange(1, (3, 4, 5), [(pol, flat(y, wrap(z + i), x)) for i in (1, 2, 3)])
    sums[2] = sums[1] + sums_in[3] + sums_in[4] + sums_in[5]
    exchange(2, (6, 7, 8), [(pol, flat(1 - y, z, x)), (partner(), me), (partner(), flat(1 - y, z, x))])
    own_sums = jnp.sum(sums[2] + sums_in[6], axis=1, keepdims=True)
    part_sums = jnp.sum(sums_in[7] + sums_in[8], axis=1, keepdims=True)

    def spread_row(column, i):
        return jnp.broadcast_to(column[i : i + 1], (1, 128))

    grad_oo, tgrad_oo, tgrad_po, task_oo, task_op, grad_op = (spread_row(own_sums, i) for i in range(6))
    grad_pp, tgrad_pp, tgrad_op, task_pp = (spread_row(part_sums, i) for i in range(4))
    is_first = lax.rem(pol, 2) == 0
    scale_own = step_rate * clip_factor(grad_oo)
    scale_part = step_rate * clip_factor(grad_pp)
    own_total = task_oo - 2.0 * scale_own * tgrad_oo + scale_own * scale_own * grad_oo
    part_total = task_pp - 2.0 * scale_part * tgrad_pp + scale_part * scale_part * grad_pp
    cross_dot = (
        task_op - scale_part * tgrad_op - scale_own * tgrad_po + scale_own * scale_part * grad_op
    )
    first_sq = jnp.where(is_first, own_total, part_total)
    second_sq = jnp.where(is_first, part_total, own_total)
    weight_first, weight_second = slerp_weights(first_sq, second_sq, cross_dot)
    weight_own = jnp.where(is_first, weight_first, weight_second)
    weight_part = jnp.where(is_first, weight_second, weight_first)

    for i in range(ff // band):

        def settle_outputs(k):
            at = tile_at(k)
            for i in range(cols // 128):
                lanes = slice(i * 128, (i + 1) * 128)
                update = scale_own * grad[at, lanes].astype(jnp.float32)
                delta_own = task[at, lanes].astype(jnp.float32) - update
                delta_part = other_task[at, lanes].astype(jnp.float32) - scale_part * other_grad[
                    at, lanes
                ].astype(jnp.float32)
                lag[at, lanes] = ((1.0 - ema_rate) * (lag[at, lanes].astype(jnp.float32) - update)).astype(
                    jnp.bfloat16
                )
                other_grad[at, lanes] = (weight_own * delta_own + weight_part * delta_part).astype(jnp.bfloat16)

        each(band // tile, lambda k: settle_outputs(i * (band // tile) + k))
        at = pl.ds(i * band, band)
        pltpu.make_async_copy(lag.at[at], lag_out.at[at], out_sem.at[0]).start()
        pltpu.make_async_copy(other_grad.at[at], merged_out.at[at], out_sem.at[1]).start()

    pltpu.make_async_copy(lag, lag_out, out_sem.at[0]).wait()
    pltpu.make_async_copy(other_grad, merged_out, out_sem.at[1]).wait()
    remote_to(grad, other_grad, grad_send, grad_recv.at[0], (partner(), me)).wait_send()
    remote_to(sums_in, sums_in, sums_send, sums_recv.at[0], (partner(), me)).wait_send()
    sent = pl.ds(0, (BLOCKS - 1) * rows)
    remote(wide.at[:, sent], wide.at[:, sent], wide_send, wide_recv.at[0, 0], flat(1 - y, z, x)).wait_send()
    remote(slim.at[:, sent], slim.at[:, sent], slim_send, slim_recv.at[0, 0], flat(1 - y, z, x)).wait_send()


def shards(gate_pre, up_pre, lag, task, cotangent, buckets, advantages):
    task_own = task[0]
    lag_own = lag[0]
    partner_task = from_partner(task_own, "pol", 0)
    tokens, ff = gate_pre.shape[1:]
    cols = lag.shape[2]
    rows = tokens // BLOCKS
    half = rows // 2
    wcols, scols = cols // 3, cols // 6
    chosen = (buckets[0][:, None] == jnp.arange(advantages.shape[1])[None, :]).astype(jnp.float32)
    adv_tok = jnp.dot(chosen, advantages[0], precision=lax.Precision.HIGHEST)
    adv_wide = jnp.broadcast_to(adv_tok[:, None], (rows, 128))
    any_spec = pl.BlockSpec(memory_space=pl.ANY)
    vmem_spec = pl.BlockSpec(memory_space=pltpu.VMEM)
    bf16 = jnp.bfloat16
    per_stream = [
        pltpu.SemaphoreType.DMA,
        pltpu.SemaphoreType.DMA,
        pltpu.SemaphoreType.DMA((4, BLOCKS)),
        pltpu.SemaphoreType.DMA((4, BLOCKS)),
    ]
    hidden, wide_own, slim_own = pl.pallas_call(
        reduce_kernel,
        name="gap_reduce",
        out_shape=(
            jax.ShapeDtypeStruct((ff, tokens), bf16),
            jax.ShapeDtypeStruct((2, rows, wcols), bf16),
            jax.ShapeDtypeStruct((2, rows, scols), bf16),
        ),
        in_specs=[any_spec, any_spec, any_spec, vmem_spec, vmem_spec],
        out_specs=(any_spec, vmem_spec, vmem_spec),
        scratch_shapes=[
            pltpu.VMEM((2, 2 * rows, ff), bf16),
            pltpu.VMEM((2, 2 * rows, ff), bf16),
            pltpu.VMEM((2, 2 * rows, ff), bf16),
            pltpu.VMEM((ff, cols), bf16),
            pltpu.VMEM((ff, tokens), bf16),
            pltpu.VMEM((2, tokens, wcols), bf16),
            pltpu.VMEM((2, tokens, scols), bf16),
            pltpu.VMEM((4, BLOCKS - 1, half, wcols), bf16),
            pltpu.VMEM((4, BLOCKS - 1, half, scols), bf16),
            pltpu.SemaphoreType.DMA((2, 4)),
            pltpu.SemaphoreType.DMA,
            pltpu.SemaphoreType.DMA,
            *per_stream,
        ],
        compiler_params=pltpu.CompilerParams(
            collective_id=0, has_side_effects=True, vmem_limit_bytes=VMEM_BYTES
        ),
        cost_estimate=pl.CostEstimate(
            flops=2 * tokens * ff * cols, bytes_accessed=6 * tokens * ff, transcendentals=tokens * ff
        ),
    )(gate_pre[0], up_pre[0], lag_own, adv_wide, cotangent[0])
    new_lag, merged = pl.pallas_call(
        spread_kernel,
        name="signal_spread",
        out_shape=(
            jax.ShapeDtypeStruct((ff, cols), bf16),
            jax.ShapeDtypeStruct((ff, cols), bf16),
        ),
        in_specs=[any_spec] * 6,
        out_specs=(any_spec, any_spec),
        scratch_shapes=[
            pltpu.VMEM((ff, tokens), bf16),
            pltpu.VMEM((2, tokens, wcols), bf16),
            pltpu.VMEM((2, tokens, scols), bf16),
            pltpu.VMEM((ff, cols), jnp.float32),
            *[pltpu.VMEM((ff, cols), bf16)] * 5,
            pltpu.VMEM((3, 8, 128), jnp.float32),
            pltpu.VMEM((9, 8, 128), jnp.float32),
            pltpu.SemaphoreType.DMA,
            pltpu.SemaphoreType.DMA((4,)),
            *per_stream,
            pltpu.SemaphoreType.DMA((3,)),
            pltpu.SemaphoreType.DMA,
            pltpu.SemaphoreType.DMA((ff // 128,)),
            pltpu.SemaphoreType.DMA((2,)),
            pltpu.SemaphoreType.DMA,
            pltpu.SemaphoreType.DMA((9,)),
        ],
        compiler_params=pltpu.CompilerParams(
            collective_id=1, has_side_effects=True, vmem_limit_bytes=VMEM_BYTES
        ),
        cost_estimate=pl.CostEstimate(
            flops=2 * tokens * ff * cols, bytes_accessed=2 * tokens * ff, transcendentals=0
        ),
    )(hidden, wide_own, slim_own, task_own, partner_task, lag_own)
    return (new_lag[None], merged[None])


def solution(mesh):
    return jax.shard_map(
        shards,
        mesh=mesh,
        in_specs=(
            P("pol", None, "fsdp"),
            P("pol", None, "fsdp"),
            P("pol", "fsdp", None),
            P("pol", "fsdp", None),
            P("pol", "fsdp", None),
            P("pol", "fsdp"),
            P("pol", None),
        ),
        out_specs=(P("pol", "fsdp", None), P("pol", "fsdp", None)),
        check_vma=False,
    )
```

```python
import functools
import math

import jax
import jax.numpy as jnp
from jax import lax
from jax.experimental import pallas as pl
from jax.experimental.pallas import tpu as pltpu
from jax.sharding import PartitionSpec as P

D = 2304
FF = 20480

kl_coef = 0.5
clip_level = 0.15
step_rate = 8.0
ema_rate = 0.1

MESH = pl.DeviceIdType.MESH
VMEM_BYTES = 67_000_000
RING = 4
BLOCKS = 32


def slerp_weights(first_sq, second_sq, cross_dot):
    norm_first = jnp.sqrt(first_sq)
    norm_second = jnp.sqrt(second_sq)
    blend = norm_second / (norm_first + norm_second)
    cosine = jnp.clip(cross_dot / (norm_first * norm_second), -1.0, 1.0)
    opening = jnp.arctan2(jnp.sqrt((1.0 - cosine) * (1.0 + cosine)), cosine)
    sine_val = jnp.sin(opening)
    weight_first = jnp.sin((1.0 - blend) * opening) / sine_val
    weight_second = jnp.sin(blend * opening) / sine_val
    return (weight_first, weight_second)


def clip_factor(grad_sq):
    return jnp.minimum(1.0, clip_level / (jnp.sqrt(grad_sq / (FF * D)) + 1e-06))


def position():
    me = lax.axis_index("fsdp")
    return lax.div(me, 16), lax.rem(lax.div(me, 4), 4), lax.rem(me, 4)


def wrap(value):
    return lax.rem(value + 2 * RING, RING)


def flat(y, z, x):
    return y * 16 + z * 4 + x


FAR = (2, 3, 1, 0)
NEAR = (0, 1, 3, 2)

ORDER = (
    ("s0 m2 s4 m0", "m3 m1 m5 m4", "m6 m7 s1 s2", "s8 s5 r0 s6", "r1 s12 s3 s9", "s10 r4 r2 s13", "s7 s11 s14 r3", "r5 r6 s15 S0", "r7 R0 S1 S2", "S4 S8 R2 M0", "R1 S3 S6 S5", "R4 S9 S10 S12", "M2"),
    ("R5 M1 R3 S7", "R6 M4 S11 S13", "S14 M5"),
    ("M3",),
    ("M6 R7 S15",),
    (),
    ("M7",),
    (),
    (),
)


def far_first(index):
    return jnp.where(index == 0, 2, jnp.where(index == 1, 3, jnp.where(index == 2, 1, 0)))


def near_first(index):
    return jnp.where(index == 2, 3, jnp.where(index == 3, 2, index))


def steps_of(order, bodies):
    for step in " ".join(order).split():
        body, index = bodies[step[0]], int(step[1:])
        each(4, functools.partial(body, index))


def each(count, body):
    lax.fori_loop(0, count, lambda i, _: (body(i), None)[1], None)


def partner():
    pol = lax.axis_index("pol")
    return pol + 1 - 2 * lax.rem(pol, 2)


def neighbours():
    y, z, x = position()
    pol = lax.axis_index("pol")
    return [
        (pol, flat(y, z, wrap(x + 1))),
        (pol, flat(y, z, wrap(x - 1))),
        (pol, flat(y, wrap(z + 1), x)),
        (pol, flat(y, wrap(z - 1), x)),
        (pol, flat(1 - y, z, x)),
    ]


def farther():
    y, z, x = position()
    pol = lax.axis_index("pol")
    return [
        (pol, flat(y, z, wrap(x + 2))),
        (pol, flat(y, wrap(z + 2), x)),
        (partner(), flat(y, z, x)),
        (partner(), flat(1 - y, z, x)),
    ]


def greet(devices):
    for device in devices:
        pl.semaphore_signal(pltpu.get_barrier_semaphore(), inc=1, device_id=device, device_id_type=MESH)


def meet(devices):
    pl.semaphore_wait(pltpu.get_barrier_semaphore(), len(devices))


def remote(src, dst, send_sem, recv_sem, target):
    return remote_to(src, dst, send_sem, recv_sem, (lax.axis_index("pol"), target))


def remote_to(src, dst, send_sem, recv_sem, device):
    return pltpu.make_async_remote_copy(
        src_ref=src,
        dst_ref=dst,
        send_sem=send_sem,
        recv_sem=recv_sem,
        device_id=device,
        device_id_type=MESH,
    )


def axes_of(color):
    _, z, x = position()
    first = jnp.where(color == 0, x, z)
    second = jnp.where(color == 0, z, x)
    return 1 + 3 * color, 4 - 3 * color, first, second


def step_kernel(
    gate, up, lag_in, task_in, cot, buckets, adv,
    lag_out, merged_out,
    gate_buf, up_buf, active, lag, hid, wide, slim, wide_in, slim_in,
    total, other_task, grad, other_grad, scale, sums, sums_in,
    load_sem, task_sem, task_send, task_recv, grad_send, grad_recv, out_sem, sums_send, sums_recv,
    fold_wide_send, fold_slim_send, fold_wide_recv, fold_slim_recv,
    wide_send, slim_send, wide_recv, slim_recv, clear,
):
    y, z, x = position()
    ff = lag.shape[0]
    rows = gate_buf.shape[1] // 2
    me = flat(y, z, x)
    half = rows // 2
    wcols, scols = wide.shape[2], slim.shape[2]
    inv_root = 1.0 / math.sqrt(FF)
    greet(neighbours() + farther())
    lag_copy = pltpu.make_async_copy(lag_in, lag, task_sem)

    def place(j):
        ez, ex = far_first(lax.div(j, 4)), far_first(lax.rem(j, 4))
        return ez, ex, flat(1 - y, wrap(z + ez), wrap(x + ex)), flat(y, wrap(z + ez), wrap(x + ex))

    def loads(j):
        slot = lax.rem(j, 2)
        copies = []
        for i, block in enumerate(place(j)[2:]):
            start = pl.multiple_of(block * rows, rows)
            there = pl.ds(i * rows, rows)
            copies.append(
                pltpu.make_async_copy(gate.at[pl.ds(start, rows)], gate_buf.at[slot, there], load_sem.at[slot, i])
            )
            copies.append(
                pltpu.make_async_copy(up.at[pl.ds(start, rows)], up_buf.at[slot, there], load_sem.at[slot, 2 + i])
            )
        return copies

    def activate(j):
        slot = lax.rem(j, 2)
        for copy in loads(j):
            copy.wait()
        active[slot] = (
            jax.nn.gelu(gate_buf[slot].astype(jnp.float32), approximate=True)
            * up_buf[slot].astype(jnp.float32)
        ).astype(jnp.bfloat16)

    for copy in loads(0):
        copy.start()
    lag_copy.start()
    for copy in loads(1):
        copy.start()
    activate(0)
    meet(neighbours() + farther())

    def push_wide(cv, block, target, slot):
        color, part = lax.div(cv, 2), lax.rem(cv, 2)
        start = pl.multiple_of(block * rows + part * half, half)
        remote(
            wide.at[color, pl.ds(start, half)], wide_in.at[cv, slot], fold_wide_send, fold_wide_recv.at[cv, slot], target
        ).start()

    def push_slim(cv, block, target, slot):
        color, part = lax.div(cv, 2), lax.rem(cv, 2)
        start = pl.multiple_of(block * rows + part * half, half)
        remote(
            slim.at[color, pl.ds(start, half)], slim_in.at[cv, slot], fold_slim_send, fold_slim_recv.at[cv, slot], target
        ).start()

    def compute(j):
        ez, ex, other, mine = place(j)
        slot = lax.rem(j, 2)

        @pl.when(j + 2 < BLOCKS // 2)
        def _():
            for copy in loads(j + 2):
                copy.start()

        @pl.when(j + 1 < BLOCKS // 2)
        def _():
            for copy in loads(j + 1):
                copy.wait()

        later = 1 - slot
        active[later] = (
            jax.nn.gelu(gate_buf[later].astype(jnp.float32), approximate=True)
            * up_buf[later].astype(jnp.float32)
        ).astype(jnp.bfloat16)
        hidden = active[slot]
        places = [pl.ds(pl.multiple_of(block * rows, rows), rows) for block in (other, mine)]

        def product(begin, width):
            return (
                jnp.dot(hidden, lag[:, begin : begin + width], preferred_element_type=jnp.float32) * inv_root
            ).astype(jnp.bfloat16)

        for color in range(2):
            value = product(color * wcols, wcols)
            for i, here in enumerate(places):
                wide[color, here, :] = value[i * rows : (i + 1) * rows]
        for color in range(2):
            value = product(2 * wcols + color * scols, scols)
            for i, here in enumerate(places):
                slim[color, here, :] = value[i * rows : (i + 1) * rows]
        for i, here in enumerate(places):
            hid[:, here] = hidden[i * rows : (i + 1) * rows].T

        def leaf(cv):
            color, s = lax.div(cv, 2), 1 - 2 * lax.rem(cv, 2)
            sp, sq, p, q = axes_of(color)
            ep = jnp.where(color == 0, ex, ez)
            eq = jnp.where(color == 0, ez, ex)
            u = wrap(s * ep)
            push_slim(cv, other, flat(1 - y, z, x), ep * 4 + eq)

            @pl.when(u >= 2)
            def _():
                step = jnp.where(u == 2, s, -s)
                target = y * 16 + wrap(p + step) * sp + q * sq
                slot_of = jnp.where(u == 2, 0, 16) + eq * 2
                push_wide(cv, other, target, slot_of + 1)
                push_wide(cv, mine, target, slot_of)

        each(4, leaf)

    lag_copy.wait()
    each(BLOCKS // 2, compute)

    def gather(total, parts):
        def tile(i):
            at = pl.ds(pl.multiple_of(i * 16, 16), 16)
            value = total[at, :].astype(jnp.float32)
            for part in parts:
                value = value + part[at, :].astype(jnp.float32)
            total[at, :] = value.astype(jnp.bfloat16)

        each(half // 16, tile)

    def take_wide(cv, block, slots):
        color, part = lax.div(cv, 2), lax.rem(cv, 2)
        start = pl.multiple_of(block * rows + part * half, half)
        for slot in slots:
            remote(
                wide_in.at[cv, slot], wide_in.at[cv, slot], fold_wide_send, fold_wide_recv.at[cv, slot], flat(1 - y, z, x)
            ).wait_recv()
        gather(wide.at[color, pl.ds(start, half)], [wide_in.at[cv, slot] for slot in slots])

    def take_slim(cv, block, slots):
        color, part = lax.div(cv, 2), lax.rem(cv, 2)
        start = pl.multiple_of(block * rows + part * half, half)
        for slot in slots:
            remote(
                slim_in.at[cv, slot], slim_in.at[cv, slot], fold_slim_send, fold_slim_recv.at[cv, slot], flat(1 - y, z, x)
            ).wait_recv()
        gather(slim.at[color, pl.ds(start, half)], [slim_in.at[cv, slot] for slot in slots])

    def fold_wide_middle(k, cv):
        color, s = lax.div(cv, 2), 1 - 2 * lax.rem(cv, 2)
        sp, sq, p, q = axes_of(color)
        eq, ey = FAR[k // 2], 1 - k % 2
        block = lax.rem(y + ey, 2) * 16 + wrap(p + s) * sp + wrap(q + eq) * sq
        take_wide(cv, block, (eq * 2 + ey,))
        push_wide(cv, block, y * 16 + wrap(p + s) * sp + q * sq, 8 + eq * 2 + ey)

    def fold_wide_root(k, cv):
        color, s = lax.div(cv, 2), 1 - 2 * lax.rem(cv, 2)
        sp, sq, p, q = axes_of(color)
        eq, ey = FAR[k // 2], 1 - k % 2
        v = wrap(s * eq)
        block = lax.rem(y + ey, 2) * 16 + p * sp + wrap(q + eq) * sq
        arrived = (8 + eq * 2 + ey, 16 + eq * 2 + ey)
        if eq == 0:
            take_wide(cv, block, arrived + (26 + ey, 28 + ey) + ((30,) if ey == 0 else ()))
            if ey == 1:
                push_wide(cv, block, flat(1 - y, z, x), 30)
            return
        take_wide(cv, block, arrived)
        if eq != 2:

            @pl.when(v == 1)
            def _():
                take_wide(cv, block, (24 + ey,))

        step = jnp.where(v == 3, -s, s)
        slot = jnp.where(v == 2, 24, jnp.where(v == 3, 28, 26)) + ey
        push_wide(cv, block, y * 16 + p * sp + wrap(q + step) * sq, slot)

    def fold_slim_step(t, cv):
        color, s = lax.div(cv, 2), 1 - 2 * lax.rem(cv, 2)
        sq, sr, q, r = axes_of(color)
        er, eq = FAR[t // 4], FAR[t % 4]
        v, w = wrap(s * eq), wrap(s * er)
        block = y * 16 + wrap(q + eq) * sq + wrap(r + er) * sr
        if eq != 0:
            take_slim(cv, block, (eq * 4 + er,))
            if eq != 2:

                @pl.when(v == 1)
                def _():
                    take_slim(cv, block, (16 + er,))

            step = jnp.where(v == 3, -s, s)
            slot = jnp.where(v == 2, 16, jnp.where(v == 3, 24, 20)) + er
            push_slim(cv, block, y * 16 + wrap(q + step) * sq + r * sr, slot)
            return
        take_slim(cv, block, (er, 20 + er, 24 + er) + ((29, 30) if er == 0 else ()))
        if er in (1, 3):

            @pl.when(w == 1)
            def _():
                take_slim(cv, block, (28,))

        if er != 0:
            step = jnp.where(w == 3, -s, s)
            slot = jnp.where(w == 2, 28, jnp.where(w == 3, 30, 29))
            push_slim(cv, block, y * 16 + q * sq + wrap(r + step) * sr, slot)

    task_swap = remote_to(task_in, other_task, task_send, task_recv, (partner(), me))
    task_swap.start()
    total[...] = jnp.zeros_like(total)

    buckets_of = lax.broadcasted_iota(jnp.int32, (adv.shape[1], rows), 0)
    chosen = (buckets_of == buckets[...]).astype(jnp.float32)
    diagonal = (adv.shape[1], adv.shape[1])
    adv_column = jnp.sum(
        jnp.where(
            lax.broadcasted_iota(jnp.int32, diagonal, 0) == lax.broadcasted_iota(jnp.int32, diagonal, 1),
            jnp.broadcast_to(adv[...], diagonal),
            0.0,
        ),
        axis=1,
        keepdims=True,
    )
    scale[...] = lax.dot_general(
        chosen,
        jnp.broadcast_to(adv_column, (adv.shape[1], 128)),
        (((0,), (0,)), ((), ())),
        precision=lax.Precision.HIGHEST,
        preferred_element_type=jnp.float32,
    )
    own = pl.ds(pl.multiple_of(me * rows, rows), rows)

    def release(kind, received, send_sem, recv_sem):
        remote(received, received, send_sem, recv_sem.at[0, 0], flat(1 - y, z, x)).wait_send()
        for device in neighbours():
            pl.semaphore_signal(clear.at[kind], inc=1, device_id=device, device_id_type=MESH)

    def finish(ref, begin):
        width = ref.shape[2]
        for color in range(2):
            for i in range(width // 128):
                lanes = slice(i * 128, (i + 1) * 128)
                first = begin + color * width + i * 128
                weighted = scale[...] * cot[:, first : first + 128].astype(jnp.float32)
                gap = ref[color, own, lanes].astype(jnp.float32)
                ref[color, own, lanes] = (weighted + kl_coef * gap).astype(jnp.bfloat16)

    task = "task"
    task_pieces = task_in.shape[0] // half

    def load_task():
        def rows_from(j):
            at = pl.ds(pl.multiple_of(j * half, half), half)
            for i in range(task_in.shape[1] // wcols):
                columns = pl.ds(i * wcols, wcols)
                pltpu.make_async_copy(task_in.at[at, columns], wide_in.at[i, j], task_sem).start()

        each(task_pieces, rows_from)

    def wait_for_task():
        everything = wide_in.at[pl.ds(0, task_in.shape[1] // wcols), pl.ds(0, task_pieces)]
        pltpu.make_async_copy(everything, everything, task_sem).wait()

    def read(ref, k, lanes):
        if ref is not task:
            return ref[tile_at(k), lanes].astype(jnp.float32)
        tiles = half // 16
        at = pl.ds(pl.multiple_of(lax.rem(k, tiles) * 16, 16), 16)
        start = lanes.start % wcols
        return wide_in[lanes.start // wcols, lax.div(k, tiles), at, start : start + 128].astype(jnp.float32)

    def piece(ref, cv, block):
        color, part = lax.div(cv, 2), lax.rem(cv, 2)
        start = pl.multiple_of(block * rows + part * half, half)
        return ref.at[color, pl.ds(start, half)]

    def send_wide(cv, block, target, slot):
        here = piece(wide, cv, block)
        remote(here, here, wide_send, wide_recv.at[cv, slot], target).start()

    def send_slim(cv, block, target, slot):
        here = piece(slim, cv, block)
        remote(here, here, slim_send, slim_recv.at[cv, slot], target).start()

    def wait_wide(cv, block, slot):
        here = piece(wide, cv, block)
        remote(here, here, wide_send, wide_recv.at[cv, slot], flat(1 - y, z, x)).wait_recv()

    def wait_slim(cv, block, slot):
        here = piece(slim, cv, block)
        remote(here, here, slim_send, slim_recv.at[cv, slot], flat(1 - y, z, x)).wait_recv()

    def wide_root(n, cv):
        color, s = lax.div(cv, 2), 1 - 2 * lax.rem(cv, 2)
        sp, sq, p, q = axes_of(color)
        oq, oy = NEAR[n // 2], n % 2
        b = wrap(s * oq)
        block = lax.rem(y + oy, 2) * 16 + p * sp + wrap(q - oq) * sq
        slot = oy * 16 + oq * 4
        if n > 0:
            wait_wide(cv, block, slot)
        else:
            send_wide(cv, block, flat(1 - y, z, x), 16)

        def forward():
            send_wide(cv, block, y * 16 + p * sp + wrap(q + s) * sq, oy * 16 + wrap(oq + s) * 4)

        if oq == 0:
            forward()
            send_wide(cv, block, y * 16 + p * sp + wrap(q - s) * sq, oy * 16 + wrap(oq - s) * 4)
        elif oq != 2:
            pl.when(b == 1)(forward)
        send_wide(cv, block, y * 16 + wrap(p + s) * sp + q * sq, slot + wrap(s))
        send_wide(cv, block, y * 16 + wrap(p - s) * sp + q * sq, slot + wrap(-s))

    def wide_middle(n, cv):
        color, s = lax.div(cv, 2), 1 - 2 * lax.rem(cv, 2)
        sp, sq, p, q = axes_of(color)
        oq, oy = NEAR[n // 2], n % 2
        block = lax.rem(y + oy, 2) * 16 + wrap(p - s) * sp + wrap(q - oq) * sq
        slot = oy * 16 + oq * 4
        wait_wide(cv, block, slot + wrap(s))
        send_wide(cv, block, y * 16 + wrap(p + s) * sp + q * sq, slot + 2)

    def wide_leaf(cv, n):
        color, s = lax.div(cv, 2), 1 - 2 * lax.rem(cv, 2)
        sp, sq, p, q = axes_of(color)
        oq, oy = near_first(lax.div(n, 2)), lax.rem(n, 2)
        slot = oy * 16 + oq * 4
        base = lax.rem(y + oy, 2) * 16 + wrap(q - oq) * sq
        wait_wide(cv, base + wrap(p + s) * sp, slot + wrap(-s))
        wait_wide(cv, base + wrap(p + 2) * sp, slot + 2)

    def slim_step(t, cv):
        color, s = lax.div(cv, 2), 1 - 2 * lax.rem(cv, 2)
        sq, sr, q, r = axes_of(color)
        orr, oq = NEAR[t // 4], NEAR[t % 4]
        b, c = wrap(s * oq), wrap(s * orr)
        block = y * 16 + wrap(q - oq) * sq + wrap(r - orr) * sr
        slot = orr * 4 + oq
        if t > 0:
            wait_slim(cv, block, slot)
        send_slim(cv, block, flat(1 - y, z, x), 16 + slot)

        def forward_third():
            send_slim(cv, block, y * 16 + q * sq + wrap(r + s) * sr, wrap(orr + s) * 4)

        def forward_second():
            send_slim(cv, block, y * 16 + wrap(q + s) * sq + r * sr, orr * 4 + wrap(oq + s))

        if oq == 0:
            if orr == 0:
                forward_third()
                send_slim(cv, block, y * 16 + q * sq + wrap(r - s) * sr, wrap(orr - s) * 4)
            elif orr != 2:
                pl.when(c == 1)(forward_third)
            forward_second()
            send_slim(cv, block, y * 16 + wrap(q - s) * sq + r * sr, orr * 4 + wrap(oq - s))
        elif oq != 2:
            pl.when(b == 1)(forward_second)

    def slim_leaf(cv, n):
        color = lax.div(cv, 2)
        sq, sr, q, r = axes_of(color)
        orr, oy = near_first(lax.div(n, 2)), lax.rem(n, 2)

        @pl.when(oy == 1)
        def _():
            def one(oq):
                block = (1 - y) * 16 + wrap(q - oq) * sq + wrap(r - orr) * sr
                wait_slim(cv, block, 16 + orr * 4 + oq)

            each(4, one)

    def parts_of(n):
        each(4, lambda cv: wide_leaf(cv, n))
        each(4, lambda cv: slim_leaf(cv, n))
        oo, oy = near_first(lax.div(n, 2)), lax.rem(n, 2)
        yy = lax.rem(y + oy, 2)
        for color in range(2):
            if color == 0:
                start = pl.multiple_of((yy * 4 + wrap(z - oo)) * 4 * rows, 4 * rows)
                at = [pl.ds(start, 4 * rows)]
            else:
                start = yy * 16 + wrap(x - oo)
                at = [pl.ds(pl.multiple_of((start + 4 * i) * rows, rows), rows) for i in range(4)]
            left = jnp.concatenate([hid[:, a] for a in at], axis=1)
            for ref, begin in ((wide, color * wcols), (slim, 2 * wcols + color * scols)):
                right = jnp.concatenate([ref[color, a, :] for a in at], axis=0)
                yield begin, jnp.dot(left, right, preferred_element_type=jnp.float32)

    band = 128
    tile = 16
    zero = jnp.zeros((tile, 128), jnp.float32)
    ff, cols = grad.shape

    def products(pairs, sums_of, k, columns):
        done = list(sums_of)
        for i in range(columns.start // 128, columns.stop // 128):
            lanes = slice(i * 128, (i + 1) * 128)
            values = {}
            for pair, (one, two) in enumerate(pairs):
                for ref in (one, two):
                    if id(ref) not in values:
                        values[id(ref)] = read(ref, k, lanes)
                done[pair] = done[pair] + values[id(one)] * values[id(two)]
        return tuple(done)

    def sum_products(pairs, start, columns):
        return lax.fori_loop(
            0, ff // tile, lambda k, sums_of: products(pairs, sums_of, k, columns), start
        )

    def tile_at(i):
        return pl.ds(pl.multiple_of(i * tile, tile), tile)

    column_parts = [
        slice(0, wcols),
        slice(2 * wcols, 2 * wcols + scols),
        slice(wcols, 2 * wcols),
        slice(2 * wcols + scols, cols),
    ]

    def grad_copy(part):
        columns = pl.ds(column_parts[part].start, column_parts[part].stop - column_parts[part].start)
        return remote_to(
            grad.at[:, columns], other_grad.at[:, columns], grad_send, grad_recv.at[part], (partner(), me)
        )

    bodies = {
        "m": fold_wide_middle,
        "r": fold_wide_root,
        "s": fold_slim_step,
        "M": wide_middle,
        "R": wide_root,
        "S": slim_step,
    }
    for step in " ".join(ORDER[0]).split():
        if step == "R0":
            pl.semaphore_wait(clear.at[0], 5)
        if step == "S0":
            pl.semaphore_wait(clear.at[1], 5)
        steps_of((step,), bodies)
        if step == "r7":
            release(0, wide_in, fold_wide_send, fold_wide_recv)
            finish(wide, 0)
            load_task()
        if step == "s15":
            release(1, slim_in, fold_slim_send, fold_slim_recv)
            finish(slim, 2 * wcols)
    wait_for_task()
    task_swap.wait_recv()
    tasks = sum_products(((task, task), (task, other_task)), (zero, zero), slice(0, cols))

    def group(n):
        for i in range(1, len(ORDER) - 1):
            pl.when(n == i)(functools.partial(steps_of, ORDER[i], bodies))
        for begin, product in parts_of(n):
            total[:, begin : begin + product.shape[1]] += product

    each(7, group)
    steps_of(ORDER[7], bodies)
    kept = (zero, zero, zero)
    for part, (begin, product) in enumerate(parts_of(7)):
        columns = column_parts[part]
        grad[:, columns] = ((total[:, columns] + product) * inv_root).astype(jnp.bfloat16)
        grad_copy(part).start()
        kept = sum_products(((grad, grad), (task, grad), (other_task, grad)), kept, columns)
    crossed = (zero,)
    for part in range(4):
        grad_copy(part).wait_recv()
        crossed = sum_products(((grad, other_grad),), crossed, column_parts[part])
    for i, value in enumerate(kept + tasks + crossed):
        sums[0, i : i + 1, :] = jnp.sum(value, axis=0, keepdims=True)
    sums[0, 6:8, :] = jnp.zeros((2, 128), jnp.float32)

    def exchange(source, slots, devices):
        copies = [
            remote_to(sums.at[source], sums_in.at[slot], sums_send, sums_recv.at[slot], device)
            for slot, device in zip(slots, devices)
        ]
        for copy in copies:
            copy.start()
        for copy in copies:
            copy.wait_recv()

    pol = lax.axis_index("pol")
    exchange(0, (0, 1, 2), [(pol, flat(y, z, wrap(x + i))) for i in (1, 2, 3)])
    sums[1] = sums[0] + sums_in[0] + sums_in[1] + sums_in[2]
    exchange(1, (3, 4, 5), [(pol, flat(y, wrap(z + i), x)) for i in (1, 2, 3)])
    sums[2] = sums[1] + sums_in[3] + sums_in[4] + sums_in[5]
    exchange(2, (6, 7, 8), [(pol, flat(1 - y, z, x)), (partner(), me), (partner(), flat(1 - y, z, x))])
    own_sums = jnp.sum(sums[2] + sums_in[6], axis=1, keepdims=True)
    part_sums = jnp.sum(sums_in[7] + sums_in[8], axis=1, keepdims=True)

    def spread_row(column, i):
        return jnp.broadcast_to(column[i : i + 1], (1, 128))

    grad_oo, tgrad_oo, tgrad_po, task_oo, task_op, grad_op = (spread_row(own_sums, i) for i in range(6))
    grad_pp, tgrad_pp, tgrad_op, task_pp = (spread_row(part_sums, i) for i in range(4))
    is_first = lax.rem(pol, 2) == 0
    scale_own = step_rate * clip_factor(grad_oo)
    scale_part = step_rate * clip_factor(grad_pp)
    own_total = task_oo - 2.0 * scale_own * tgrad_oo + scale_own * scale_own * grad_oo
    part_total = task_pp - 2.0 * scale_part * tgrad_pp + scale_part * scale_part * grad_pp
    cross_dot = (
        task_op - scale_part * tgrad_op - scale_own * tgrad_po + scale_own * scale_part * grad_op
    )
    first_sq = jnp.where(is_first, own_total, part_total)
    second_sq = jnp.where(is_first, part_total, own_total)
    weight_first, weight_second = slerp_weights(first_sq, second_sq, cross_dot)
    weight_own = jnp.where(is_first, weight_first, weight_second)
    weight_part = jnp.where(is_first, weight_second, weight_first)

    for i in range(ff // band):

        def settle_outputs(k):
            at = tile_at(k)
            for i in range(cols // 128):
                lanes = slice(i * 128, (i + 1) * 128)
                update = scale_own * grad[at, lanes].astype(jnp.float32)
                delta_own = read(task, k, lanes) - update
                delta_part = other_task[at, lanes].astype(jnp.float32) - scale_part * other_grad[
                    at, lanes
                ].astype(jnp.float32)
                lag[at, lanes] = ((1.0 - ema_rate) * (lag[at, lanes].astype(jnp.float32) - update)).astype(
                    jnp.bfloat16
                )
                other_grad[at, lanes] = (weight_own * delta_own + weight_part * delta_part).astype(jnp.bfloat16)

        each(band // tile, lambda k: settle_outputs(i * (band // tile) + k))
        at = pl.ds(i * band, band)
        pltpu.make_async_copy(lag.at[at], lag_out.at[at], out_sem.at[0]).start()
        pltpu.make_async_copy(other_grad.at[at], merged_out.at[at], out_sem.at[1]).start()

    pltpu.make_async_copy(lag, lag_out, out_sem.at[0]).wait()
    pltpu.make_async_copy(other_grad, merged_out, out_sem.at[1]).wait()
    task_swap.wait_send()
    remote_to(grad, other_grad, grad_send, grad_recv.at[0], (partner(), me)).wait_send()
    remote_to(sums_in, sums_in, sums_send, sums_recv.at[0], (partner(), me)).wait_send()
    sent = pl.ds(0, (BLOCKS - 1) * rows)
    remote(wide.at[:, sent], wide.at[:, sent], wide_send, wide_recv.at[0, 0], flat(1 - y, z, x)).wait_send()
    remote(slim.at[:, sent], slim.at[:, sent], slim_send, slim_recv.at[0, 0], flat(1 - y, z, x)).wait_send()


def shards(gate_pre, up_pre, lag, task, cotangent, buckets, advantages):
    tokens, ff = gate_pre.shape[1:]
    cols = lag.shape[2]
    rows = tokens // BLOCKS
    half = rows // 2
    wcols, scols = cols // 3, cols // 6
    any_spec = pl.BlockSpec(memory_space=pl.ANY)
    vmem_spec = pl.BlockSpec(memory_space=pltpu.VMEM)
    bf16 = jnp.bfloat16
    dma = pltpu.SemaphoreType.DMA
    per_stream = [dma, dma, dma((4, BLOCKS)), dma((4, BLOCKS))]
    new_lag, merged = pl.pallas_call(
        step_kernel,
        name="policy_step",
        out_shape=(jax.ShapeDtypeStruct((ff, cols), bf16), jax.ShapeDtypeStruct((ff, cols), bf16)),
        in_specs=[any_spec] * 4 + [vmem_spec] * 3,
        out_specs=(any_spec, any_spec),
        scratch_shapes=[
            *[pltpu.VMEM((2, 2 * rows, ff), bf16)] * 3,
            pltpu.VMEM((ff, cols), bf16),
            pltpu.VMEM((ff, tokens), bf16),
            pltpu.VMEM((2, tokens, wcols), bf16),
            pltpu.VMEM((2, tokens, scols), bf16),
            pltpu.VMEM((4, BLOCKS - 1, half, wcols), bf16),
            pltpu.VMEM((4, BLOCKS - 1, half, scols), bf16),
            pltpu.VMEM((ff, cols), jnp.float32),
            *[pltpu.VMEM((ff, cols), bf16)] * 3,
            pltpu.VMEM((rows, 128), jnp.float32),
            pltpu.VMEM((3, 8, 128), jnp.float32),
            pltpu.VMEM((9, 8, 128), jnp.float32),
            dma((2, 4)),
            dma,
            dma,
            dma,
            dma,
            dma((4,)),
            dma((2,)),
            dma,
            dma((9,)),
            *per_stream,
            *per_stream,
            pltpu.SemaphoreType.REGULAR((2,)),
        ],
        compiler_params=pltpu.CompilerParams(
            collective_id=0, has_side_effects=True, vmem_limit_bytes=VMEM_BYTES
        ),
        cost_estimate=pl.CostEstimate(
            flops=4 * tokens * ff * cols, bytes_accessed=6 * tokens * ff, transcendentals=tokens * ff
        ),
    )(gate_pre[0], up_pre[0], lag[0], task[0], cotangent[0], buckets, advantages)
    return (new_lag[None], merged[None])


def solution(mesh):
    return jax.shard_map(
        shards,
        mesh=mesh,
        in_specs=(
            P("pol", None, "fsdp"),
            P("pol", None, "fsdp"),
            P("pol", "fsdp", None),
            P("pol", "fsdp", None),
            P("pol", "fsdp", None),
            P("pol", "fsdp"),
            P("pol", None),
        ),
        out_specs=(P("pol", "fsdp", None), P("pol", "fsdp", None)),
        check_vma=False,
    )
```

```python
import functools
import math

import jax
import jax.numpy as jnp
from jax import lax
from jax.experimental import pallas as pl
from jax.experimental.pallas import tpu as pltpu
from jax.sharding import PartitionSpec as P

D = 2304
FF = 20480

kl_coef = 0.5
clip_level = 0.15
step_rate = 8.0
ema_rate = 0.1

MESH = pl.DeviceIdType.MESH
VMEM_BYTES = 67_000_000
RING = 4
BLOCKS = 32


def slerp_weights(first_sq, second_sq, cross_dot):
    norm_first = jnp.sqrt(first_sq)
    norm_second = jnp.sqrt(second_sq)
    blend = norm_second / (norm_first + norm_second)
    cosine = jnp.clip(cross_dot / (norm_first * norm_second), -1.0, 1.0)
    opening = jnp.arctan2(jnp.sqrt((1.0 - cosine) * (1.0 + cosine)), cosine)
    sine_val = jnp.sin(opening)
    weight_first = jnp.sin((1.0 - blend) * opening) / sine_val
    weight_second = jnp.sin(blend * opening) / sine_val
    return (weight_first, weight_second)


def clip_factor(grad_sq):
    return jnp.minimum(1.0, clip_level / (jnp.sqrt(grad_sq / (FF * D)) + 1e-06))


def position():
    me = lax.axis_index("fsdp")
    return lax.div(me, 16), lax.rem(lax.div(me, 4), 4), lax.rem(me, 4)


def wrap(value):
    return lax.rem(value + 2 * RING, RING)


def flat(y, z, x):
    return y * 16 + z * 4 + x


FAR = (2, 3, 1, 0)
NEAR = (0, 1, 3, 2)

ORDER = (
    ("s0 s4 m0 m2", "m5 m3 m1 m4", "m6 m7 s1 s5", "s8 s2 r0 s6", "r1 s12 s10 s3", "s9 r2 r4 s13", "s7 s14 s11 r3", "r5 r6 s15 S0", "r7 R0 S1 S2", "S4 S8 M0 R1", "R4 R2 S3 S6", "S5 S10 S9 S12"),
    ("M1 R3 R5 M4", "R6 M2 S7 S11", "S13 S14"),
    ("M3 M5 R7",),
    ("M6",),
    ("S15",),
    (),
    ("M7",),
    (),
)
GROUPS = (0, 1, 4, 2, 3, 5, 6, 7)


def far_first(index):
    return jnp.where(index == 0, 2, jnp.where(index == 1, 3, jnp.where(index == 2, 1, 0)))


def near_first(index):
    return jnp.where(index == 2, 3, jnp.where(index == 3, 2, index))


def steps_of(order, bodies):
    for step in " ".join(order).split():
        body, index = bodies[step[0]], int(step[1:])
        each(4, functools.partial(body, index))


def each(count, body):
    lax.fori_loop(0, count, lambda i, _: (body(i), None)[1], None)


def partner():
    pol = lax.axis_index("pol")
    return pol + 1 - 2 * lax.rem(pol, 2)


def neighbours():
    y, z, x = position()
    pol = lax.axis_index("pol")
    return [
        (pol, flat(y, z, wrap(x + 1))),
        (pol, flat(y, z, wrap(x - 1))),
        (pol, flat(y, wrap(z + 1), x)),
        (pol, flat(y, wrap(z - 1), x)),
        (pol, flat(1 - y, z, x)),
    ]


def plane():
    y, z, x = position()
    offsets = sorted(((i, j) for i in range(4) for j in range(4) if i or j), key=lambda o: o.count(2) * 4 - o.count(0))
    offsets.reverse()
    return [(lax.axis_index("pol"), flat(y, wrap(z + i), wrap(x + j))) for i, j in offsets]


def across():
    y, z, x = position()
    return [
        (partner(), flat(1 - y, z, x)),
        (lax.axis_index("pol"), flat(1 - y, z, x)),
        (partner(), flat(y, z, x)),
    ]


def greet(devices):
    for device in devices:
        pl.semaphore_signal(pltpu.get_barrier_semaphore(), inc=1, device_id=device, device_id_type=MESH)


def meet(devices):
    pl.semaphore_wait(pltpu.get_barrier_semaphore(), len(devices))


def remote(src, dst, send_sem, recv_sem, target):
    return remote_to(src, dst, send_sem, recv_sem, (lax.axis_index("pol"), target))


def remote_to(src, dst, send_sem, recv_sem, device):
    return pltpu.make_async_remote_copy(
        src_ref=src,
        dst_ref=dst,
        send_sem=send_sem,
        recv_sem=recv_sem,
        device_id=device,
        device_id_type=MESH,
    )


def axes_of(color):
    _, z, x = position()
    first = jnp.where(color == 0, x, z)
    second = jnp.where(color == 0, z, x)
    return 1 + 3 * color, 4 - 3 * color, first, second


def step_kernel(
    gate, up, lag_in, task_in, cot, buckets, adv,
    lag_out, merged_out,
    gate_buf, up_buf, active, lag, hid, wide, slim, wide_in, slim_in,
    total, other_task, grad, other_grad, scale, sums, sums_in,
    load_sem, lag_sem, task_sem, task_send, task_recv, grad_send, grad_recv, out_sem, sums_send, sums_recv,
    fold_wide_send, fold_slim_send, fold_wide_recv, fold_slim_recv,
    wide_send, slim_send, wide_recv, slim_recv, clear,
):
    y, z, x = position()
    rows = gate_buf.shape[1] // 2
    me = flat(y, z, x)
    half = rows // 2
    wcols, scols = wide.shape[2], slim.shape[2]
    inv_root = 1.0 / math.sqrt(FF)
    greet(plane() + across())
    lag_copies = []
    for i, columns in enumerate((pl.ds(0, wcols), pl.ds(wcols, wcols), pl.ds(2 * wcols, 2 * scols))):
        lag_copies.append(pltpu.make_async_copy(lag_in.at[:, columns], lag.at[:, columns], lag_sem.at[i]))

    def place(j):
        ez, ex = far_first(lax.div(j, 4)), far_first(lax.rem(j, 4))
        return ez, ex, flat(1 - y, wrap(z + ez), wrap(x + ex)), flat(y, wrap(z + ez), wrap(x + ex))

    def loads(j):
        slot = lax.rem(j, 2)
        copies = []
        for i, block in enumerate(place(j)[2:]):
            start = pl.multiple_of(block * rows, rows)
            there = pl.ds(i * rows, rows)
            copies.append(
                pltpu.make_async_copy(gate.at[pl.ds(start, rows)], gate_buf.at[slot, there], load_sem.at[slot, i])
            )
            copies.append(
                pltpu.make_async_copy(up.at[pl.ds(start, rows)], up_buf.at[slot, there], load_sem.at[slot, 2 + i])
            )
        return copies

    def activate(j):
        slot = lax.rem(j, 2)
        for copy in loads(j):
            copy.wait()
        active[slot] = (
            jax.nn.gelu(gate_buf[slot].astype(jnp.float32), approximate=True)
            * up_buf[slot].astype(jnp.float32)
        ).astype(jnp.bfloat16)

    for copy in loads(0) + lag_copies + loads(1):
        copy.start()
    activate(0)

    def push_wide(cv, block, target, slot):
        color, part = lax.div(cv, 2), lax.rem(cv, 2)
        start = pl.multiple_of(block * rows + part * half, half)
        remote(
            wide.at[color, pl.ds(start, half)], wide_in.at[cv, slot], fold_wide_send, fold_wide_recv.at[cv, slot], target
        ).start()

    def push_slim(cv, block, target, slot):
        color, part = lax.div(cv, 2), lax.rem(cv, 2)
        start = pl.multiple_of(block * rows + part * half, half)
        remote(
            slim.at[color, pl.ds(start, half)], slim_in.at[cv, slot], fold_slim_send, fold_slim_recv.at[cv, slot], target
        ).start()

    def product(hidden, begin, width):
        return (
            jnp.dot(hidden, lag[:, begin : begin + width], preferred_element_type=jnp.float32) * inv_root
        ).astype(jnp.bfloat16)

    def keep_product(j, ref, color, begin):
        value = product(active[lax.rem(j, 2)], begin, ref.shape[2])
        for i, block in enumerate(place(j)[2:]):
            here = pl.ds(pl.multiple_of(block * rows, rows), rows)
            ref[color, here, :] = value[i * rows : (i + 1) * rows]

    def keep_hidden(j):
        hidden = active[lax.rem(j, 2)]
        for i, block in enumerate(place(j)[2:]):
            here = pl.ds(pl.multiple_of(block * rows, rows), rows)
            hid[:, here] = hidden[i * rows : (i + 1) * rows].T

    def activate_next(j):
        later = 1 - lax.rem(j, 2)
        active[later] = (
            jax.nn.gelu(gate_buf[later].astype(jnp.float32), approximate=True)
            * up_buf[later].astype(jnp.float32)
        ).astype(jnp.bfloat16)

    def leaf_wide(j, cv):
        ez, ex, other, mine = place(j)
        color, s = lax.div(cv, 2), 1 - 2 * lax.rem(cv, 2)
        sp, sq, p, q = axes_of(color)
        ep = jnp.where(color == 0, ex, ez)
        eq = jnp.where(color == 0, ez, ex)
        u = wrap(s * ep)

        @pl.when(u >= 2)
        def _():
            step = jnp.where(u == 2, s, -s)
            target = y * 16 + wrap(p + step) * sp + q * sq
            slot_of = jnp.where(u == 2, 0, 16) + eq * 2
            push_wide(cv, other, target, slot_of + 1)
            push_wide(cv, mine, target, slot_of)

    def leaf_slim(j, cv):
        ez, ex, other, _ = place(j)
        color = lax.div(cv, 2)
        ep = jnp.where(color == 0, ex, ez)
        eq = jnp.where(color == 0, ez, ex)
        push_slim(cv, other, flat(1 - y, z, x), ep * 4 + eq)

    def compute(j):
        @pl.when(j + 2 < BLOCKS // 2)
        def _():
            for copy in loads(j + 2):
                copy.start()

        @pl.when(j + 1 < BLOCKS // 2)
        def _():
            for copy in loads(j + 1):
                copy.wait()

        activate_next(j)
        for color in range(2):
            keep_product(j, wide, color, color * wcols)
        for color in range(2):
            keep_product(j, slim, color, 2 * wcols + color * scols)
        keep_hidden(j)

        def leaves(cv):
            leaf_slim(j, cv)
            leaf_wide(j, cv)

        each(4, leaves)

    for color in range(2):
        lag_copies[color].wait()
        keep_product(0, wide, color, color * wcols)
        if color == 0:
            meet(plane() + across())
        each(2, lambda i: leaf_wide(0, 2 * color + i))
    lag_copies[2].wait()
    for color in range(2):
        keep_product(0, slim, color, 2 * wcols + color * scols)
        each(2, lambda i: leaf_slim(0, 2 * color + i))
    for copy in loads(2):
        copy.start()
    for copy in loads(1):
        copy.wait()
    keep_hidden(0)
    activate_next(0)
    each(BLOCKS // 2 - 1, lambda j: compute(j + 1))

    def gather(total, parts):
        def tile(i):
            at = pl.ds(pl.multiple_of(i * 16, 16), 16)
            value = total[at, :].astype(jnp.float32)
            for part in parts:
                value = value + part[at, :].astype(jnp.float32)
            total[at, :] = value.astype(jnp.bfloat16)

        each(half // 16, tile)

    def take_wide(cv, block, slots):
        color, part = lax.div(cv, 2), lax.rem(cv, 2)
        start = pl.multiple_of(block * rows + part * half, half)
        for slot in slots:
            remote(
                wide_in.at[cv, slot], wide_in.at[cv, slot], fold_wide_send, fold_wide_recv.at[cv, slot], flat(1 - y, z, x)
            ).wait_recv()
        gather(wide.at[color, pl.ds(start, half)], [wide_in.at[cv, slot] for slot in slots])

    def take_slim(cv, block, slots):
        color, part = lax.div(cv, 2), lax.rem(cv, 2)
        start = pl.multiple_of(block * rows + part * half, half)
        for slot in slots:
            remote(
                slim_in.at[cv, slot], slim_in.at[cv, slot], fold_slim_send, fold_slim_recv.at[cv, slot], flat(1 - y, z, x)
            ).wait_recv()
        gather(slim.at[color, pl.ds(start, half)], [slim_in.at[cv, slot] for slot in slots])

    def fold_wide_middle(k, cv):
        color, s = lax.div(cv, 2), 1 - 2 * lax.rem(cv, 2)
        sp, sq, p, q = axes_of(color)
        eq, ey = FAR[k // 2], 1 - k % 2
        block = lax.rem(y + ey, 2) * 16 + wrap(p + s) * sp + wrap(q + eq) * sq
        take_wide(cv, block, (eq * 2 + ey,))
        push_wide(cv, block, y * 16 + wrap(p + s) * sp + q * sq, 8 + eq * 2 + ey)

    def fold_wide_root(k, cv):
        color, s = lax.div(cv, 2), 1 - 2 * lax.rem(cv, 2)
        sp, sq, p, q = axes_of(color)
        eq, ey = FAR[k // 2], 1 - k % 2
        v = wrap(s * eq)
        block = lax.rem(y + ey, 2) * 16 + p * sp + wrap(q + eq) * sq
        arrived = (8 + eq * 2 + ey, 16 + eq * 2 + ey)
        if eq == 0:
            take_wide(cv, block, arrived + (26 + ey, 28 + ey) + ((30,) if ey == 0 else ()))
            if ey == 1:
                push_wide(cv, block, flat(1 - y, z, x), 30)
            return
        take_wide(cv, block, arrived)
        if eq != 2:

            @pl.when(v == 1)
            def _():
                take_wide(cv, block, (24 + ey,))

        step = jnp.where(v == 3, -s, s)
        slot = jnp.where(v == 2, 24, jnp.where(v == 3, 28, 26)) + ey
        push_wide(cv, block, y * 16 + p * sp + wrap(q + step) * sq, slot)

    def fold_slim_step(t, cv):
        color, s = lax.div(cv, 2), 1 - 2 * lax.rem(cv, 2)
        sq, sr, q, r = axes_of(color)
        er, eq = FAR[t // 4], FAR[t % 4]
        v, w = wrap(s * eq), wrap(s * er)
        block = y * 16 + wrap(q + eq) * sq + wrap(r + er) * sr
        if eq != 0:
            take_slim(cv, block, (eq * 4 + er,))
            if eq != 2:

                @pl.when(v == 1)
                def _():
                    take_slim(cv, block, (16 + er,))

            step = jnp.where(v == 3, -s, s)
            slot = jnp.where(v == 2, 16, jnp.where(v == 3, 24, 20)) + er
            push_slim(cv, block, y * 16 + wrap(q + step) * sq + r * sr, slot)
            return
        take_slim(cv, block, (er, 20 + er, 24 + er) + ((29, 30) if er == 0 else ()))
        if er in (1, 3):

            @pl.when(w == 1)
            def _():
                take_slim(cv, block, (28,))

        if er != 0:
            step = jnp.where(w == 3, -s, s)
            slot = jnp.where(w == 2, 28, jnp.where(w == 3, 30, 29))
            push_slim(cv, block, y * 16 + q * sq + wrap(r + step) * sr, slot)

    task_swap = remote_to(task_in, other_task, task_send, task_recv, (partner(), me))
    task_swap.start()
    total[...] = jnp.zeros_like(total)

    buckets_of = lax.broadcasted_iota(jnp.int32, (adv.shape[1], rows), 0)
    chosen = (buckets_of == buckets[...]).astype(jnp.float32)
    diagonal = (adv.shape[1], adv.shape[1])
    adv_column = jnp.sum(
        jnp.where(
            lax.broadcasted_iota(jnp.int32, diagonal, 0) == lax.broadcasted_iota(jnp.int32, diagonal, 1),
            jnp.broadcast_to(adv[...], diagonal),
            0.0,
        ),
        axis=1,
        keepdims=True,
    )
    scale[...] = lax.dot_general(
        chosen,
        jnp.broadcast_to(adv_column, (adv.shape[1], 128)),
        (((0,), (0,)), ((), ())),
        precision=lax.Precision.HIGHEST,
        preferred_element_type=jnp.float32,
    )
    own = pl.ds(pl.multiple_of(me * rows, rows), rows)

    def release(kind, received, send_sem, recv_sem):
        remote(received, received, send_sem, recv_sem.at[0, 0], flat(1 - y, z, x)).wait_send()
        for device in neighbours():
            pl.semaphore_signal(clear.at[kind], inc=1, device_id=device, device_id_type=MESH)

    def finish(ref, begin):
        width = ref.shape[2]
        for color in range(2):
            for i in range(width // 128):
                lanes = slice(i * 128, (i + 1) * 128)
                first = begin + color * width + i * 128
                weighted = scale[...] * cot[:, first : first + 128].astype(jnp.float32)
                gap = ref[color, own, lanes].astype(jnp.float32)
                ref[color, own, lanes] = (weighted + kl_coef * gap).astype(jnp.bfloat16)

    task = "task"
    task_pieces = task_in.shape[0] // half

    def load_task():
        def rows_from(j):
            at = pl.ds(pl.multiple_of(j * half, half), half)
            for i in range(task_in.shape[1] // wcols):
                columns = pl.ds(i * wcols, wcols)
                pltpu.make_async_copy(task_in.at[at, columns], wide_in.at[i, j], task_sem).start()

        each(task_pieces, rows_from)

    def wait_for_task():
        everything = wide_in.at[pl.ds(0, task_in.shape[1] // wcols), pl.ds(0, task_pieces)]
        pltpu.make_async_copy(everything, everything, task_sem).wait()

    def read(ref, k, lanes):
        if ref is not task:
            return ref[tile_at(k), lanes].astype(jnp.float32)
        tiles = half // 16
        at = pl.ds(pl.multiple_of(lax.rem(k, tiles) * 16, 16), 16)
        start = lanes.start % wcols
        return wide_in[lanes.start // wcols, lax.div(k, tiles), at, start : start + 128].astype(jnp.float32)

    def piece(ref, cv, block):
        color, part = lax.div(cv, 2), lax.rem(cv, 2)
        start = pl.multiple_of(block * rows + part * half, half)
        return ref.at[color, pl.ds(start, half)]

    def send_wide(cv, block, target, slot):
        here = piece(wide, cv, block)
        remote(here, here, wide_send, wide_recv.at[cv, slot], target).start()

    def send_slim(cv, block, target, slot):
        here = piece(slim, cv, block)
        remote(here, here, slim_send, slim_recv.at[cv, slot], target).start()

    def wait_wide(cv, block, slot):
        here = piece(wide, cv, block)
        remote(here, here, wide_send, wide_recv.at[cv, slot], flat(1 - y, z, x)).wait_recv()

    def wait_slim(cv, block, slot):
        here = piece(slim, cv, block)
        remote(here, here, slim_send, slim_recv.at[cv, slot], flat(1 - y, z, x)).wait_recv()

    def wide_root(n, cv):
        color, s = lax.div(cv, 2), 1 - 2 * lax.rem(cv, 2)
        sp, sq, p, q = axes_of(color)
        oq, oy = NEAR[n // 2], n % 2
        b = wrap(s * oq)
        block = lax.rem(y + oy, 2) * 16 + p * sp + wrap(q - oq) * sq
        slot = oy * 16 + oq * 4
        if n > 0:
            wait_wide(cv, block, slot)
        else:
            send_wide(cv, block, flat(1 - y, z, x), 16)

        def forward():
            send_wide(cv, block, y * 16 + p * sp + wrap(q + s) * sq, oy * 16 + wrap(oq + s) * 4)

        if oq == 0:
            forward()
            send_wide(cv, block, y * 16 + p * sp + wrap(q - s) * sq, oy * 16 + wrap(oq - s) * 4)
        elif oq != 2:
            pl.when(b == 1)(forward)
        send_wide(cv, block, y * 16 + wrap(p + s) * sp + q * sq, slot + wrap(s))
        send_wide(cv, block, y * 16 + wrap(p - s) * sp + q * sq, slot + wrap(-s))

    def wide_middle(n, cv):
        color, s = lax.div(cv, 2), 1 - 2 * lax.rem(cv, 2)
        sp, sq, p, q = axes_of(color)
        oq, oy = NEAR[n // 2], n % 2
        block = lax.rem(y + oy, 2) * 16 + wrap(p - s) * sp + wrap(q - oq) * sq
        slot = oy * 16 + oq * 4
        wait_wide(cv, block, slot + wrap(s))
        send_wide(cv, block, y * 16 + wrap(p + s) * sp + q * sq, slot + 2)

    def wide_leaf(cv, n):
        color, s = lax.div(cv, 2), 1 - 2 * lax.rem(cv, 2)
        sp, sq, p, q = axes_of(color)
        oq, oy = near_first(lax.div(n, 2)), lax.rem(n, 2)
        slot = oy * 16 + oq * 4
        base = lax.rem(y + oy, 2) * 16 + wrap(q - oq) * sq
        wait_wide(cv, base + wrap(p + s) * sp, slot + wrap(-s))
        wait_wide(cv, base + wrap(p + 2) * sp, slot + 2)

    def slim_step(t, cv):
        color, s = lax.div(cv, 2), 1 - 2 * lax.rem(cv, 2)
        sq, sr, q, r = axes_of(color)
        orr, oq = NEAR[t // 4], NEAR[t % 4]
        b, c = wrap(s * oq), wrap(s * orr)
        block = y * 16 + wrap(q - oq) * sq + wrap(r - orr) * sr
        slot = orr * 4 + oq
        if t > 0:
            wait_slim(cv, block, slot)
        send_slim(cv, block, flat(1 - y, z, x), 16 + slot)

        def forward_third():
            send_slim(cv, block, y * 16 + q * sq + wrap(r + s) * sr, wrap(orr + s) * 4)

        def forward_second():
            send_slim(cv, block, y * 16 + wrap(q + s) * sq + r * sr, orr * 4 + wrap(oq + s))

        if oq == 0:
            if orr == 0:
                forward_third()
                send_slim(cv, block, y * 16 + q * sq + wrap(r - s) * sr, wrap(orr - s) * 4)
            elif orr != 2:
                pl.when(c == 1)(forward_third)
            forward_second()
            send_slim(cv, block, y * 16 + wrap(q - s) * sq + r * sr, orr * 4 + wrap(oq - s))
        elif oq != 2:
            pl.when(b == 1)(forward_second)

    def slim_leaf(cv, n):
        color = lax.div(cv, 2)
        sq, sr, q, r = axes_of(color)
        orr, oy = near_first(lax.div(n, 2)), lax.rem(n, 2)

        @pl.when(oy == 1)
        def _():
            def one(oq):
                block = (1 - y) * 16 + wrap(q - oq) * sq + wrap(r - orr) * sr
                wait_slim(cv, block, 16 + orr * 4 + oq)

            each(4, one)

    def parts_of(n):
        each(4, lambda cv: wide_leaf(cv, n))
        each(4, lambda cv: slim_leaf(cv, n))
        oo, oy = near_first(lax.div(n, 2)), lax.rem(n, 2)
        yy = lax.rem(y + oy, 2)
        for color in range(2):
            if color == 0:
                start = pl.multiple_of((yy * 4 + wrap(z - oo)) * 4 * rows, 4 * rows)
                at = [pl.ds(start, 4 * rows)]
            else:
                start = yy * 16 + wrap(x - oo)
                at = [pl.ds(pl.multiple_of((start + 4 * i) * rows, rows), rows) for i in range(4)]
            left = jnp.concatenate([hid[:, a] for a in at], axis=1)
            for ref, begin in ((wide, color * wcols), (slim, 2 * wcols + color * scols)):
                right = jnp.concatenate([ref[color, a, :] for a in at], axis=0)
                yield begin, jnp.dot(left, right, preferred_element_type=jnp.float32)

    band = 128
    tile = 16
    zero = jnp.zeros((tile, 128), jnp.float32)
    ff, cols = grad.shape

    def products(pairs, sums_of, k, columns):
        done = list(sums_of)
        for i in range(columns.start // 128, columns.stop // 128):
            lanes = slice(i * 128, (i + 1) * 128)
            values = {}
            for pair, (one, two) in enumerate(pairs):
                for ref in (one, two):
                    if id(ref) not in values:
                        values[id(ref)] = read(ref, k, lanes)
                done[pair] = done[pair] + values[id(one)] * values[id(two)]
        return tuple(done)

    def sum_products(pairs, start, columns):
        return lax.fori_loop(
            0, ff // tile, lambda k, sums_of: products(pairs, sums_of, k, columns), start
        )

    def tile_at(i):
        return pl.ds(pl.multiple_of(i * tile, tile), tile)

    column_parts = [
        slice(0, wcols),
        slice(2 * wcols, 2 * wcols + scols),
        slice(wcols, 2 * wcols),
        slice(2 * wcols + scols, cols),
    ]

    def grad_copy(part):
        columns = pl.ds(column_parts[part].start, column_parts[part].stop - column_parts[part].start)
        return remote_to(
            grad.at[:, columns], other_grad.at[:, columns], grad_send, grad_recv.at[part], (partner(), me)
        )

    bodies = {
        "m": fold_wide_middle,
        "r": fold_wide_root,
        "s": fold_slim_step,
        "M": wide_middle,
        "R": wide_root,
        "S": slim_step,
    }
    for step in " ".join(ORDER[0]).split():
        if step == "R0":
            pl.semaphore_wait(clear.at[0], 5)
        if step == "S0":
            pl.semaphore_wait(clear.at[1], 5)
        steps_of((step,), bodies)
        if step == "r7":
            release(0, wide_in, fold_wide_send, fold_wide_recv)
            finish(wide, 0)
            load_task()
        if step == "s15":
            release(1, slim_in, fold_slim_send, fold_slim_recv)
            finish(slim, 2 * wcols)
    wait_for_task()
    task_swap.wait_recv()
    tasks = sum_products(((task, task), (task, other_task)), (zero, zero), slice(0, cols))

    def group(n):
        for i in range(1, len(ORDER) - 1):
            pl.when(n == i)(functools.partial(steps_of, ORDER[i], bodies))
        which = GROUPS[0]
        for i in range(1, len(GROUPS) - 1):
            which = jnp.where(n == i, GROUPS[i], which)
        for begin, product in parts_of(which):
            total[:, begin : begin + product.shape[1]] += product

    each(7, group)
    steps_of(ORDER[7], bodies)
    kept = (zero, zero, zero)
    for part, (begin, product) in enumerate(parts_of(GROUPS[7])):
        columns = column_parts[part]
        grad[:, columns] = ((total[:, columns] + product) * inv_root).astype(jnp.bfloat16)
        grad_copy(part).start()
        kept = sum_products(((grad, grad), (task, grad), (other_task, grad)), kept, columns)
    crossed = (zero,)
    for part in range(4):
        grad_copy(part).wait_recv()
        crossed = sum_products(((grad, other_grad),), crossed, column_parts[part])
    for i, value in enumerate(kept + tasks + crossed):
        sums[0, i : i + 1, :] = jnp.sum(value, axis=0, keepdims=True)
    sums[0, 6:8, :] = jnp.zeros((2, 128), jnp.float32)

    def exchange(source, slots, devices):
        copies = [
            remote_to(sums.at[source], sums_in.at[slot], sums_send, sums_recv.at[slot], device)
            for slot, device in zip(slots, devices)
        ]
        for copy in copies:
            copy.start()
        for copy in copies:
            copy.wait_recv()

    exchange(0, range(15), plane())
    partly = sums[0]
    for i in range(15):
        partly = partly + sums_in[i]
    sums[1] = partly
    exchange(1, (15, 16, 17), across())
    own_sums = jnp.sum(sums[1] + sums_in[16], axis=1, keepdims=True)
    part_sums = jnp.sum(sums_in[15] + sums_in[17], axis=1, keepdims=True)

    def spread_row(column, i):
        return jnp.broadcast_to(column[i : i + 1], (1, 128))

    grad_oo, tgrad_oo, tgrad_po, task_oo, task_op, grad_op = (spread_row(own_sums, i) for i in range(6))
    grad_pp, tgrad_pp, tgrad_op, task_pp = (spread_row(part_sums, i) for i in range(4))
    is_first = lax.rem(lax.axis_index("pol"), 2) == 0
    scale_own = step_rate * clip_factor(grad_oo)
    scale_part = step_rate * clip_factor(grad_pp)
    own_total = task_oo - 2.0 * scale_own * tgrad_oo + scale_own * scale_own * grad_oo
    part_total = task_pp - 2.0 * scale_part * tgrad_pp + scale_part * scale_part * grad_pp
    cross_dot = (
        task_op - scale_part * tgrad_op - scale_own * tgrad_po + scale_own * scale_part * grad_op
    )
    first_sq = jnp.where(is_first, own_total, part_total)
    second_sq = jnp.where(is_first, part_total, own_total)
    weight_first, weight_second = slerp_weights(first_sq, second_sq, cross_dot)
    weight_own = jnp.where(is_first, weight_first, weight_second)
    weight_part = jnp.where(is_first, weight_second, weight_first)

    for i in range(ff // band):

        def settle_outputs(k):
            at = tile_at(k)
            for i in range(cols // 128):
                lanes = slice(i * 128, (i + 1) * 128)
                update = scale_own * grad[at, lanes].astype(jnp.float32)
                delta_own = read(task, k, lanes) - update
                delta_part = other_task[at, lanes].astype(jnp.float32) - scale_part * other_grad[
                    at, lanes
                ].astype(jnp.float32)
                lag[at, lanes] = ((1.0 - ema_rate) * (lag[at, lanes].astype(jnp.float32) - update)).astype(
                    jnp.bfloat16
                )
                other_grad[at, lanes] = (weight_own * delta_own + weight_part * delta_part).astype(jnp.bfloat16)

        each(band // tile, lambda k: settle_outputs(i * (band // tile) + k))
        at = pl.ds(i * band, band)
        pltpu.make_async_copy(lag.at[at], lag_out.at[at], out_sem.at[0]).start()
        pltpu.make_async_copy(other_grad.at[at], merged_out.at[at], out_sem.at[1]).start()

    pltpu.make_async_copy(lag, lag_out, out_sem.at[0]).wait()
    pltpu.make_async_copy(other_grad, merged_out, out_sem.at[1]).wait()
    task_swap.wait_send()
    remote_to(grad, other_grad, grad_send, grad_recv.at[0], (partner(), me)).wait_send()
    remote_to(sums_in, sums_in, sums_send, sums_recv.at[0], (partner(), me)).wait_send()
    sent = pl.ds(0, (BLOCKS - 1) * rows)
    remote(wide.at[:, sent], wide.at[:, sent], wide_send, wide_recv.at[0, 0], flat(1 - y, z, x)).wait_send()
    remote(slim.at[:, sent], slim.at[:, sent], slim_send, slim_recv.at[0, 0], flat(1 - y, z, x)).wait_send()


def shards(gate_pre, up_pre, lag, task, cotangent, buckets, advantages):
    tokens, ff = gate_pre.shape[1:]
    cols = lag.shape[2]
    rows = tokens // BLOCKS
    half = rows // 2
    wcols, scols = cols // 3, cols // 6
    any_spec = pl.BlockSpec(memory_space=pl.ANY)
    vmem_spec = pl.BlockSpec(memory_space=pltpu.VMEM)
    bf16 = jnp.bfloat16
    dma = pltpu.SemaphoreType.DMA
    per_stream = [dma, dma, dma((4, BLOCKS)), dma((4, BLOCKS))]
    new_lag, merged = pl.pallas_call(
        step_kernel,
        name="policy_step",
        out_shape=(jax.ShapeDtypeStruct((ff, cols), bf16), jax.ShapeDtypeStruct((ff, cols), bf16)),
        in_specs=[any_spec] * 4 + [vmem_spec] * 3,
        out_specs=(any_spec, any_spec),
        scratch_shapes=[
            *[pltpu.VMEM((2, 2 * rows, ff), bf16)] * 3,
            pltpu.VMEM((ff, cols), bf16),
            pltpu.VMEM((ff, tokens), bf16),
            pltpu.VMEM((2, tokens, wcols), bf16),
            pltpu.VMEM((2, tokens, scols), bf16),
            pltpu.VMEM((4, BLOCKS - 1, half, wcols), bf16),
            pltpu.VMEM((4, BLOCKS - 1, half, scols), bf16),
            pltpu.VMEM((ff, cols), jnp.float32),
            *[pltpu.VMEM((ff, cols), bf16)] * 3,
            pltpu.VMEM((rows, 128), jnp.float32),
            pltpu.VMEM((2, 8, 128), jnp.float32),
            pltpu.VMEM((18, 8, 128), jnp.float32),
            dma((2, 4)),
            dma((3,)),
            dma,
            dma,
            dma,
            dma,
            dma((4,)),
            dma((2,)),
            dma,
            dma((18,)),
            *per_stream,
            *per_stream,
            pltpu.SemaphoreType.REGULAR((2,)),
        ],
        compiler_params=pltpu.CompilerParams(
            collective_id=0, has_side_effects=True, vmem_limit_bytes=VMEM_BYTES
        ),
        cost_estimate=pl.CostEstimate(
            flops=4 * tokens * ff * cols, bytes_accessed=6 * tokens * ff, transcendentals=tokens * ff
        ),
    )(gate_pre[0], up_pre[0], lag[0], task[0], cotangent[0], buckets, advantages)
    return (new_lag[None], merged[None])


def solution(mesh):
    return jax.shard_map(
        shards,
        mesh=mesh,
        in_specs=(
            P("pol", None, "fsdp"),
            P("pol", None, "fsdp"),
            P("pol", "fsdp", None),
            P("pol", "fsdp", None),
            P("pol", "fsdp", None),
            P("pol", "fsdp"),
            P("pol", None),
        ),
        out_specs=(P("pol", "fsdp", None), P("pol", "fsdp", None)),
        check_vma=False,
    )
```

```python
import functools
import math

import jax
import jax.numpy as jnp
from jax import lax
from jax.experimental import pallas as pl
from jax.experimental.pallas import tpu as pltpu
from jax.sharding import PartitionSpec as P

D = 2304
FF = 20480

kl_coef = 0.5
clip_level = 0.15
step_rate = 8.0
ema_rate = 0.1

MESH = pl.DeviceIdType.MESH
VMEM_BYTES = 60_600_000
RING = 4
BLOCKS = 32


def slerp_weights(first_sq, second_sq, cross_dot):
    norm_first = jnp.sqrt(first_sq)
    norm_second = jnp.sqrt(second_sq)
    blend = norm_second / (norm_first + norm_second)
    cosine = jnp.clip(cross_dot / (norm_first * norm_second), -1.0, 1.0)
    opening = jnp.arctan2(jnp.sqrt((1.0 - cosine) * (1.0 + cosine)), cosine)
    sine_val = jnp.sin(opening)
    weight_first = jnp.sin((1.0 - blend) * opening) / sine_val
    weight_second = jnp.sin(blend * opening) / sine_val
    return (weight_first, weight_second)


def clip_factor(grad_sq):
    return jnp.minimum(1.0, clip_level / (jnp.sqrt(grad_sq / (FF * D)) + 1e-06))


def position():
    me = lax.axis_index("fsdp")
    return lax.div(me, 16), lax.rem(lax.div(me, 4), 4), lax.rem(me, 4)


def wrap(value):
    return lax.rem(value + 2 * RING, RING)


def flat(y, z, x):
    return y * 16 + z * 4 + x


FAR = (2, 3, 1, 0)
NEAR = (0, 1, 3, 2)

ORDER = (
    ("s0 s4 m0 m2", "m5 m3 m1 m4", "m6 m7 s1 s5", "s8 s2 r0 s6", "r1 s12 s10 s3", "s9 r2 r4 s13", "s7 s14 s11 r3", "r5 r6 s15 S0", "r7 R0 S1 S2", "S4 S8 M0 R1", "R4 R2 S3 S6", "S5 S10 S9 S12"),
    ("M1 R3 R5 M4", "R6 M2 S7 S11", "S13 S14"),
    ("M3 M5 R7",),
    ("M6",),
    ("S15",),
    (),
    ("M7",),
    (),
)
GROUPS = (0, 1, 4, 2, 3, 5, 6, 7)


def far_first(index):
    return jnp.where(index == 0, 2, jnp.where(index == 1, 3, jnp.where(index == 2, 1, 0)))


def near_first(index):
    return jnp.where(index == 2, 3, jnp.where(index == 3, 2, index))


def steps_of(order, bodies):
    for step in " ".join(order).split():
        body, index = bodies[step[0]], int(step[1:])
        each(4, functools.partial(body, index))


def each(count, body):
    lax.fori_loop(0, count, lambda i, _: (body(i), None)[1], None)


def partner():
    pol = lax.axis_index("pol")
    return pol + 1 - 2 * lax.rem(pol, 2)


def neighbours():
    y, z, x = position()
    pol = lax.axis_index("pol")
    return [
        (pol, flat(y, z, wrap(x + 1))),
        (pol, flat(y, z, wrap(x - 1))),
        (pol, flat(y, wrap(z + 1), x)),
        (pol, flat(y, wrap(z - 1), x)),
        (pol, flat(1 - y, z, x)),
    ]


def plane():
    y, z, x = position()
    offsets = sorted(((i, j) for i in range(4) for j in range(4) if i or j), key=lambda o: o.count(2) * 4 - o.count(0))
    offsets.reverse()
    return [(lax.axis_index("pol"), flat(y, wrap(z + i), wrap(x + j))) for i, j in offsets]


def across():
    y, z, x = position()
    return [
        (partner(), flat(1 - y, z, x)),
        (lax.axis_index("pol"), flat(1 - y, z, x)),
        (partner(), flat(y, z, x)),
    ]


def greet(devices):
    for device in devices:
        pl.semaphore_signal(pltpu.get_barrier_semaphore(), inc=1, device_id=device, device_id_type=MESH)


def meet(devices):
    pl.semaphore_wait(pltpu.get_barrier_semaphore(), len(devices))


def remote(src, dst, send_sem, recv_sem, target):
    return remote_to(src, dst, send_sem, recv_sem, (lax.axis_index("pol"), target))


def remote_to(src, dst, send_sem, recv_sem, device):
    return pltpu.make_async_remote_copy(
        src_ref=src,
        dst_ref=dst,
        send_sem=send_sem,
        recv_sem=recv_sem,
        device_id=device,
        device_id_type=MESH,
    )


def axes_of(color):
    _, z, x = position()
    first = jnp.where(color == 0, x, z)
    second = jnp.where(color == 0, z, x)
    return 1 + 3 * color, 4 - 3 * color, first, second


def step_kernel(
    gate, up, lag_in, task_in, cot, buckets, adv,
    lag, other_grad,
    gate_buf, up_buf, active, hid, wide, slim, wide_in, slim_in,
    total, other_task, grad, scale, sums, sums_in,
    load_sem, lag_sem, task_sem, task_send, task_recv, grad_send, grad_recv, sums_send, sums_recv,
    fold_wide_send, fold_slim_send, fold_wide_recv, fold_slim_recv,
    wide_send, slim_send, wide_recv, slim_recv, clear,
):
    y, z, x = position()
    rows = gate_buf.shape[1] // 2
    me = flat(y, z, x)
    half = rows // 2
    wcols, scols = wide.shape[2], slim.shape[2]
    inv_root = 1.0 / math.sqrt(FF)
    greet(plane() + across())
    lag_copies = []
    for i, columns in enumerate((pl.ds(0, wcols), pl.ds(wcols, wcols), pl.ds(2 * wcols, 2 * scols))):
        lag_copies.append(pltpu.make_async_copy(lag_in.at[:, columns], lag.at[:, columns], lag_sem.at[i]))

    def place(j):
        ez, ex = far_first(lax.div(j, 4)), far_first(lax.rem(j, 4))
        return ez, ex, flat(1 - y, wrap(z + ez), wrap(x + ex)), flat(y, wrap(z + ez), wrap(x + ex))

    def loads(j):
        slot = lax.rem(j, 2)
        copies = []
        for i, block in enumerate(place(j)[2:]):
            start = pl.multiple_of(block * rows, rows)
            there = pl.ds(i * rows, rows)
            copies.append(
                pltpu.make_async_copy(gate.at[pl.ds(start, rows)], gate_buf.at[slot, there], load_sem.at[slot, i])
            )
            copies.append(
                pltpu.make_async_copy(up.at[pl.ds(start, rows)], up_buf.at[slot, there], load_sem.at[slot, 2 + i])
            )
        return copies

    def activate(j):
        slot = lax.rem(j, 2)
        for copy in loads(j):
            copy.wait()
        active[slot] = (
            jax.nn.gelu(gate_buf[slot].astype(jnp.float32), approximate=True)
            * up_buf[slot].astype(jnp.float32)
        ).astype(jnp.bfloat16)

    for copy in loads(0) + lag_copies + loads(1):
        copy.start()
    activate(0)

    def push_wide(cv, block, target, slot):
        color, part = lax.div(cv, 2), lax.rem(cv, 2)
        start = pl.multiple_of(block * rows + part * half, half)
        remote(
            wide.at[color, pl.ds(start, half)], wide_in.at[cv, slot], fold_wide_send, fold_wide_recv.at[cv, slot], target
        ).start()

    def push_slim(cv, block, target, slot):
        color, part = lax.div(cv, 2), lax.rem(cv, 2)
        start = pl.multiple_of(block * rows + part * half, half)
        remote(
            slim.at[color, pl.ds(start, half)], slim_in.at[cv, slot], fold_slim_send, fold_slim_recv.at[cv, slot], target
        ).start()

    def product(hidden, begin, width):
        return (
            jnp.dot(hidden, lag[:, begin : begin + width], preferred_element_type=jnp.float32) * inv_root
        ).astype(jnp.bfloat16)

    def keep_product(j, ref, color, begin):
        value = product(active[lax.rem(j, 2)], begin, ref.shape[2])
        for i, block in enumerate(place(j)[2:]):
            here = pl.ds(pl.multiple_of(block * rows, rows), rows)
            ref[color, here, :] = value[i * rows : (i + 1) * rows]

    def keep_hidden(j):
        hidden = active[lax.rem(j, 2)]
        for i, block in enumerate(place(j)[2:]):
            here = pl.ds(pl.multiple_of(block * rows, rows), rows)
            hid[:, here] = hidden[i * rows : (i + 1) * rows].T

    def activate_next(j):
        later = 1 - lax.rem(j, 2)
        active[later] = (
            jax.nn.gelu(gate_buf[later].astype(jnp.float32), approximate=True)
            * up_buf[later].astype(jnp.float32)
        ).astype(jnp.bfloat16)

    def leaf_wide(j, cv):
        ez, ex, other, mine = place(j)
        color, s = lax.div(cv, 2), 1 - 2 * lax.rem(cv, 2)
        sp, sq, p, q = axes_of(color)
        ep = jnp.where(color == 0, ex, ez)
        eq = jnp.where(color == 0, ez, ex)
        u = wrap(s * ep)

        @pl.when(u >= 2)
        def _():
            step = jnp.where(u == 2, s, -s)
            target = y * 16 + wrap(p + step) * sp + q * sq
            slot_of = jnp.where(u == 2, 0, 16) + eq * 2
            push_wide(cv, other, target, slot_of + 1)
            push_wide(cv, mine, target, slot_of)

    def leaf_slim(j, cv):
        ez, ex, other, _ = place(j)
        color = lax.div(cv, 2)
        ep = jnp.where(color == 0, ex, ez)
        eq = jnp.where(color == 0, ez, ex)
        push_slim(cv, other, flat(1 - y, z, x), ep * 4 + eq)

    def compute(j):
        @pl.when(j + 2 < BLOCKS // 2)
        def _():
            for copy in loads(j + 2):
                copy.start()

        @pl.when(j + 1 < BLOCKS // 2)
        def _():
            for copy in loads(j + 1):
                copy.wait()

        activate_next(j)
        for color in range(2):
            keep_product(j, wide, color, color * wcols)
        for color in range(2):
            keep_product(j, slim, color, 2 * wcols + color * scols)
        keep_hidden(j)

        def leaves(cv):
            leaf_slim(j, cv)
            leaf_wide(j, cv)

        each(4, leaves)

    for color in range(2):
        lag_copies[color].wait()
        keep_product(0, wide, color, color * wcols)
        if color == 0:
            meet(plane() + across())
        each(2, lambda i: leaf_wide(0, 2 * color + i))
    lag_copies[2].wait()
    for color in range(2):
        keep_product(0, slim, color, 2 * wcols + color * scols)
        each(2, lambda i: leaf_slim(0, 2 * color + i))
    for copy in loads(2):
        copy.start()
    for copy in loads(1):
        copy.wait()
    keep_hidden(0)
    activate_next(0)
    each(BLOCKS // 2 - 1, lambda j: compute(j + 1))

    def gather(total, parts):
        def tile(i):
            at = pl.ds(pl.multiple_of(i * 16, 16), 16)
            value = total[at, :].astype(jnp.float32)
            for part in parts:
                value = value + part[at, :].astype(jnp.float32)
            total[at, :] = value.astype(jnp.bfloat16)

        each(half // 16, tile)

    def take_wide(cv, block, slots):
        color, part = lax.div(cv, 2), lax.rem(cv, 2)
        start = pl.multiple_of(block * rows + part * half, half)
        for slot in slots:
            remote(
                wide_in.at[cv, slot], wide_in.at[cv, slot], fold_wide_send, fold_wide_recv.at[cv, slot], flat(1 - y, z, x)
            ).wait_recv()
        gather(wide.at[color, pl.ds(start, half)], [wide_in.at[cv, slot] for slot in slots])

    def take_slim(cv, block, slots):
        color, part = lax.div(cv, 2), lax.rem(cv, 2)
        start = pl.multiple_of(block * rows + part * half, half)
        for slot in slots:
            remote(
                slim_in.at[cv, slot], slim_in.at[cv, slot], fold_slim_send, fold_slim_recv.at[cv, slot], flat(1 - y, z, x)
            ).wait_recv()
        gather(slim.at[color, pl.ds(start, half)], [slim_in.at[cv, slot] for slot in slots])

    def fold_wide_middle(k, cv):
        color, s = lax.div(cv, 2), 1 - 2 * lax.rem(cv, 2)
        sp, sq, p, q = axes_of(color)
        eq, ey = FAR[k // 2], 1 - k % 2
        block = lax.rem(y + ey, 2) * 16 + wrap(p + s) * sp + wrap(q + eq) * sq
        take_wide(cv, block, (eq * 2 + ey,))
        push_wide(cv, block, y * 16 + wrap(p + s) * sp + q * sq, 8 + eq * 2 + ey)

    def fold_wide_root(k, cv):
        color, s = lax.div(cv, 2), 1 - 2 * lax.rem(cv, 2)
        sp, sq, p, q = axes_of(color)
        eq, ey = FAR[k // 2], 1 - k % 2
        v = wrap(s * eq)
        block = lax.rem(y + ey, 2) * 16 + p * sp + wrap(q + eq) * sq
        arrived = (8 + eq * 2 + ey, 16 + eq * 2 + ey)
        if eq == 0:
            take_wide(cv, block, arrived + (26 + ey, 28 + ey) + ((30,) if ey == 0 else ()))
            if ey == 1:
                push_wide(cv, block, flat(1 - y, z, x), 30)
            return
        take_wide(cv, block, arrived)
        if eq != 2:

            @pl.when(v == 1)
            def _():
                take_wide(cv, block, (24 + ey,))

        step = jnp.where(v == 3, -s, s)
        slot = jnp.where(v == 2, 24, jnp.where(v == 3, 28, 26)) + ey
        push_wide(cv, block, y * 16 + p * sp + wrap(q + step) * sq, slot)

    def fold_slim_step(t, cv):
        color, s = lax.div(cv, 2), 1 - 2 * lax.rem(cv, 2)
        sq, sr, q, r = axes_of(color)
        er, eq = FAR[t // 4], FAR[t % 4]
        v, w = wrap(s * eq), wrap(s * er)
        block = y * 16 + wrap(q + eq) * sq + wrap(r + er) * sr
        if eq != 0:
            take_slim(cv, block, (eq * 4 + er,))
            if eq != 2:

                @pl.when(v == 1)
                def _():
                    take_slim(cv, block, (16 + er,))

            step = jnp.where(v == 3, -s, s)
            slot = jnp.where(v == 2, 16, jnp.where(v == 3, 24, 20)) + er
            push_slim(cv, block, y * 16 + wrap(q + step) * sq + r * sr, slot)
            return
        take_slim(cv, block, (er, 20 + er, 24 + er) + ((29, 30) if er == 0 else ()))
        if er in (1, 3):

            @pl.when(w == 1)
            def _():
                take_slim(cv, block, (28,))

        if er != 0:
            step = jnp.where(w == 3, -s, s)
            slot = jnp.where(w == 2, 28, jnp.where(w == 3, 30, 29))
            push_slim(cv, block, y * 16 + q * sq + wrap(r + step) * sr, slot)

    task_swap = remote_to(task_in, other_task, task_send, task_recv, (partner(), me))
    task_swap.start()
    total[...] = jnp.zeros_like(total)

    buckets_of = lax.broadcasted_iota(jnp.int32, (adv.shape[1], rows), 0)
    chosen = (buckets_of == buckets[...]).astype(jnp.float32)
    diagonal = (adv.shape[1], adv.shape[1])
    adv_column = jnp.sum(
        jnp.where(
            lax.broadcasted_iota(jnp.int32, diagonal, 0) == lax.broadcasted_iota(jnp.int32, diagonal, 1),
            jnp.broadcast_to(adv[...], diagonal),
            0.0,
        ),
        axis=1,
        keepdims=True,
    )
    scale[...] = lax.dot_general(
        chosen,
        jnp.broadcast_to(adv_column, (adv.shape[1], 128)),
        (((0,), (0,)), ((), ())),
        precision=lax.Precision.HIGHEST,
        preferred_element_type=jnp.float32,
    )
    own = pl.ds(pl.multiple_of(me * rows, rows), rows)

    def release(kind, received, send_sem, recv_sem):
        remote(received, received, send_sem, recv_sem.at[0, 0], flat(1 - y, z, x)).wait_send()
        for device in neighbours():
            pl.semaphore_signal(clear.at[kind], inc=1, device_id=device, device_id_type=MESH)

    def finish(ref, begin):
        width = ref.shape[2]
        for color in range(2):
            for i in range(width // 128):
                lanes = slice(i * 128, (i + 1) * 128)
                first = begin + color * width + i * 128
                weighted = scale[...] * cot[:, first : first + 128].astype(jnp.float32)
                gap = ref[color, own, lanes].astype(jnp.float32)
                ref[color, own, lanes] = (weighted + kl_coef * gap).astype(jnp.bfloat16)

    task = "task"
    task_pieces = task_in.shape[0] // half

    def load_task():
        def rows_from(j):
            at = pl.ds(pl.multiple_of(j * half, half), half)
            for i in range(task_in.shape[1] // wcols):
                columns = pl.ds(i * wcols, wcols)
                pltpu.make_async_copy(task_in.at[at, columns], wide_in.at[i, j], task_sem).start()

        each(task_pieces, rows_from)

    def wait_for_task():
        everything = wide_in.at[pl.ds(0, task_in.shape[1] // wcols), pl.ds(0, task_pieces)]
        pltpu.make_async_copy(everything, everything, task_sem).wait()

    def read(ref, k, lanes):
        if ref is not task:
            return ref[tile_at(k), lanes].astype(jnp.float32)
        tiles = half // 16
        at = pl.ds(pl.multiple_of(lax.rem(k, tiles) * 16, 16), 16)
        start = lanes.start % wcols
        return wide_in[lanes.start // wcols, lax.div(k, tiles), at, start : start + 128].astype(jnp.float32)

    def piece(ref, cv, block):
        color, part = lax.div(cv, 2), lax.rem(cv, 2)
        start = pl.multiple_of(block * rows + part * half, half)
        return ref.at[color, pl.ds(start, half)]

    def send_wide(cv, block, target, slot):
        here = piece(wide, cv, block)
        remote(here, here, wide_send, wide_recv.at[cv, slot], target).start()

    def send_slim(cv, block, target, slot):
        here = piece(slim, cv, block)
        remote(here, here, slim_send, slim_recv.at[cv, slot], target).start()

    def wait_wide(cv, block, slot):
        here = piece(wide, cv, block)
        remote(here, here, wide_send, wide_recv.at[cv, slot], flat(1 - y, z, x)).wait_recv()

    def wait_slim(cv, block, slot):
        here = piece(slim, cv, block)
        remote(here, here, slim_send, slim_recv.at[cv, slot], flat(1 - y, z, x)).wait_recv()

    def wide_root(n, cv):
        color, s = lax.div(cv, 2), 1 - 2 * lax.rem(cv, 2)
        sp, sq, p, q = axes_of(color)
        oq, oy = NEAR[n // 2], n % 2
        b = wrap(s * oq)
        block = lax.rem(y + oy, 2) * 16 + p * sp + wrap(q - oq) * sq
        slot = oy * 16 + oq * 4
        if n > 0:
            wait_wide(cv, block, slot)
        else:
            send_wide(cv, block, flat(1 - y, z, x), 16)

        def forward():
            send_wide(cv, block, y * 16 + p * sp + wrap(q + s) * sq, oy * 16 + wrap(oq + s) * 4)

        if oq == 0:
            forward()
            send_wide(cv, block, y * 16 + p * sp + wrap(q - s) * sq, oy * 16 + wrap(oq - s) * 4)
        elif oq != 2:
            pl.when(b == 1)(forward)
        send_wide(cv, block, y * 16 + wrap(p + s) * sp + q * sq, slot + wrap(s))
        send_wide(cv, block, y * 16 + wrap(p - s) * sp + q * sq, slot + wrap(-s))

    def wide_middle(n, cv):
        color, s = lax.div(cv, 2), 1 - 2 * lax.rem(cv, 2)
        sp, sq, p, q = axes_of(color)
        oq, oy = NEAR[n // 2], n % 2
        block = lax.rem(y + oy, 2) * 16 + wrap(p - s) * sp + wrap(q - oq) * sq
        slot = oy * 16 + oq * 4
        wait_wide(cv, block, slot + wrap(s))
        send_wide(cv, block, y * 16 + wrap(p + s) * sp + q * sq, slot + 2)

    def wide_leaf(cv, n):
        color, s = lax.div(cv, 2), 1 - 2 * lax.rem(cv, 2)
        sp, sq, p, q = axes_of(color)
        oq, oy = near_first(lax.div(n, 2)), lax.rem(n, 2)
        slot = oy * 16 + oq * 4
        base = lax.rem(y + oy, 2) * 16 + wrap(q - oq) * sq
        wait_wide(cv, base + wrap(p + s) * sp, slot + wrap(-s))
        wait_wide(cv, base + wrap(p + 2) * sp, slot + 2)

    def slim_step(t, cv):
        color, s = lax.div(cv, 2), 1 - 2 * lax.rem(cv, 2)
        sq, sr, q, r = axes_of(color)
        orr, oq = NEAR[t // 4], NEAR[t % 4]
        b, c = wrap(s * oq), wrap(s * orr)
        block = y * 16 + wrap(q - oq) * sq + wrap(r - orr) * sr
        slot = orr * 4 + oq
        if t > 0:
            wait_slim(cv, block, slot)
        send_slim(cv, block, flat(1 - y, z, x), 16 + slot)

        def forward_third():
            send_slim(cv, block, y * 16 + q * sq + wrap(r + s) * sr, wrap(orr + s) * 4)

        def forward_second():
            send_slim(cv, block, y * 16 + wrap(q + s) * sq + r * sr, orr * 4 + wrap(oq + s))

        if oq == 0:
            if orr == 0:
                forward_third()
                send_slim(cv, block, y * 16 + q * sq + wrap(r - s) * sr, wrap(orr - s) * 4)
            elif orr != 2:
                pl.when(c == 1)(forward_third)
            forward_second()
            send_slim(cv, block, y * 16 + wrap(q - s) * sq + r * sr, orr * 4 + wrap(oq - s))
        elif oq != 2:
            pl.when(b == 1)(forward_second)

    def slim_leaf(cv, n):
        color = lax.div(cv, 2)
        sq, sr, q, r = axes_of(color)
        orr, oy = near_first(lax.div(n, 2)), lax.rem(n, 2)

        @pl.when(oy == 1)
        def _():
            def one(oq):
                block = (1 - y) * 16 + wrap(q - oq) * sq + wrap(r - orr) * sr
                wait_slim(cv, block, 16 + orr * 4 + oq)

            each(4, one)

    def parts_of(n):
        each(4, lambda cv: wide_leaf(cv, n))
        each(4, lambda cv: slim_leaf(cv, n))
        oo, oy = near_first(lax.div(n, 2)), lax.rem(n, 2)
        yy = lax.rem(y + oy, 2)
        for color in range(2):
            if color == 0:
                start = pl.multiple_of((yy * 4 + wrap(z - oo)) * 4 * rows, 4 * rows)
                at = [pl.ds(start, 4 * rows)]
            else:
                start = yy * 16 + wrap(x - oo)
                at = [pl.ds(pl.multiple_of((start + 4 * i) * rows, rows), rows) for i in range(4)]
            left = jnp.concatenate([hid[:, a] for a in at], axis=1)
            for ref, begin in ((wide, color * wcols), (slim, 2 * wcols + color * scols)):
                right = jnp.concatenate([ref[color, a, :] for a in at], axis=0)
                yield begin, jnp.dot(left, right, preferred_element_type=jnp.float32)

    band = 128
    tile = 16
    zero = jnp.zeros((tile, 128), jnp.float32)
    ff, cols = grad.shape

    def products(pairs, sums_of, k, columns):
        done = list(sums_of)
        for i in range(columns.start // 128, columns.stop // 128):
            lanes = slice(i * 128, (i + 1) * 128)
            values = {}
            for pair, (one, two) in enumerate(pairs):
                for ref in (one, two):
                    if id(ref) not in values:
                        values[id(ref)] = read(ref, k, lanes)
                done[pair] = done[pair] + values[id(one)] * values[id(two)]
        return tuple(done)

    def sum_products(pairs, start, columns):
        return lax.fori_loop(
            0, ff // tile, lambda k, sums_of: products(pairs, sums_of, k, columns), start
        )

    def tile_at(i):
        return pl.ds(pl.multiple_of(i * tile, tile), tile)

    column_parts = [
        slice(0, wcols),
        slice(2 * wcols, 2 * wcols + scols),
        slice(wcols, 2 * wcols),
        slice(2 * wcols + scols, cols),
    ]

    def grad_copy(part):
        columns = pl.ds(column_parts[part].start, column_parts[part].stop - column_parts[part].start)
        return remote_to(
            grad.at[:, columns], other_grad.at[:, columns], grad_send, grad_recv.at[part], (partner(), me)
        )

    bodies = {
        "m": fold_wide_middle,
        "r": fold_wide_root,
        "s": fold_slim_step,
        "M": wide_middle,
        "R": wide_root,
        "S": slim_step,
    }
    for step in " ".join(ORDER[0]).split():
        if step == "R0":
            pl.semaphore_wait(clear.at[0], 5)
        if step == "S0":
            pl.semaphore_wait(clear.at[1], 5)
        steps_of((step,), bodies)
        if step == "r7":
            release(0, wide_in, fold_wide_send, fold_wide_recv)
            finish(wide, 0)
            load_task()
        if step == "s15":
            release(1, slim_in, fold_slim_send, fold_slim_recv)
            finish(slim, 2 * wcols)
    wait_for_task()
    task_swap.wait_recv()
    tasks = sum_products(((task, task), (task, other_task)), (zero, zero), slice(0, cols))

    def group(n):
        for i in range(1, len(ORDER) - 1):
            pl.when(n == i)(functools.partial(steps_of, ORDER[i], bodies))
        which = GROUPS[0]
        for i in range(1, len(GROUPS) - 1):
            which = jnp.where(n == i, GROUPS[i], which)
        for begin, product in parts_of(which):
            total[:, begin : begin + product.shape[1]] += product

    each(7, group)
    steps_of(ORDER[7], bodies)
    kept = (zero, zero, zero)
    for part, (begin, product) in enumerate(parts_of(GROUPS[7])):
        columns = column_parts[part]
        grad[:, columns] = ((total[:, columns] + product) * inv_root).astype(jnp.bfloat16)
        grad_copy(part).start()
        kept = sum_products(((grad, grad), (task, grad), (other_task, grad)), kept, columns)
    crossed = (zero,)
    for part in range(4):
        grad_copy(part).wait_recv()
        crossed = sum_products(((grad, other_grad),), crossed, column_parts[part])
    for i, value in enumerate(kept + tasks + crossed):
        sums[0, i : i + 1, :] = jnp.sum(value, axis=0, keepdims=True)
    sums[0, 6:8, :] = jnp.zeros((2, 128), jnp.float32)

    def exchange(source, slots, devices):
        copies = [
            remote_to(sums.at[source], sums_in.at[slot], sums_send, sums_recv.at[slot], device)
            for slot, device in zip(slots, devices)
        ]
        for copy in copies:
            copy.start()
        for copy in copies:
            copy.wait_recv()

    exchange(0, range(15), plane())
    partly = sums[0]
    for i in range(15):
        partly = partly + sums_in[i]
    sums[1] = partly
    exchange(1, (15, 16, 17), across())
    own_sums = jnp.sum(sums[1] + sums_in[16], axis=1, keepdims=True)
    part_sums = jnp.sum(sums_in[15] + sums_in[17], axis=1, keepdims=True)

    def spread_row(column, i):
        return jnp.broadcast_to(column[i : i + 1], (1, 128))

    grad_oo, tgrad_oo, tgrad_po, task_oo, task_op, grad_op = (spread_row(own_sums, i) for i in range(6))
    grad_pp, tgrad_pp, tgrad_op, task_pp = (spread_row(part_sums, i) for i in range(4))
    is_first = lax.rem(lax.axis_index("pol"), 2) == 0
    scale_own = step_rate * clip_factor(grad_oo)
    scale_part = step_rate * clip_factor(grad_pp)
    own_total = task_oo - 2.0 * scale_own * tgrad_oo + scale_own * scale_own * grad_oo
    part_total = task_pp - 2.0 * scale_part * tgrad_pp + scale_part * scale_part * grad_pp
    cross_dot = (
        task_op - scale_part * tgrad_op - scale_own * tgrad_po + scale_own * scale_part * grad_op
    )
    first_sq = jnp.where(is_first, own_total, part_total)
    second_sq = jnp.where(is_first, part_total, own_total)
    weight_first, weight_second = slerp_weights(first_sq, second_sq, cross_dot)
    weight_own = jnp.where(is_first, weight_first, weight_second)
    weight_part = jnp.where(is_first, weight_second, weight_first)

    for i in range(ff // band):

        def settle_outputs(k):
            at = tile_at(k)
            for i in range(cols // 128):
                lanes = slice(i * 128, (i + 1) * 128)
                update = scale_own * grad[at, lanes].astype(jnp.float32)
                delta_own = read(task, k, lanes) - update
                delta_part = other_task[at, lanes].astype(jnp.float32) - scale_part * other_grad[
                    at, lanes
                ].astype(jnp.float32)
                lag[at, lanes] = ((1.0 - ema_rate) * (lag[at, lanes].astype(jnp.float32) - update)).astype(
                    jnp.bfloat16
                )
                other_grad[at, lanes] = (weight_own * delta_own + weight_part * delta_part).astype(jnp.bfloat16)

        each(band // tile, lambda k: settle_outputs(i * (band // tile) + k))
    task_swap.wait_send()
    remote_to(grad, other_grad, grad_send, grad_recv.at[0], (partner(), me)).wait_send()
    remote_to(sums_in, sums_in, sums_send, sums_recv.at[0], (partner(), me)).wait_send()
    sent = pl.ds(0, (BLOCKS - 1) * rows)
    remote(wide.at[:, sent], wide.at[:, sent], wide_send, wide_recv.at[0, 0], flat(1 - y, z, x)).wait_send()
    remote(slim.at[:, sent], slim.at[:, sent], slim_send, slim_recv.at[0, 0], flat(1 - y, z, x)).wait_send()


def shards(gate_pre, up_pre, lag, task, cotangent, buckets, advantages):
    tokens, ff = gate_pre.shape[1:]
    cols = lag.shape[2]
    rows = tokens // BLOCKS
    half = rows // 2
    wcols, scols = cols // 3, cols // 6
    any_spec = pl.BlockSpec(memory_space=pl.ANY)
    vmem_spec = pl.BlockSpec(memory_space=pltpu.VMEM)
    bf16 = jnp.bfloat16
    dma = pltpu.SemaphoreType.DMA
    per_stream = [dma, dma, dma((4, BLOCKS)), dma((4, BLOCKS))]
    new_lag, merged = pl.pallas_call(
        step_kernel,
        name="policy_step",
        out_shape=(pltpu.VMEM((ff, cols), bf16), pltpu.VMEM((ff, cols), bf16)),
        in_specs=[any_spec] * 4 + [vmem_spec] * 3,
        out_specs=(vmem_spec, vmem_spec),
        scratch_shapes=[
            *[pltpu.VMEM((2, 2 * rows, ff), bf16)] * 3,
            pltpu.VMEM((ff, tokens), bf16),
            pltpu.VMEM((2, tokens, wcols), bf16),
            pltpu.VMEM((2, tokens, scols), bf16),
            pltpu.VMEM((4, BLOCKS - 1, half, wcols), bf16),
            pltpu.VMEM((4, BLOCKS - 1, half, scols), bf16),
            pltpu.VMEM((ff, cols), jnp.float32),
            *[pltpu.VMEM((ff, cols), bf16)] * 2,
            pltpu.VMEM((rows, 128), jnp.float32),
            pltpu.VMEM((2, 8, 128), jnp.float32),
            pltpu.VMEM((18, 8, 128), jnp.float32),
            dma((2, 4)),
            dma((3,)),
            dma,
            dma,
            dma,
            dma,
            dma((4,)),
            dma,
            dma((18,)),
            *per_stream,
            *per_stream,
            pltpu.SemaphoreType.REGULAR((2,)),
        ],
        compiler_params=pltpu.CompilerParams(
            collective_id=0, has_side_effects=True, vmem_limit_bytes=VMEM_BYTES
        ),
        cost_estimate=pl.CostEstimate(
            flops=4 * tokens * ff * cols, bytes_accessed=6 * tokens * ff, transcendentals=tokens * ff
        ),
    )(gate_pre[0], up_pre[0], lag[0], task[0], cotangent[0], buckets, advantages)
    return (new_lag[None], merged[None])


def solution(mesh):
    return jax.shard_map(
        shards,
        mesh=mesh,
        in_specs=(
            P("pol", None, "fsdp"),
            P("pol", None, "fsdp"),
            P("pol", "fsdp", None),
            P("pol", "fsdp", None),
            P("pol", "fsdp", None),
            P("pol", "fsdp"),
            P("pol", None),
        ),
        out_specs=(P("pol", "fsdp", None), P("pol", "fsdp", None)),
        check_vma=False,
    )
```
